256 devices in a mesh: ang: 64 (over x, z, core), sy: 2 (over y_hi), sx: 2 (over y_lo).
Axes of the slice: x: 4, y: 4 (y_hi: 2, y_lo: 2; y = y_hi * 2 + y_lo), z: 8, core: 2. Of those that a mesh axis runs over, the one named last changes fastest.
Arguments:
- objects: bfloat16 [64, 2, 1024, 1024], P('ang', None, 'sy', 'sx'), may hold values from -4 to 4
- probe: float32 [2, 2, 256, 256], replicated, may hold values from -4 to 4
- data: bfloat16 [64, 2, 2, 2, 256, 256], P('ang', 'sy', 'sx'), may hold values from 0 to 4
- positions: int32 [64, 2, 2, 2, 2], P('ang', 'sy', 'sx'), may hold values from 0 to 384
- block_index: int32 [8, 16], replicated, may hold values from 0 to 511, as said below
- block_values: bfloat16 [8, 16, 128, 128], replicated, may hold values from -0.125 to 0.125
Outputs:
- object_grad: float32 [64, 2, 1024, 1024], P('ang', None, 'sy', 'sx')
- probe_grad: float32 [64, 2, 2, 256, 256], P('ang')
- vol_grad: float32 [2, 512, 2, 1024], P('sy', ('ang', 'sx'))
The draws below stay inside these ranges and needn't reach their ends.
Inputs may be any that keep to these rules, and one draw needn't show every extreme that they name: `positions`: A position counts cells from 64 cells before the tile's first row or column. `block_index`: entry g names the angle g // 8 and the column block g % 8; every angle is named by exactly 2 entries.
All inputs are finite; a program needn't handle non-finite values.
Results may differ from the reference program's by a relative error of at most 0.011.
Values may be sent and summed in bfloat16 or wider, within the bound.
A program may use at most 64 MiB of HBM per device.

```python
import math
from functools import partial
import jax
import jax.numpy as jnp
from jax import lax

PATCH = 256
MODES = 2
TILE = 512
RIM = 64
PATCH_DEV = 2
BLK = 128
KBLK = 16
ANGLES = 64
YTILES = 2
XTILES = 2
OROWS = 1024
W = 1024
LINEB = 8


def draw_block_index(key, part):
    entries = LINEB * KBLK
    ranking = jax.random.permutation(jax.random.fold_in(key, 101), entries)
    angle_of = ranking % ANGLES
    column_of = jax.random.randint(jax.random.fold_in(key, 102), (entries,), 0, LINEB)
    column_of = jnp.where(ranking == entries - 1, LINEB - 1, column_of)
    column_of = jnp.where(ranking == 0, 0, column_of)
    return (angle_of * LINEB + column_of).astype(jnp.int32).reshape(LINEB, KBLK)


def plant(values, key, least, top_value):
    longest = values.shape.index(max(values.shape))
    spots = []
    for shift in (0, 1):
        where = [jax.random.randint(jax.random.fold_in(key, axis), (), 0, length) for axis, length in enumerate(values.shape)]
        where[longest] = (where[longest] + shift) % values.shape[longest]
        spots.append(tuple(where))
    return values.at[spots[0]].set(least).at[spots[1]].set(top_value)


def block_levels(stream_key, extent, pieces, low, high):
    def one(dim, shards_of):
        draws = jax.random.uniform(jax.random.fold_in(jax.random.fold_in(stream_key, 6), dim), (shards_of,), jnp.float32, low / len(pieces), high / len(pieces))
        return jnp.repeat(jnp.exp(draws), extent[dim] // shards_of).reshape((-1,) + (1,) * (len(extent) - dim - 1))

    factor_of = one(*pieces[0])
    for cut in pieces[1:]:
        factor_of = factor_of * one(*cut)
    return factor_of


def normal_values(stream_key, extent, deviation, limit, split=(), kind=jnp.bfloat16):
    gain = block_levels(stream_key, extent, split, -0.22, 0.18) if split else 1.0
    values = jax.random.normal(stream_key, extent, jnp.float32) * deviation * gain
    return jnp.minimum(jnp.maximum(values, -limit), limit).astype(kind)


def setup_inputs(seed: int = 0) -> dict:
    keys = jax.random.split(jax.random.key(seed), 7)
    objects = normal_values(keys[0], (ANGLES, 2, OROWS, W), 0.7, 4.0, ((0, 64), (2, 2), (3, 2)))
    probe = normal_values(keys[1], (MODES, 2, PATCH, PATCH), 0.7, 4.0, (), jnp.float32)
    data = jnp.clip(4.0 * jax.random.uniform(keys[2], (ANGLES, YTILES, XTILES, PATCH_DEV, PATCH, PATCH), jnp.float32) ** block_levels(keys[2], (ANGLES, YTILES, XTILES, PATCH_DEV, PATCH, PATCH), ((0, 64), (1, 2), (2, 2)), -0.2, 0.2), 0.0, 4.0).astype(jnp.bfloat16)
    positions = plant(jax.random.randint(keys[3], (ANGLES, YTILES, XTILES, PATCH_DEV, 2), 0, TILE + 2 * RIM - PATCH + 1), jax.random.fold_in(keys[3], 1), 0, TILE + 2 * RIM - PATCH).astype(jnp.int32)
    block_index = draw_block_index(jax.random.fold_in(keys[6], 71), 0)
    block_values = normal_values(keys[5], (LINEB, KBLK, BLK, BLK), (KBLK * BLK) ** -0.5, 0.125)
    return dict(objects=objects, probe=probe, data=data, positions=positions, block_index=block_index, block_values=block_values)


def dft_parts(length):
    sample_ids = jnp.arange(length, dtype=jnp.int32)
    product = sample_ids[:, None] * sample_ids[None, :] % length
    phases = product.astype(jnp.float32) * (2.0 * math.pi / length)
    factor = 1.0 / math.sqrt(length)
    return (jnp.cos(phases) * factor, -jnp.sin(phases) * factor)

def dft_blocks(length):
    real_part, imag_part = dft_parts(length)
    forward = jnp.stack([jnp.stack([real_part, -imag_part], 1), jnp.stack([imag_part, real_part], 1)], 0)
    backward = jnp.stack([jnp.stack([real_part, imag_part], 1), jnp.stack([-imag_part, real_part], 1)], 0)
    return (forward.astype(jnp.bfloat16), backward.astype(jnp.bfloat16))

def ramp_table(width):
    column_ids = jnp.arange(width, dtype=jnp.int32)
    offsets = column_ids[None, :] - column_ids[:, None]
    odd_cells = offsets % 2 != 0
    scaled = offsets.astype(jnp.float32) * math.pi
    values = jnp.where(odd_cells, -1.0 / jnp.maximum(scaled * scaled, 1.0), 0.0)
    values = jnp.where(offsets == 0, 0.25, values)
    return values.astype(jnp.bfloat16)

def left_product(matrix, fields):
    return jnp.einsum('srtk,btkc->bsrc', matrix.astype(jnp.float32), fields.astype(jnp.float32))

def right_product(fields, matrix):
    return jnp.einsum('btrc,tcsq->bsrq', fields.astype(jnp.float32), matrix.astype(jnp.float32))

def cut_window(field, corner):
    return lax.dynamic_slice(field, (jnp.int32(0), corner[0], corner[1]), (field.shape[0], PATCH, PATCH))

def patch_gradients(patches, measured, probe, forward, backward):
    patch_count = patches.shape[0]
    mode_count = probe.shape[0]
    side = patches.shape[2]
    object_real = patches[:, 0].astype(jnp.float32)[:, None]
    object_imag = patches[:, 1].astype(jnp.float32)[:, None]
    probe_real = probe[None, :, 0]
    probe_imag = probe[None, :, 1]
    exit_real = probe_real * object_real - probe_imag * object_imag
    exit_imag = probe_real * object_imag + probe_imag * object_real
    exit_waves = jnp.stack([exit_real, exit_imag], 2).reshape(patch_count * mode_count, 2, side, side).astype(jnp.bfloat16)
    half_done = left_product(forward, exit_waves).astype(jnp.bfloat16)
    far_field = right_product(half_done, backward).reshape(patch_count, mode_count, 2, side, side)
    intensity = lax.optimization_barrier(jnp.sum(far_field * far_field, axis=(1, 2)))
    misfit = intensity - measured.astype(jnp.float32)
    weighted = (misfit[:, None, None] * far_field).reshape(patch_count * mode_count, 2, side, side).astype(jnp.bfloat16)
    back_half = left_product(backward, weighted).astype(jnp.bfloat16)
    spread = right_product(back_half, forward).reshape(patch_count, mode_count, 2, side, side)
    chi_real = spread[:, :, 0]
    chi_imag = spread[:, :, 1]
    grad_real = lax.optimization_barrier(jnp.sum(probe_real * chi_real + probe_imag * chi_imag, axis=1))
    grad_imag = lax.optimization_barrier(jnp.sum(probe_real * chi_imag - probe_imag * chi_real, axis=1))
    patch_grad = jnp.stack([grad_real, grad_imag], 1)
    probe_real_part = lax.optimization_barrier(jnp.sum(object_real * chi_real + object_imag * chi_imag, axis=0))
    probe_imag_part = lax.optimization_barrier(jnp.sum(object_real * chi_imag - object_imag * chi_real, axis=0))
    probe_part = jnp.stack([probe_real_part, probe_imag_part], 1)
    return (patch_grad, probe_part)

def reference(objects, probe, data, positions, block_index, block_values):
    forward, backward = dft_blocks(PATCH)
    ramp_matrix = ramp_table(W)

    def per_angle(inputs):
        object_angle, data_angle, place_angle = inputs
        padded = jnp.pad(object_angle, ((0, 0), (RIM, RIM), (RIM, RIM)))
        row_base = jnp.arange(YTILES, dtype=jnp.int32)[:, None, None] * TILE
        col_base = jnp.arange(XTILES, dtype=jnp.int32)[None, :, None] * TILE
        row_start = (place_angle[..., 0] + row_base).reshape(-1).astype(jnp.int32)
        col_start = (place_angle[..., 1] + col_base).reshape(-1).astype(jnp.int32)
        starts = jnp.stack([row_start, col_start], 1)
        patches = jax.vmap(partial(cut_window, padded))(starts)
        measured = data_angle.reshape(-1, PATCH, PATCH)
        patch_grad, probe_part = patch_gradients(patches, measured, probe, forward, backward)

        def add_patch(number, current_sum):
            corner = (jnp.int32(0), starts[number, 0], starts[number, 1])
            window = lax.dynamic_slice(current_sum, corner, (2, PATCH, PATCH))
            return lax.dynamic_update_slice(current_sum, window + patch_grad[number], corner)
        running_sum = lax.fori_loop(0, starts.shape[0], add_patch, jnp.zeros(padded.shape, jnp.float32))
        grad_angle = running_sum[:, RIM:RIM + OROWS, RIM:RIM + W]
        sinogram = grad_angle.astype(jnp.bfloat16)
        filtered = jnp.dot(sinogram.reshape(-1, W), ramp_matrix, preferred_element_type=jnp.float32)
        filtered = filtered.reshape(sinogram.shape).astype(jnp.bfloat16)
        return (grad_angle, probe_part, filtered)
    object_grad, probe_parts, filtered_all = lax.map(per_angle, (objects, data, positions))
    probe_grad = probe_parts / math.sqrt(YTILES * XTILES * PATCH_DEV)
    line_data = filtered_all.reshape(ANGLES, 2, OROWS, LINEB, BLK)
    angle_of = block_index // LINEB
    column_of = block_index % LINEB
    picked = line_data[angle_of, :, :, column_of, :]
    volume = jnp.einsum('bkcru,bkuv->rcbv', picked.astype(jnp.float32), block_values.astype(jnp.float32))
    vol_grad = volume.reshape(YTILES, TILE, 2, W)
    return (object_grad, probe_grad, vol_grad)
```

```python
import functools
import math

import jax
import jax.numpy as jnp
import numpy as np
from jax import lax
from jax.experimental import pallas as pl
from jax.experimental.pallas import tpu as pltpu
from jax.sharding import PartitionSpec as P

PATCH = 256
RIM = 64
BLK = 128
TILE = 512
ROWS = 640
COLS = 768
MESH = pl.DeviceIdType.MESH
BF = jnp.bfloat16
F32 = jnp.float32


def dft_tables():
    ids = np.arange(PATCH)
    phases = (np.outer(ids, ids) % PATCH).astype(np.float64) * (2.0 * math.pi / PATCH)
    factor = 1.0 / math.sqrt(PATCH)
    real = (np.cos(phases) * factor).astype(np.float32)
    imag = (-np.sin(phases) * factor).astype(np.float32)
    forward = np.block([[real, -imag], [imag, real]])
    backward = np.block([[real, imag], [-imag, real]])
    return forward.astype(BF), backward.astype(BF)


def ramp_blocks(line_blocks):
    x = np.arange((2 * line_blocks - 1) * BLK)
    n = np.arange(BLK)[None, :] - (x - (line_blocks - 1) * BLK)[:, None]
    odd = n % 2 != 0
    scaled = n.astype(np.float32) * np.float32(math.pi)
    values = np.where(odd, -1.0 / np.maximum(scaled * scaled, 1.0), 0.0)
    values = np.where(n == 0, 0.25, values).astype(np.float32)
    return values.astype(BF)


def strips_kernel(obj_ref, row_out, col_out, cor_out, send_sem, recv_sem):
    ang, sy, sx = lax.axis_index("ang"), lax.axis_index("sy"), lax.axis_index("sx")
    oy, ox = 1 - sy, 1 - sx
    devices = [(ang, oy, sx), (ang, sy, ox), (ang, oy, ox)]
    barrier = pltpu.get_barrier_semaphore()
    for dev in devices:
        pl.semaphore_signal(barrier, inc=1, device_id=dev, device_id_type=MESH)
    pl.semaphore_wait(barrier, 3)
    rows = pl.ds(pl.multiple_of((TILE - RIM) * oy, RIM), RIM)
    cols = pl.ds(pl.multiple_of((TILE - BLK) * ox, BLK), BLK)
    sources = [obj_ref.at[0, :, rows, :], obj_ref.at[0, :, :, cols], obj_ref.at[0, :, rows, cols]]
    copies = [
        pltpu.make_async_remote_copy(
            src_ref=src, dst_ref=dst, send_sem=send_sem.at[i], recv_sem=recv_sem.at[i],
            device_id=dev, device_id_type=MESH,
        )
        for i, (src, dst, dev) in enumerate(zip(sources, (row_out, col_out, cor_out), devices))
    ]
    for copy in copies:
        copy.start()
    for copy in copies:
        copy.wait()


def patch_kernel(
    angles,
    pos_ref, bi_ref,
    obj_ref, halo_row, halo_col, halo_cor, probe_ref, data_ref, fwd_ref, bwd_ref, ramp_ref, bv_ref,
    og_out, row_out, col_out, cor_out, part_out, ramp_out, bv_out,
    big, probe, data, fwd, bwd, ramp, bv,
    win, patch, exits, half, far, chi, placed, og,
    rim_row, rim_col, rim_cor, part,
    load_sem, pick_sem, out_sem,
):
    ang, sy, sx = lax.axis_index("ang"), lax.axis_index("sy"), lax.axis_index("sx")
    oy, ox = 1 - sy, 1 - sx
    dst_row = pl.ds(pl.multiple_of((ROWS - RIM) * oy, RIM), RIM)
    dst_col = pl.ds(pl.multiple_of((COLS - BLK) * ox, BLK), BLK)
    loads = [
        pltpu.make_async_copy(src, dst, load_sem.at[i])
        for i, (src, dst) in enumerate(
            [
                (obj_ref.at[0], big.at[:, pl.ds(RIM, TILE), pl.ds(BLK, TILE)]),
                (halo_row, big.at[:, dst_row, pl.ds(BLK, TILE)]),
                (halo_col, big.at[:, pl.ds(RIM, TILE), dst_col]),
                (halo_cor, big.at[:, dst_row, dst_col]),
                (probe_ref, probe),
                (fwd_ref, fwd),
                (bwd_ref, bwd),
                (data_ref.at[0, 0, 0], data),
            ]
        )
    ]
    for copy in loads:
        copy.start()

    big[:, pl.ds(pl.multiple_of((ROWS - RIM) * sy, RIM), RIM), :] = jnp.zeros((2, RIM, COLS), BF)
    big[:, :, pl.ds(pl.multiple_of((COLS - BLK) * sx, BLK), BLK)] = jnp.zeros((2, ROWS, BLK), BF)
    for q in range(4):
        placed[q, :, 0:RIM, :] = jnp.zeros((5, RIM, BLK), F32)
        placed[q, :, RIM + PATCH :, :] = jnp.zeros((5, RIM, BLK), F32)
        placed[q, 0, RIM : RIM + PATCH, :] = jnp.zeros((PATCH, BLK), F32)
        placed[q, 4, RIM : RIM + PATCH, :] = jnp.zeros((PATCH, BLK), F32)

    named = [(jnp.int32(-1), jnp.int32(0)), (jnp.int32(0), jnp.int32(0))]
    for j in range(2 * angles):
        entry = bi_ref[j // 16, j % 16]
        mine = (entry >> 3) == ang
        early = jnp.logical_and(mine, named[0][0] < 0)
        named = [
            (jnp.where(take, j, at), jnp.where(take, entry & 7, column))
            for take, (at, column) in zip((early, mine), named)
        ]
    named[0] = (jnp.maximum(named[0][0], 0), named[0][1])
    picks = []
    for s, (entry, column) in enumerate(named):
        at = pl.multiple_of((7 - column + 4 * sx) * BLK, BLK)
        picks.append(
            pltpu.make_async_copy(ramp_ref.at[pl.ds(at, TILE), :], ramp.at[s], pick_sem.at[2 * s])
        )
        picks.append(
            pltpu.make_async_copy(bv_ref.at[entry >> 4, entry & 15], bv.at[s], pick_sem.at[2 * s + 1])
        )
    for copy in picks:
        copy.start()
    for copy in loads:
        copy.wait()

    def corner(p):
        return pos_ref[0, 0, 0, p, 0], pos_ref[0, 0, 0, p, 1] + RIM

    def forward_patch(p, carry):
        u, v = corner(p)
        base = jnp.minimum(u >> 4, 23) * 16
        lead = u - base
        block, shift = v >> 7, v & (BLK - 1)
        across = lax.broadcasted_iota(jnp.int32, (384, PATCH), 0)
        pick = jnp.where(
            across == lax.broadcasted_iota(jnp.int32, (384, PATCH), 1) + shift, 1.0, 0.0
        ).astype(BF)
        for c in range(2):
            cells = big[
                c, pl.ds(pl.multiple_of(base, 16), 272), pl.ds(pl.multiple_of(block * BLK, BLK), 384)
            ]
            cells = jnp.dot(cells, pick, preferred_element_type=F32)
            for b in range(2):
                win[c, b] = cells[:, b * BLK : (b + 1) * BLK]
        for c in range(2):
            for b in range(2):
                patch[p, c, :, b * BLK : (b + 1) * BLK] = win[c, b, pl.ds(lead, PATCH), :]
        for m in range(2):
            exits[m, 0:PATCH] = (probe[m, 0] * patch[p, 0] - probe[m, 1] * patch[p, 1]).astype(BF)
            exits[m, PATCH:] = (probe[m, 0] * patch[p, 1] + probe[m, 1] * patch[p, 0]).astype(BF)
        for m in range(2):
            done = jnp.dot(fwd[...], exits[m], preferred_element_type=F32)
            half[m, :, 0:PATCH] = done[0:PATCH].astype(BF)
            half[m, :, PATCH:] = done[PATCH:].astype(BF)
        for m in range(2):
            far[m] = jnp.dot(half[m], bwd[...], preferred_element_type=F32)
        misfit = (
            far[0, :, 0:PATCH] * far[0, :, 0:PATCH]
            + far[0, :, PATCH:] * far[0, :, PATCH:]
            + far[1, :, 0:PATCH] * far[1, :, 0:PATCH]
            + far[1, :, PATCH:] * far[1, :, PATCH:]
            - data[p].astype(F32)
        )
        for m in range(2):
            exits[m, 0:PATCH] = (misfit * far[m, :, 0:PATCH]).astype(BF)
            exits[m, PATCH:] = (misfit * far[m, :, PATCH:]).astype(BF)
        for m in range(2):
            done = jnp.dot(bwd[...], exits[m], preferred_element_type=F32)
            half[m, :, 0:PATCH] = done[0:PATCH].astype(BF)
            half[m, :, PATCH:] = done[PATCH:].astype(BF)
        for m in range(2):
            chi[p, m] = jnp.dot(half[m], fwd[...], preferred_element_type=F32)
        cr = [chi[p, m, :, 0:PATCH] for m in range(2)]
        ci = [chi[p, m, :, PATCH:] for m in range(2)]
        grad = [
            probe[0, 0] * cr[0] + probe[0, 1] * ci[0] + probe[1, 0] * cr[1] + probe[1, 1] * ci[1],
            probe[0, 0] * ci[0] - probe[0, 1] * cr[0] + probe[1, 0] * ci[1] - probe[1, 1] * cr[1],
        ]
        spots = lax.broadcasted_iota(jnp.int32, (PATCH, 384), 1)
        put = jnp.where(
            spots == lax.broadcasted_iota(jnp.int32, (PATCH, 384), 0) + shift, 1.0, 0.0
        ).astype(BF)
        for c in range(2):
            high = grad[c].astype(BF)
            low = (grad[c] - high.astype(F32)).astype(BF)
            moved = jnp.dot(high, put, preferred_element_type=F32) + jnp.dot(
                low, put, preferred_element_type=F32
            )
            for b in range(3):
                placed[p * 2 + c, b + 1, RIM : RIM + PATCH, :] = moved[:, b * BLK : (b + 1) * BLK]
        return carry

    lax.fori_loop(0, 2, forward_patch, 0)

    def cells_at(c, row_chunk, lane_block):
        total_cells = None
        for p in range(2):
            u, v = corner(p)
            row = jnp.minimum(jnp.maximum(row_chunk * RIM - u + RIM, 0), PATCH + RIM)
            lane = jnp.minimum(jnp.maximum(lane_block - (v >> 7), -1), 3) + 1
            term = placed[p * 2 + c, lane, pl.ds(row, RIM), :]
            total_cells = term if total_cells is None else total_cells + term
        return total_cells

    rim_chunk = 9 * oy
    rim_block = 5 * ox
    for c in range(2):
        for b in range(4):
            rim_row[c, :, b * BLK : (b + 1) * BLK] = cells_at(c, rim_chunk, b + 1).astype(BF)
        rim_cor[c] = cells_at(c, rim_chunk, rim_block).astype(BF)

    def rim_columns(r, carry):
        for c in range(2):
            rim_col[c, pl.ds(pl.multiple_of(r * RIM, RIM), RIM), :] = cells_at(
                c, r + 1, rim_block
            ).astype(BF)
        return carry

    lax.fori_loop(0, 8, rim_columns, 0)
    outs = [
        pltpu.make_async_copy(src, dst, out_sem.at[i])
        for i, (src, dst) in enumerate(
            [
                (rim_row, row_out), (rim_col, col_out), (rim_cor, cor_out),
                (og, og_out), (part, part_out), (ramp, ramp_out), (bv, bv_out),
            ]
        )
    ]
    for copy in outs[:3]:
        copy.start()
    for copy in picks:
        copy.wait()
    for copy in outs[5:]:
        copy.start()

    def interior(r, carry):
        for c in range(2):
            for b in range(4):
                og[c, pl.ds(pl.multiple_of(r * RIM, RIM), RIM), b * BLK : (b + 1) * BLK] = cells_at(
                    c, r + 1, b + 1
                )
        return carry

    lax.fori_loop(0, 8, interior, 0)

    outs[3].start()

    for m in range(2):
        part[2 * m] = (
            patch[0, 0] * chi[0, m, :, 0:PATCH] + patch[0, 1] * chi[0, m, :, PATCH:]
            + patch[1, 0] * chi[1, m, :, 0:PATCH] + patch[1, 1] * chi[1, m, :, PATCH:]
        ).astype(BF)
        part[2 * m + 1] = (
            patch[0, 0] * chi[0, m, :, PATCH:] - patch[0, 1] * chi[0, m, :, 0:PATCH]
            + patch[1, 0] * chi[1, m, :, PATCH:] - patch[1, 1] * chi[1, m, :, 0:PATCH]
        ).astype(BF)
    outs[4].start()
    for copy in outs:
        copy.wait()


def regroup_kernel(
    angles,
    og_ref, row_ref, col_ref, cor_ref, part_ref, ramp_ref, bv_ref,
    og_out, total_out, inbox_out,
    og, part, ramp, bv, got_row, got_col, got_cor, part_got, total_send, total, sino, msgs, inbox,
    load_sem, rim_send, rim_recv,
    part_ssem, part_rsem, tot_ssem, tot_rsem, a2a_send, a2a_recv, own_sem, out_sem,
):
    ang, sy, sx = lax.axis_index("ang"), lax.axis_index("sy"), lax.axis_index("sx")
    oy, ox = 1 - sy, 1 - sx
    group = 2 * angles
    me = ang * 2 + sx
    tile = sy * 2 + sx

    barrier = pltpu.get_barrier_semaphore()
    for dev in ((ang, oy, sx), (ang, oy, ox)):
        pl.semaphore_signal(barrier, inc=1, device_id=dev, device_id_type=MESH)

    def greet(k, carry):
        d = lax.rem(me + k, group)
        pl.semaphore_signal(
            barrier, inc=1, device_id=(d // 2, sy, lax.rem(d, 2)), device_id_type=MESH
        )
        return carry

    lax.fori_loop(1, group, greet, 0)
    loads = [
        pltpu.make_async_copy(src, dst, load_sem.at[i])
        for i, (src, dst) in enumerate(
            [(og_ref, og), (ramp_ref, ramp), (bv_ref, bv), (part_ref.at[tile], part)]
        )
    ]
    for copy in loads:
        copy.start()
    pl.semaphore_wait(barrier, group + 1)

    rims = [
        pltpu.make_async_remote_copy(
            src_ref=src, dst_ref=dst, send_sem=rim_send.at[i], recv_sem=rim_recv.at[i],
            device_id=dev, device_id_type=MESH,
        )
        for i, (src, dst, dev) in enumerate(
            [
                (row_ref, got_row, (ang, oy, sx)),
                (col_ref, got_col, (ang, sy, ox)),
                (cor_ref, got_cor, (ang, oy, ox)),
            ]
        )
    ]
    for copy in rims:
        copy.start()
    others = [(sy, ox), (oy, sx), (oy, ox)]
    part_copies = [
        pltpu.make_async_remote_copy(
            src_ref=part_ref.at[ty * 2 + tx], dst_ref=part_got.at[i],
            send_sem=part_ssem.at[i], recv_sem=part_rsem.at[i],
            device_id=(ang, ty, tx), device_id_type=MESH,
        )
        for i, (ty, tx) in enumerate(others)
    ]
    for copy in part_copies:
        copy.start()
    for copy in loads:
        copy.wait()
    for copy in rims:
        copy.wait()
    row_at = pl.ds(pl.multiple_of((TILE - RIM) * oy, RIM), RIM)
    col_at = pl.ds(pl.multiple_of((TILE - BLK) * ox, BLK), BLK)
    for c in range(2):
        og[c, row_at, :] = og[c, row_at, :] + got_row[c].astype(F32)
        og[c, :, col_at] = og[c, :, col_at] + got_col[c].astype(F32)
        og[c, row_at, col_at] = og[c, row_at, col_at] + got_cor[c].astype(F32)
    og_copy = pltpu.make_async_copy(og, og_out, out_sem.at[0])
    og_copy.start()

    sino[...] = og[...].astype(BF).reshape(2 * TILE, TILE)
    lines = []
    for s in range(2):
        filtered = jnp.dot(sino[...], ramp[s], preferred_element_type=F32).astype(BF)
        lines.append(jnp.dot(filtered, bv[s], preferred_element_type=F32))
    top = lax.broadcasted_iota(jnp.int32, (64, 8, BLK), 1) < 4
    for s in range(2):
        a = lines[s][0:TILE].reshape(64, 8, BLK)
        b = lines[s][TILE:].reshape(64, 8, BLK)
        lanes = slice(s * BLK, (s + 1) * BLK)
        msgs[:, 0, :, lanes] = jnp.where(top, a, pltpu.roll(b, 4, 1)).astype(BF)
        msgs[:, 1, :, lanes] = jnp.where(top, pltpu.roll(a, 4, 1), b).astype(BF)

    def send(k, carry):
        d = lax.rem(me + k, group)
        pltpu.make_async_remote_copy(
            src_ref=msgs.at[d // 2, lax.rem(d, 2)], dst_ref=inbox.at[me],
            send_sem=a2a_send, recv_sem=a2a_recv,
            device_id=(d // 2, sy, lax.rem(d, 2)), device_id_type=MESH,
        ).start()
        return carry

    lax.fori_loop(1, group, send, 0)
    own = pltpu.make_async_copy(msgs.at[ang, sx], inbox.at[me], own_sem)
    own.start()

    for copy in part_copies:
        copy.wait()
    summed = part[...].astype(F32) + part_got[0].astype(F32) + part_got[1].astype(F32) + part_got[2].astype(F32)
    total_send[...] = summed.astype(BF)
    total[tile] = total_send[...]
    total_copies = [
        pltpu.make_async_remote_copy(
            src_ref=total_send, dst_ref=total.at[tile],
            send_sem=tot_ssem.at[i], recv_sem=tot_rsem.at[i],
            device_id=(ang, ty, tx), device_id_type=MESH,
        )
        for i, (ty, tx) in enumerate(others)
    ]
    for copy in total_copies:
        copy.start()

    own.wait()
    pltpu.make_async_copy(
        inbox.at[pl.ds(0, group - 1)], inbox.at[pl.ds(0, group - 1)], a2a_recv
    ).wait()
    inbox_copy = pltpu.make_async_copy(inbox, inbox_out, out_sem.at[1])
    inbox_copy.start()
    for copy in total_copies:
        copy.wait()
    total_copy = pltpu.make_async_copy(total, total_out, out_sem.at[2])
    total_copy.start()
    pltpu.make_async_copy(
        inbox.at[pl.ds(0, group - 1)], inbox.at[pl.ds(0, group - 1)], a2a_send
    ).wait()
    og_copy.wait()
    inbox_copy.wait()
    total_copy.wait()


def finish_kernel(
    angles, bi_ref, og_ref, total_ref, inbox_ref, og_out, pg_out, vol_out,
    og, total, pg, inbox, vol, seen, in_sem, og_sem, out_sem,
):
    arrived = pltpu.make_async_copy(inbox_ref, inbox, in_sem.at[0])
    summed = pltpu.make_async_copy(total_ref, total, in_sem.at[1])
    arrived.start()
    summed.start()
    pieces = [
        (
            pltpu.make_async_copy(og_ref.at[:, pl.ds(i * 128, 128)], og.at[:, pl.ds(i * 128, 128)], og_sem.at[i]),
            pltpu.make_async_copy(og.at[:, pl.ds(i * 128, 128)], og_out.at[0, :, pl.ds(i * 128, 128)], og_sem.at[i + 4]),
        )
        for i in range(4)
    ]
    for load, _ in pieces:
        load.start()
    for a in range(angles):
        seen[a] = 0
    summed.wait()
    for q in range(4):
        pg[0, q // 2, q % 2] = total[q].astype(F32) * (1.0 / math.sqrt(8.0))
    pg_copy = pltpu.make_async_copy(pg, pg_out, out_sem.at[0])
    pg_copy.start()
    for load, store in pieces:
        load.wait()
        store.start()
    arrived.wait()
    for b in range(8):
        line = jnp.zeros((8, BLK), F32)
        for k in range(16):
            source = bi_ref[b, k] >> 3
            slot = seen[source]
            seen[source] = 1
            lane = pl.multiple_of(slot * BLK, BLK)
            for h in range(2):
                line = line + inbox[source * 2 + h, :, pl.ds(lane, BLK)].astype(F32)
        for c in range(2):
            for r in range(4):
                vol[0, r, c, b * BLK : (b + 1) * BLK] = line[c * 4 + r]
    vol_copy = pltpu.make_async_copy(vol, vol_out, out_sem.at[1])
    vol_copy.start()
    for _, store in pieces:
        store.wait()
    pg_copy.wait()
    vol_copy.wait()


def body(angles, tables, objects, probe, data, positions, block_index, block_values):
    forward, backward, ramp = (jnp.asarray(t) for t in tables)
    group = 2 * angles
    dma = pltpu.SemaphoreType.DMA
    smem = pl.BlockSpec(memory_space=pltpu.SMEM)
    hbm = pl.BlockSpec(memory_space=pl.ANY)

    def shape(dims, kind):
        return jax.ShapeDtypeStruct(dims, kind)

    rim_shapes = (shape((2, RIM, TILE), BF), shape((2, TILE, BLK), BF), shape((2, RIM, BLK), BF))
    halos = pl.pallas_call(
        strips_kernel,
        out_shape=rim_shapes,
        in_specs=[hbm],
        out_specs=[hbm] * 3,
        scratch_shapes=[dma((3,)), dma((3,))],
        compiler_params=pltpu.CompilerParams(collective_id=0, has_side_effects=True),
    )(objects)
    og_part, row, col, cor, parts, ramp_two, bv_two = pl.pallas_call(
        functools.partial(patch_kernel, angles),
        out_shape=(shape((2, TILE, TILE), F32),) + rim_shapes + (
            shape((4, PATCH, PATCH), BF), shape((2, TILE, BLK), BF), shape((2, BLK, BLK), BF),
        ),
        in_specs=[smem] * 2 + [hbm] * 10,
        out_specs=[hbm] * 7,
        scratch_shapes=[
            pltpu.VMEM((2, ROWS, COLS), BF),
            pltpu.VMEM((2, 2, PATCH, PATCH), F32),
            pltpu.VMEM((2, PATCH, PATCH), BF),
            pltpu.VMEM((512, 512), BF),
            pltpu.VMEM((512, 512), BF),
            pltpu.VMEM((2, TILE, BLK), BF),
            pltpu.VMEM((2, BLK, BLK), BF),
            pltpu.VMEM((2, 2, 272, BLK), F32),
            pltpu.VMEM((2, 2, PATCH, PATCH), F32),
            pltpu.VMEM((2, 512, PATCH), BF),
            pltpu.VMEM((2, PATCH, 512), BF),
            pltpu.VMEM((2, PATCH, 512), F32),
            pltpu.VMEM((2, 2, PATCH, 512), F32),
            pltpu.VMEM((4, 5, 384, BLK), F32),
            pltpu.VMEM((2, TILE, TILE), F32),
            pltpu.VMEM((2, RIM, TILE), BF),
            pltpu.VMEM((2, TILE, BLK), BF),
            pltpu.VMEM((2, RIM, BLK), BF),
            pltpu.VMEM((4, PATCH, PATCH), BF),
            dma((8,)), dma((4,)), dma((7,)),
        ],
        compiler_params=pltpu.CompilerParams(vmem_limit_bytes=40 * 1024 * 1024),
    )(positions, block_index, objects, *halos, probe, data, forward, backward, ramp, block_values)
    og, total, inbox = pl.pallas_call(
        functools.partial(regroup_kernel, angles),
        out_shape=(
            shape((2, TILE, TILE), F32), shape((4, PATCH, PATCH), BF), shape((group, 8, 2 * BLK), BF),
        ),
        in_specs=[hbm] * 7,
        out_specs=[hbm] * 3,
        scratch_shapes=[
            pltpu.VMEM((2, TILE, TILE), F32),
            pltpu.VMEM((PATCH, PATCH), BF),
            pltpu.VMEM((2, TILE, BLK), BF),
            pltpu.VMEM((2, BLK, BLK), BF),
            pltpu.VMEM((2, RIM, TILE), BF),
            pltpu.VMEM((2, TILE, BLK), BF),
            pltpu.VMEM((2, RIM, BLK), BF),
            pltpu.VMEM((3, PATCH, PATCH), BF),
            pltpu.VMEM((PATCH, PATCH), BF),
            pltpu.VMEM((4, PATCH, PATCH), BF),
            pltpu.VMEM((2 * TILE, TILE), BF),
            pltpu.VMEM((group // 2, 2, 8, 2 * BLK), BF),
            pltpu.VMEM((group, 8, 2 * BLK), BF),
            dma((4,)), dma((3,)), dma((3,)),
            dma((3,)), dma((3,)), dma((3,)), dma((3,)), dma, dma, dma, dma((3,)),
        ],
        compiler_params=pltpu.CompilerParams(
            collective_id=1, has_side_effects=True, vmem_limit_bytes=40 * 1024 * 1024
        ),
    )(og_part, row, col, cor, parts, ramp_two, bv_two)
    return pl.pallas_call(
        functools.partial(finish_kernel, angles),
        out_shape=(
            shape((1, 2, TILE, TILE), F32), shape((1, 2, 2, PATCH, PATCH), F32), shape((1, 4, 2, 1024), F32),
        ),
        in_specs=[smem] + [hbm] * 3,
        out_specs=[hbm] * 3,
        scratch_shapes=[
            pltpu.VMEM((2, TILE, TILE), F32),
            pltpu.VMEM((4, PATCH, PATCH), BF),
            pltpu.VMEM((1, 2, 2, PATCH, PATCH), F32),
            pltpu.VMEM((group, 8, 2 * BLK), BF),
            pltpu.VMEM((1, 4, 2, 1024), F32),
            pltpu.SMEM((angles,), jnp.int32),
            dma((2,)), dma((8,)), dma((2,)),
        ],
        compiler_params=pltpu.CompilerParams(vmem_limit_bytes=40 * 1024 * 1024),
    )(block_index, og, total, inbox)


def solution(mesh):
    tables = dft_tables() + (ramp_blocks(8),)
    return jax.shard_map(
        functools.partial(body, mesh.shape["ang"], tables),
        mesh=mesh,
        in_specs=(
            P("ang", None, "sy", "sx"),
            P(),
            P("ang", "sy", "sx", None, None, None),
            P("ang", "sy", "sx", None, None),
            P(),
            P(),
        ),
        out_specs=(
            P("ang", None, "sy", "sx"),
            P("ang", None, None, None, None),
            P("sy", ("ang", "sx"), None, None),
        ),
        check_vma=False,
    )
```

```python
import functools
import math

import jax
import jax.numpy as jnp
import numpy as np
from jax import lax
from jax.experimental import pallas as pl
from jax.experimental.pallas import tpu as pltpu
from jax.sharding import PartitionSpec as P

PATCH = 256
RIM = 64
BLK = 128
TILE = 512
ROWS = 640
COLS = 768
MESH = pl.DeviceIdType.MESH
BF = jnp.bfloat16
F32 = jnp.float32


def dft_tables():
    ids = np.arange(PATCH)
    phases = (np.outer(ids, ids) % PATCH).astype(np.float64) * (2.0 * math.pi / PATCH)
    factor = 1.0 / math.sqrt(PATCH)
    real = (np.cos(phases) * factor).astype(np.float32)
    imag = (-np.sin(phases) * factor).astype(np.float32)
    forward = np.block([[real, -imag], [imag, real]])
    backward = np.block([[real, imag], [-imag, real]])
    return forward.astype(BF), backward.astype(BF)


def ramp_blocks(line_blocks):
    x = np.arange((2 * line_blocks - 1) * BLK)
    n = np.arange(BLK)[None, :] - (x - (line_blocks - 1) * BLK)[:, None]
    odd = n % 2 != 0
    scaled = n.astype(np.float32) * np.float32(math.pi)
    values = np.where(odd, -1.0 / np.maximum(scaled * scaled, 1.0), 0.0)
    values = np.where(n == 0, 0.25, values).astype(np.float32)
    return values.astype(BF)


def swap_halves(cells):
    return pltpu.roll(cells, BLK // 2, cells.ndim - 1)


def strips_kernel(obj_ref, row_out, col_out, cor_out, block, packed, load_sem, send_sem, recv_sem):
    ang, sy, sx = lax.axis_index("ang"), lax.axis_index("sy"), lax.axis_index("sx")
    oy, ox = 1 - sy, 1 - sx
    devices = [(ang, oy, sx), (ang, sy, ox), (ang, oy, ox)]
    rows = pl.ds(pl.multiple_of((TILE - RIM) * oy, RIM), RIM)
    cols = pl.ds(pl.multiple_of((TILE - BLK) * ox, BLK), BLK)
    load = pltpu.make_async_copy(obj_ref.at[0, :, :, cols], block, load_sem)
    load.start()
    barrier = pltpu.get_barrier_semaphore()
    for dev in devices:
        pl.semaphore_signal(barrier, inc=1, device_id=dev, device_id_type=MESH)
    load.wait()
    real, imag = block[0].astype(F32), block[1].astype(F32)
    low = lax.broadcasted_iota(jnp.int32, (TILE, BLK), 1) < RIM
    packed[...] = jnp.where(
        low, jnp.where(sx == 0, swap_halves(real), real), jnp.where(sx == 0, imag, swap_halves(imag))
    ).astype(BF)
    pl.semaphore_wait(barrier, 3)
    sources = [obj_ref.at[0, :, rows, :], packed, packed.at[rows]]
    copies = [
        pltpu.make_async_remote_copy(
            src_ref=src, dst_ref=dst, send_sem=send_sem.at[i], recv_sem=recv_sem.at[i],
            device_id=dev, device_id_type=MESH,
        )
        for i, (src, dst, dev) in enumerate(zip(sources, (row_out, col_out, cor_out), devices))
    ]
    for copy in copies:
        copy.start()
    for copy in copies:
        copy.wait()


def patch_kernel(
    angles,
    pos_ref, bi_ref,
    obj_ref, halo_row, halo_col, halo_cor, probe_ref, data_ref, fwd_ref, bwd_ref, ramp_ref, bv_ref,
    og_out, row_out, col_out, cor_out, part_out, ramp_out, bv_out,
    big, side, probe, data, fwd, bwd, ramp, bv,
    win, patch, exits, half, far, chi, placed, og,
    rim_row, rim_col, rim_cor, part,
    load_sem, pick_sem, out_sem,
):
    ang, sy, sx = lax.axis_index("ang"), lax.axis_index("sy"), lax.axis_index("sx")
    oy, ox = 1 - sy, 1 - sx
    dst_row = pl.ds(pl.multiple_of((ROWS - RIM) * oy, RIM), RIM)
    dst_col = pl.ds(pl.multiple_of((COLS - BLK) * ox, BLK), BLK)
    loads = [
        pltpu.make_async_copy(src, dst, load_sem.at[i])
        for i, (src, dst) in enumerate(
            [
                (obj_ref.at[0], big.at[:, pl.ds(RIM, TILE), pl.ds(BLK, TILE)]),
                (halo_row, big.at[:, dst_row, pl.ds(BLK, TILE)]),
                (halo_col, side.at[pl.ds(RIM, TILE)]),
                (halo_cor, side.at[dst_row]),
                (probe_ref, probe),
                (fwd_ref, fwd),
                (bwd_ref, bwd),
                (data_ref.at[0, 0, 0], data),
            ]
        )
    ]
    for copy in loads:
        copy.start()

    big[:, pl.ds(pl.multiple_of((ROWS - RIM) * sy, RIM), RIM), :] = jnp.zeros((2, RIM, COLS), BF)
    big[:, :, pl.ds(pl.multiple_of((COLS - BLK) * sx, BLK), BLK)] = jnp.zeros((2, ROWS, BLK), BF)
    for q in range(4):
        placed[q, :, 0:RIM, :] = jnp.zeros((5, RIM, BLK), F32)
        placed[q, :, RIM + PATCH :, :] = jnp.zeros((5, RIM, BLK), F32)
        placed[q, 0, RIM : RIM + PATCH, :] = jnp.zeros((PATCH, BLK), F32)
        placed[q, 4, RIM : RIM + PATCH, :] = jnp.zeros((PATCH, BLK), F32)

    named = [(jnp.int32(-1), jnp.int32(0)), (jnp.int32(0), jnp.int32(0))]
    for j in range(2 * angles):
        entry = bi_ref[j // 16, j % 16]
        mine = (entry >> 3) == ang
        early = jnp.logical_and(mine, named[0][0] < 0)
        named = [
            (jnp.where(take, j, at), jnp.where(take, entry & 7, column))
            for take, (at, column) in zip((early, mine), named)
        ]
    named[0] = (jnp.maximum(named[0][0], 0), named[0][1])
    picks = []
    for s, (entry, column) in enumerate(named):
        at = pl.multiple_of((7 - column + 4 * sx) * BLK, BLK)
        picks.append(
            pltpu.make_async_copy(ramp_ref.at[pl.ds(at, TILE), :], ramp.at[s], pick_sem.at[2 * s])
        )
        picks.append(
            pltpu.make_async_copy(bv_ref.at[entry >> 4, entry & 15], bv.at[s], pick_sem.at[2 * s + 1])
        )
    for copy in picks:
        copy.start()
    side[pl.ds(pl.multiple_of((ROWS - RIM) * sy, RIM), RIM), :] = jnp.zeros((RIM, BLK), BF)
    for copy in loads:
        copy.wait()
    wide = side[...].astype(F32)
    turned = swap_halves(wide)
    big[0, :, dst_col] = jnp.where(sx == 1, turned, wide).astype(BF)
    big[1, :, dst_col] = jnp.where(sx == 1, wide, turned).astype(BF)

    def corner(p):
        return pos_ref[0, 0, 0, p, 0], pos_ref[0, 0, 0, p, 1] + RIM

    def forward_patch(p, carry):
        u, v = corner(p)
        base = jnp.minimum(u >> 4, 23) * 16
        lead = u - base
        block, shift = v >> 7, v & (BLK - 1)
        across = lax.broadcasted_iota(jnp.int32, (384, PATCH), 0)
        pick = jnp.where(
            across == lax.broadcasted_iota(jnp.int32, (384, PATCH), 1) + shift, 1.0, 0.0
        ).astype(BF)
        for c in range(2):
            cells = big[
                c, pl.ds(pl.multiple_of(base, 16), 272), pl.ds(pl.multiple_of(block * BLK, BLK), 384)
            ]
            cells = jnp.dot(cells, pick, preferred_element_type=F32)
            for b in range(2):
                win[c, b] = cells[:, b * BLK : (b + 1) * BLK]
        for c in range(2):
            for b in range(2):
                patch[p, c, :, b * BLK : (b + 1) * BLK] = win[c, b, pl.ds(lead, PATCH), :]
        for m in range(2):
            exits[m, 0:PATCH] = (probe[m, 0] * patch[p, 0] - probe[m, 1] * patch[p, 1]).astype(BF)
            exits[m, PATCH:] = (probe[m, 0] * patch[p, 1] + probe[m, 1] * patch[p, 0]).astype(BF)
        for m in range(2):
            done = jnp.dot(fwd[...], exits[m], preferred_element_type=F32)
            half[m, :, 0:PATCH] = done[0:PATCH].astype(BF)
            half[m, :, PATCH:] = done[PATCH:].astype(BF)
        for m in range(2):
            far[m] = jnp.dot(half[m], bwd[...], preferred_element_type=F32)
        misfit = (
            far[0, :, 0:PATCH] * far[0, :, 0:PATCH]
            + far[0, :, PATCH:] * far[0, :, PATCH:]
            + far[1, :, 0:PATCH] * far[1, :, 0:PATCH]
            + far[1, :, PATCH:] * far[1, :, PATCH:]
            - data[p].astype(F32)
        )
        for m in range(2):
            exits[m, 0:PATCH] = (misfit * far[m, :, 0:PATCH]).astype(BF)
            exits[m, PATCH:] = (misfit * far[m, :, PATCH:]).astype(BF)
        for m in range(2):
            done = jnp.dot(bwd[...], exits[m], preferred_element_type=F32)
            half[m, :, 0:PATCH] = done[0:PATCH].astype(BF)
            half[m, :, PATCH:] = done[PATCH:].astype(BF)
        for m in range(2):
            chi[p, m] = jnp.dot(half[m], fwd[...], preferred_element_type=F32)
        cr = [chi[p, m, :, 0:PATCH] for m in range(2)]
        ci = [chi[p, m, :, PATCH:] for m in range(2)]
        grad = [
            probe[0, 0] * cr[0] + probe[0, 1] * ci[0] + probe[1, 0] * cr[1] + probe[1, 1] * ci[1],
            probe[0, 0] * ci[0] - probe[0, 1] * cr[0] + probe[1, 0] * ci[1] - probe[1, 1] * cr[1],
        ]
        spots = lax.broadcasted_iota(jnp.int32, (PATCH, 384), 1)
        put = jnp.where(
            spots == lax.broadcasted_iota(jnp.int32, (PATCH, 384), 0) + shift, 1.0, 0.0
        ).astype(BF)
        for c in range(2):
            high = grad[c].astype(BF)
            low = (grad[c] - high.astype(F32)).astype(BF)
            moved = jnp.dot(high, put, preferred_element_type=F32) + jnp.dot(
                low, put, preferred_element_type=F32
            )
            for b in range(3):
                placed[p * 2 + c, b + 1, RIM : RIM + PATCH, :] = moved[:, b * BLK : (b + 1) * BLK]
        return carry

    lax.fori_loop(0, 2, forward_patch, 0)

    def cells_at(c, row_chunk, lane_block):
        total_cells = None
        for p in range(2):
            u, v = corner(p)
            row = jnp.minimum(jnp.maximum(row_chunk * RIM - u + RIM, 0), PATCH + RIM)
            lane = jnp.minimum(jnp.maximum(lane_block - (v >> 7), -1), 3) + 1
            term = placed[p * 2 + c, lane, pl.ds(row, RIM), :]
            total_cells = term if total_cells is None else total_cells + term
        return total_cells

    rim_chunk = 9 * oy
    rim_block = 5 * ox
    for c in range(2):
        for b in range(4):
            rim_row[c, :, b * BLK : (b + 1) * BLK] = cells_at(c, rim_chunk, b + 1).astype(BF)

    def packed_rim(row_chunk):
        real, imag = (cells_at(c, row_chunk, rim_block) for c in range(2))
        kept, moved = jnp.where(sx == 0, real, imag), jnp.where(sx == 0, imag, real)
        return (kept + swap_halves(moved)).astype(BF)

    rim_cor[...] = packed_rim(rim_chunk)

    def rim_columns(r, carry):
        rim_col[pl.ds(pl.multiple_of(r * RIM, RIM), RIM), :] = packed_rim(r + 1)
        return carry

    lax.fori_loop(0, 8, rim_columns, 0)
    outs = [
        pltpu.make_async_copy(src, dst, out_sem.at[i])
        for i, (src, dst) in enumerate(
            [
                (rim_row, row_out), (rim_col, col_out), (rim_cor, cor_out),
                (og, og_out), (part, part_out), (ramp, ramp_out), (bv, bv_out),
            ]
        )
    ]
    for copy in outs[:3]:
        copy.start()
    for copy in picks:
        copy.wait()
    for copy in outs[5:]:
        copy.start()

    def interior(r, carry):
        for c in range(2):
            for b in range(4):
                og[c, pl.ds(pl.multiple_of(r * RIM, RIM), RIM), b * BLK : (b + 1) * BLK] = cells_at(
                    c, r + 1, b + 1
                )
        return carry

    lax.fori_loop(0, 8, interior, 0)

    outs[3].start()

    for m in range(2):
        part[2 * m] = (
            patch[0, 0] * chi[0, m, :, 0:PATCH] + patch[0, 1] * chi[0, m, :, PATCH:]
            + patch[1, 0] * chi[1, m, :, 0:PATCH] + patch[1, 1] * chi[1, m, :, PATCH:]
        ).astype(BF)
        part[2 * m + 1] = (
            patch[0, 0] * chi[0, m, :, PATCH:] - patch[0, 1] * chi[0, m, :, 0:PATCH]
            + patch[1, 0] * chi[1, m, :, PATCH:] - patch[1, 1] * chi[1, m, :, 0:PATCH]
        ).astype(BF)
    outs[4].start()
    for copy in outs:
        copy.wait()


def regroup_kernel(
    angles,
    og_ref, row_ref, col_ref, cor_ref, part_ref, ramp_ref, bv_ref,
    og_out, total_out, inbox_out,
    og, part, ramp, bv, got_row, got_col, got_cor, half_got, half_sum, quarter_send, quarter_got, total,
    sino, msgs, inbox,
    load_sem, rim_send, rim_recv, part_ssem, part_rsem, word_sem, a2a_send, a2a_recv, own_sem, out_sem,
):
    ang, sy, sx = lax.axis_index("ang"), lax.axis_index("sy"), lax.axis_index("sx")
    oy, ox = 1 - sy, 1 - sx
    group = 2 * angles
    me = ang * 2 + sx
    tile = sy * 2 + sx

    barrier = pltpu.get_barrier_semaphore()
    steps = group.bit_length() - 1
    partners = []
    for r in range(steps):
        d = jnp.bitwise_xor(me, 1 << r)
        partners.append((d >> 1, sy, d & 1))
    for dev in [(ang, oy, sx), (ang, oy, ox)] + partners:
        pl.semaphore_signal(barrier, inc=1, device_id=dev, device_id_type=MESH)
    loads = [
        pltpu.make_async_copy(src, dst, load_sem.at[i])
        for i, (src, dst) in enumerate(
            [(og_ref, og), (ramp_ref, ramp), (bv_ref, bv), (part_ref.at[pl.ds(2 * sy, 2)], part)]
        )
    ]
    for copy in loads:
        copy.start()
    pl.semaphore_wait(barrier, steps + 2)

    rims = [
        pltpu.make_async_remote_copy(
            src_ref=src, dst_ref=dst, send_sem=rim_send.at[i], recv_sem=rim_recv.at[i],
            device_id=dev, device_id_type=MESH,
        )
        for i, (src, dst, dev) in enumerate(
            [
                (row_ref, got_row, (ang, oy, sx)),
                (col_ref, got_col, (ang, sy, ox)),
                (cor_ref, got_cor, (ang, oy, ox)),
            ]
        )
    ]
    for copy in rims:
        copy.start()
    def exchange(i, src, dst, dev):
        return pltpu.make_async_remote_copy(
            src_ref=src, dst_ref=dst, send_sem=part_ssem.at[i], recv_sem=part_rsem.at[i],
            device_id=dev, device_id_type=MESH,
        )

    across, beside = (ang, oy, ox), (ang, sy, ox)
    halves = exchange(0, part_ref.at[pl.ds(2 * oy, 2)], half_got, across)
    halves.start()
    for copy in loads:
        copy.wait()
    for r in range(steps):
        pl.semaphore_signal(word_sem.at[r], inc=1, device_id=partners[r], device_id_type=MESH)
        pl.semaphore_wait(word_sem.at[r], 1)
    for copy in rims:
        copy.wait()
    halves.wait()
    half_sum[...] = part[...].astype(F32) + half_got[...].astype(F32)
    quarter_send[...] = half_sum[ox].astype(BF)
    quarters = exchange(1, quarter_send, quarter_got, beside)
    quarters.start()
    row_at = pl.ds(pl.multiple_of((TILE - RIM) * oy, RIM), RIM)
    col_at = pl.ds(pl.multiple_of((TILE - BLK) * ox, BLK), BLK)
    for c in range(2):
        og[c, row_at, :] = og[c, row_at, :] + got_row[c].astype(F32)
    first = lax.broadcasted_iota(jnp.int32, (TILE, BLK), 1) < RIM
    for got, at in ((got_col, pl.ds(0, TILE)), (got_cor, row_at)):
        wide = got[...].astype(F32)
        turned = swap_halves(wide)
        low = first[: wide.shape[0]]
        added = (
            jnp.where(sx == 1, jnp.where(low, wide, 0.0), jnp.where(low, 0.0, turned)),
            jnp.where(sx == 1, jnp.where(low, turned, 0.0), jnp.where(low, 0.0, wide)),
        )
        for c in range(2):
            og[c, at, col_at] = og[c, at, col_at] + added[c]
    og_copy = pltpu.make_async_copy(og, og_out, out_sem.at[0])
    og_copy.start()

    sino[...] = og[...].astype(BF).reshape(2 * TILE, TILE)
    lines = []
    for s in range(2):
        filtered = jnp.dot(sino[...], ramp[s], preferred_element_type=F32).astype(BF)
        lines.append(jnp.dot(filtered, bv[s], preferred_element_type=F32))
    top = lax.broadcasted_iota(jnp.int32, (64, 8, BLK), 1) < 4
    for s in range(2):
        a = lines[s][0:TILE].reshape(64, 8, BLK)
        b = lines[s][TILE:].reshape(64, 8, BLK)
        lanes = slice(s * BLK, (s + 1) * BLK)
        msgs[:, 0, :, lanes] = jnp.where(top, a, pltpu.roll(b, 4, 1)).astype(BF)
        msgs[:, 1, :, lanes] = jnp.where(top, pltpu.roll(a, 4, 1), b).astype(BF)

    def send(k, carry):
        d = lax.rem(me + k, group)
        pltpu.make_async_remote_copy(
            src_ref=msgs.at[d // 2, lax.rem(d, 2)], dst_ref=inbox.at[me],
            send_sem=a2a_send, recv_sem=a2a_recv,
            device_id=(d // 2, sy, lax.rem(d, 2)), device_id_type=MESH,
        ).start()
        return carry

    lax.fori_loop(1, group, send, 0)
    own = pltpu.make_async_copy(msgs.at[ang, sx], inbox.at[me], own_sem)
    own.start()

    quarters.wait()
    total[tile] = (half_sum[sx] + quarter_got[...].astype(F32)).astype(BF)
    shared = exchange(2, total.at[tile], total.at[tile], beside)
    shared.start()
    shared.wait()
    mine = pl.ds(2 * sy, 2)
    rest = exchange(3, total.at[mine], total.at[mine], across)
    rest.start()
    own.wait()
    pltpu.make_async_copy(
        inbox.at[pl.ds(0, group - 1)], inbox.at[pl.ds(0, group - 1)], a2a_recv
    ).wait()
    inbox_copy = pltpu.make_async_copy(inbox, inbox_out, out_sem.at[1])
    inbox_copy.start()
    rest.wait()
    total_copy = pltpu.make_async_copy(total, total_out, out_sem.at[2])
    total_copy.start()
    pltpu.make_async_copy(
        inbox.at[pl.ds(0, group - 1)], inbox.at[pl.ds(0, group - 1)], a2a_send
    ).wait()
    og_copy.wait()
    inbox_copy.wait()
    total_copy.wait()


def finish_kernel(
    angles, bi_ref, og_ref, total_ref, inbox_ref, og_out, pg_out, vol_out,
    og, total, pg, inbox, vol, seen, in_sem, og_sem, out_sem,
):
    arrived = pltpu.make_async_copy(inbox_ref, inbox, in_sem.at[0])
    summed = pltpu.make_async_copy(total_ref, total, in_sem.at[1])
    arrived.start()
    summed.start()
    pieces = [
        (
            pltpu.make_async_copy(og_ref.at[:, pl.ds(i * 128, 128)], og.at[:, pl.ds(i * 128, 128)], og_sem.at[i]),
            pltpu.make_async_copy(og.at[:, pl.ds(i * 128, 128)], og_out.at[0, :, pl.ds(i * 128, 128)], og_sem.at[i + 4]),
        )
        for i in range(4)
    ]
    for load, _ in pieces:
        load.start()
    for a in range(angles):
        seen[a] = 0
    summed.wait()
    for q in range(4):
        pg[0, q // 2, q % 2] = total[q].astype(F32) * (1.0 / math.sqrt(8.0))
    pg_copy = pltpu.make_async_copy(pg, pg_out, out_sem.at[0])
    pg_copy.start()
    for load, store in pieces:
        load.wait()
        store.start()
    arrived.wait()
    for b in range(8):
        line = jnp.zeros((8, BLK), F32)
        for k in range(16):
            source = bi_ref[b, k] >> 3
            slot = seen[source]
            seen[source] = 1
            lane = pl.multiple_of(slot * BLK, BLK)
            for h in range(2):
                line = line + inbox[source * 2 + h, :, pl.ds(lane, BLK)].astype(F32)
        for c in range(2):
            for r in range(4):
                vol[0, r, c, b * BLK : (b + 1) * BLK] = line[c * 4 + r]
    vol_copy = pltpu.make_async_copy(vol, vol_out, out_sem.at[1])
    vol_copy.start()
    for _, store in pieces:
        store.wait()
    pg_copy.wait()
    vol_copy.wait()


def body(angles, tables, objects, probe, data, positions, block_index, block_values):
    forward, backward, ramp = (jnp.asarray(t) for t in tables)
    group = 2 * angles
    dma = pltpu.SemaphoreType.DMA
    smem = pl.BlockSpec(memory_space=pltpu.SMEM)
    hbm = pl.BlockSpec(memory_space=pltpu.HBM)

    def shape(dims, kind):
        return jax.ShapeDtypeStruct(dims, kind)

    rim_shapes = (shape((2, RIM, TILE), BF), shape((TILE, BLK), BF), shape((RIM, BLK), BF))
    halos = pl.pallas_call(
        strips_kernel,
        out_shape=rim_shapes,
        in_specs=[hbm],
        out_specs=[hbm] * 3,
        scratch_shapes=[
            pltpu.VMEM((2, TILE, BLK), BF), pltpu.VMEM((TILE, BLK), BF), dma, dma((3,)), dma((3,)),
        ],
        compiler_params=pltpu.CompilerParams(
            collective_id=0, has_side_effects=True, vmem_limit_bytes=62 * 1024 * 1024
        ),
    )(objects)
    og_part, row, col, cor, parts, ramp_two, bv_two = pl.pallas_call(
        functools.partial(patch_kernel, angles),
        out_shape=(shape((2, TILE, TILE), F32),) + rim_shapes + (
            shape((4, PATCH, PATCH), BF), shape((2, TILE, BLK), BF), shape((2, BLK, BLK), BF),
        ),
        in_specs=[smem] * 2 + [hbm] * 10,
        out_specs=[hbm] * 7,
        scratch_shapes=[
            pltpu.VMEM((2, ROWS, COLS), BF),
            pltpu.VMEM((ROWS, BLK), BF),
            pltpu.VMEM((2, 2, PATCH, PATCH), F32),
            pltpu.VMEM((2, PATCH, PATCH), BF),
            pltpu.VMEM((512, 512), BF),
            pltpu.VMEM((512, 512), BF),
            pltpu.VMEM((2, TILE, BLK), BF),
            pltpu.VMEM((2, BLK, BLK), BF),
            pltpu.VMEM((2, 2, 272, BLK), F32),
            pltpu.VMEM((2, 2, PATCH, PATCH), F32),
            pltpu.VMEM((2, 512, PATCH), BF),
            pltpu.VMEM((2, PATCH, 512), BF),
            pltpu.VMEM((2, PATCH, 512), F32),
            pltpu.VMEM((2, 2, PATCH, 512), F32),
            pltpu.VMEM((4, 5, 384, BLK), F32),
            pltpu.VMEM((2, TILE, TILE), F32),
            pltpu.VMEM((2, RIM, TILE), BF),
            pltpu.VMEM((TILE, BLK), BF),
            pltpu.VMEM((RIM, BLK), BF),
            pltpu.VMEM((4, PATCH, PATCH), BF),
            dma((8,)), dma((4,)), dma((7,)),
        ],
        compiler_params=pltpu.CompilerParams(vmem_limit_bytes=62 * 1024 * 1024),
    )(positions, block_index, objects, *halos, probe, data, forward, backward, ramp, block_values)
    og, total, inbox = pl.pallas_call(
        functools.partial(regroup_kernel, angles),
        out_shape=(
            shape((2, TILE, TILE), F32), shape((4, PATCH, PATCH), BF), shape((group, 8, 2 * BLK), BF),
        ),
        in_specs=[hbm] * 7,
        out_specs=[hbm] * 3,
        scratch_shapes=[
            pltpu.VMEM((2, TILE, TILE), F32),
            pltpu.VMEM((2, PATCH, PATCH), BF),
            pltpu.VMEM((2, TILE, BLK), BF),
            pltpu.VMEM((2, BLK, BLK), BF),
            pltpu.VMEM((2, RIM, TILE), BF),
            pltpu.VMEM((TILE, BLK), BF),
            pltpu.VMEM((RIM, BLK), BF),
            pltpu.VMEM((2, PATCH, PATCH), BF),
            pltpu.VMEM((2, PATCH, PATCH), F32),
            pltpu.VMEM((PATCH, PATCH), BF),
            pltpu.VMEM((PATCH, PATCH), BF),
            pltpu.VMEM((4, PATCH, PATCH), BF),
            pltpu.VMEM((2 * TILE, TILE), BF),
            pltpu.VMEM((group // 2, 2, 8, 2 * BLK), BF),
            pltpu.VMEM((group, 8, 2 * BLK), BF),
            dma((4,)), dma((3,)), dma((3,)), dma((4,)), dma((4,)),
            pltpu.SemaphoreType.REGULAR((group.bit_length() - 1,)), dma, dma, dma, dma((3,)),
        ],
        compiler_params=pltpu.CompilerParams(
            collective_id=1, has_side_effects=True, vmem_limit_bytes=62 * 1024 * 1024
        ),
    )(og_part, row, col, cor, parts, ramp_two, bv_two)
    return pl.pallas_call(
        functools.partial(finish_kernel, angles),
        out_shape=(
            shape((1, 2, TILE, TILE), F32), shape((1, 2, 2, PATCH, PATCH), F32), shape((1, 4, 2, 1024), F32),
        ),
        in_specs=[smem] + [hbm] * 3,
        out_specs=[hbm] * 3,
        scratch_shapes=[
            pltpu.VMEM((2, TILE, TILE), F32),
            pltpu.VMEM((4, PATCH, PATCH), BF),
            pltpu.VMEM((1, 2, 2, PATCH, PATCH), F32),
            pltpu.VMEM((group, 8, 2 * BLK), BF),
            pltpu.VMEM((1, 4, 2, 1024), F32),
            pltpu.SMEM((angles,), jnp.int32),
            dma((2,)), dma((8,)), dma((2,)),
        ],
        compiler_params=pltpu.CompilerParams(vmem_limit_bytes=62 * 1024 * 1024),
    )(block_index, og, total, inbox)


def solution(mesh):
    tables = dft_tables() + (ramp_blocks(8),)
    return jax.shard_map(
        functools.partial(body, mesh.shape["ang"], tables),
        mesh=mesh,
        in_specs=(
            P("ang", None, "sy", "sx"),
            P(),
            P("ang", "sy", "sx", None, None, None),
            P("ang", "sy", "sx", None, None),
            P(),
            P(),
        ),
        out_specs=(
            P("ang", None, "sy", "sx"),
            P("ang", None, None, None, None),
            P("sy", ("ang", "sx"), None, None),
        ),
        check_vma=False,
    )
```

```python
import functools
import math

import jax
import jax.numpy as jnp
import numpy as np
from jax import lax
from jax.experimental import pallas as pl
from jax.experimental.pallas import tpu as pltpu
from jax.sharding import PartitionSpec as P

PATCH = 256
RIM = 64
BLK = 128
TILE = 512
ROWS = 640
SPAN = 640
COLS = 768
SECOND = (0, 2, 3, 1)
MESH = pl.DeviceIdType.MESH
BF = jnp.bfloat16
F32 = jnp.float32


def dft_tables():
    ids = np.arange(PATCH)
    phases = (np.outer(ids, ids) % PATCH).astype(np.float64) * (2.0 * math.pi / PATCH)
    factor = 1.0 / math.sqrt(PATCH)
    real = (np.cos(phases) * factor).astype(np.float32)
    imag = (-np.sin(phases) * factor).astype(np.float32)
    forward = np.block([[real, -imag], [imag, real]])
    backward = np.block([[real, imag], [-imag, real]])
    return forward.astype(BF), backward.astype(BF)


def ramp_blocks(line_blocks):
    x = np.arange((2 * line_blocks - 1) * BLK)
    n = np.arange(BLK)[None, :] - (x - (line_blocks - 1) * BLK)[:, None]
    odd = n % 2 != 0
    scaled = n.astype(np.float32) * np.float32(math.pi)
    values = np.where(odd, -1.0 / np.maximum(scaled * scaled, 1.0), 0.0)
    values = np.where(n == 0, 0.25, values).astype(np.float32)
    return values.astype(BF)


def swap_halves(cells):
    return pltpu.roll(cells, BLK // 2, cells.ndim - 1)


def strips_kernel(obj_ref, row_out, col_out, cor_out, block, packed, load_sem, send_sem, recv_sem):
    ang, sy, sx = lax.axis_index("ang"), lax.axis_index("sy"), lax.axis_index("sx")
    oy, ox = 1 - sy, 1 - sx
    devices = [(ang, oy, sx), (ang, sy, ox), (ang, oy, ox)]
    rows = pl.ds(pl.multiple_of((TILE - RIM) * oy, RIM), RIM)
    cols = pl.ds(pl.multiple_of((TILE - BLK) * ox, BLK), BLK)
    load = pltpu.make_async_copy(obj_ref.at[0, :, :, cols], block, load_sem)
    load.start()
    barrier = pltpu.get_barrier_semaphore()
    for dev in devices:
        pl.semaphore_signal(barrier, inc=1, device_id=dev, device_id_type=MESH)
    load.wait()
    real, imag = block[0].astype(F32), block[1].astype(F32)
    low = lax.broadcasted_iota(jnp.int32, (TILE, BLK), 1) < RIM
    packed[...] = jnp.where(
        low, jnp.where(sx == 0, swap_halves(real), real), jnp.where(sx == 0, imag, swap_halves(imag))
    ).astype(BF)
    pl.semaphore_wait(barrier, 3)
    sources = [obj_ref.at[0, :, rows, :], packed, packed.at[rows]]
    copies = [
        pltpu.make_async_remote_copy(
            src_ref=src, dst_ref=dst, send_sem=send_sem.at[i], recv_sem=recv_sem.at[i],
            device_id=dev, device_id_type=MESH,
        )
        for i, (src, dst, dev) in enumerate(zip(sources, (row_out, col_out, cor_out), devices))
    ]
    for copy in copies:
        copy.start()
    for copy in copies:
        copy.wait()


def patch_kernel(
    angles,
    pos_ref, bi_ref,
    obj_ref, halo_row, halo_col, halo_cor, probe_ref, data_ref, fwd_ref, bwd_ref, ramp_ref, bv_ref,
    og_out, row_out, col_out, cor_out, part_out, ramp_out, bv_out, sino_out,
    big, side, probe, data, fwd, bwd, ramp, bv,
    win, patch, exits, half, far, chi, placed, og,
    rim_row, rim_col, rim_cor, part, sino,
    load_sem, pick_sem, out_sem,
):
    ang, sy, sx = lax.axis_index("ang"), lax.axis_index("sy"), lax.axis_index("sx")
    oy, ox = 1 - sy, 1 - sx
    dst_row = pl.ds(pl.multiple_of((ROWS - RIM) * oy, RIM), RIM)
    dst_col = pl.ds(pl.multiple_of((COLS - BLK) * ox, BLK), BLK)
    loads = [
        pltpu.make_async_copy(src, dst, load_sem.at[i])
        for i, (src, dst) in enumerate(
            [
                (obj_ref.at[0], big.at[:, pl.ds(RIM, TILE), pl.ds(BLK, TILE)]),
                (halo_row, big.at[:, dst_row, pl.ds(BLK, TILE)]),
                (halo_col, side.at[pl.ds(RIM, TILE)]),
                (halo_cor, side.at[dst_row]),
                (probe_ref, probe),
                (fwd_ref, fwd),
                (bwd_ref, bwd),
                (data_ref.at[0, 0, 0], data),
            ]
        )
    ]
    for copy in loads:
        copy.start()

    big[:, pl.ds(pl.multiple_of((ROWS - RIM) * sy, RIM), RIM), :] = jnp.zeros((2, RIM, COLS), BF)
    big[:, :, pl.ds(pl.multiple_of((COLS - BLK) * sx, BLK), BLK)] = jnp.zeros((2, ROWS, BLK), BF)
    for q in range(4):
        placed[q, :, 0:RIM, :] = jnp.zeros((5, RIM, BLK), F32)
        placed[q, :, RIM + PATCH :, :] = jnp.zeros((5, RIM, BLK), F32)
        placed[q, 0, RIM : RIM + PATCH, :] = jnp.zeros((PATCH, BLK), F32)
        placed[q, 4, RIM : RIM + PATCH, :] = jnp.zeros((PATCH, BLK), F32)

    named = [(jnp.int32(-1), jnp.int32(0)), (jnp.int32(0), jnp.int32(0))]
    for j in range(2 * angles):
        entry = bi_ref[j // 16, j % 16]
        mine = (entry >> 3) == ang
        early = jnp.logical_and(mine, named[0][0] < 0)
        named = [
            (jnp.where(take, j, at), jnp.where(take, entry & 7, column))
            for take, (at, column) in zip((early, mine), named)
        ]
    named[0] = (jnp.maximum(named[0][0], 0), named[0][1])
    picks = []
    for s, (entry, column) in enumerate(named):
        at = pl.multiple_of((7 - column + 3 * sx) * BLK, BLK)
        picks.append(
            pltpu.make_async_copy(ramp_ref.at[pl.ds(at, SPAN), :], ramp.at[s], pick_sem.at[2 * s])
        )
        picks.append(
            pltpu.make_async_copy(bv_ref.at[entry >> 4, entry & 15], bv.at[s], pick_sem.at[2 * s + 1])
        )
    for copy in picks:
        copy.start()
    side[pl.ds(pl.multiple_of((ROWS - RIM) * sy, RIM), RIM), :] = jnp.zeros((RIM, BLK), BF)
    for copy in loads:
        copy.wait()
    wide = side[...].astype(F32)
    turned = swap_halves(wide)
    big[0, :, dst_col] = jnp.where(sx == 1, turned, wide).astype(BF)
    big[1, :, dst_col] = jnp.where(sx == 1, wide, turned).astype(BF)

    def corner(p):
        return pos_ref[0, 0, 0, p, 0], pos_ref[0, 0, 0, p, 1] + RIM

    def forward_patch(p, carry):
        u, v = corner(p)
        base = jnp.minimum(u >> 4, 23) * 16
        lead = u - base
        block, shift = v >> 7, v & (BLK - 1)
        across = lax.broadcasted_iota(jnp.int32, (384, PATCH), 0)
        pick = jnp.where(
            across == lax.broadcasted_iota(jnp.int32, (384, PATCH), 1) + shift, 1.0, 0.0
        ).astype(BF)
        for c in range(2):
            cells = big[
                c, pl.ds(pl.multiple_of(base, 16), 272), pl.ds(pl.multiple_of(block * BLK, BLK), 384)
            ]
            cells = jnp.dot(cells, pick, preferred_element_type=F32)
            for b in range(2):
                win[c, b] = cells[:, b * BLK : (b + 1) * BLK]
        for c in range(2):
            for b in range(2):
                patch[p, c, :, b * BLK : (b + 1) * BLK] = win[c, b, pl.ds(lead, PATCH), :]
        for m in range(2):
            exits[m, 0:PATCH] = (probe[m, 0] * patch[p, 0] - probe[m, 1] * patch[p, 1]).astype(BF)
            exits[m, PATCH:] = (probe[m, 0] * patch[p, 1] + probe[m, 1] * patch[p, 0]).astype(BF)
        for m in range(2):
            done = jnp.dot(fwd[...], exits[m], preferred_element_type=F32)
            half[m, :, 0:PATCH] = done[0:PATCH].astype(BF)
            half[m, :, PATCH:] = done[PATCH:].astype(BF)
        for m in range(2):
            far[m] = jnp.dot(half[m], bwd[...], preferred_element_type=F32)
        misfit = (
            far[0, :, 0:PATCH] * far[0, :, 0:PATCH]
            + far[0, :, PATCH:] * far[0, :, PATCH:]
            + far[1, :, 0:PATCH] * far[1, :, 0:PATCH]
            + far[1, :, PATCH:] * far[1, :, PATCH:]
            - data[p].astype(F32)
        )
        for m in range(2):
            exits[m, 0:PATCH] = (misfit * far[m, :, 0:PATCH]).astype(BF)
            exits[m, PATCH:] = (misfit * far[m, :, PATCH:]).astype(BF)
        for m in range(2):
            done = jnp.dot(bwd[...], exits[m], preferred_element_type=F32)
            half[m, :, 0:PATCH] = done[0:PATCH].astype(BF)
            half[m, :, PATCH:] = done[PATCH:].astype(BF)
        for m in range(2):
            chi[p, m] = jnp.dot(half[m], fwd[...], preferred_element_type=F32)
        cr = [chi[p, m, :, 0:PATCH] for m in range(2)]
        ci = [chi[p, m, :, PATCH:] for m in range(2)]
        grad = [
            probe[0, 0] * cr[0] + probe[0, 1] * ci[0] + probe[1, 0] * cr[1] + probe[1, 1] * ci[1],
            probe[0, 0] * ci[0] - probe[0, 1] * cr[0] + probe[1, 0] * ci[1] - probe[1, 1] * cr[1],
        ]
        spots = lax.broadcasted_iota(jnp.int32, (PATCH, 384), 1)
        put = jnp.where(
            spots == lax.broadcasted_iota(jnp.int32, (PATCH, 384), 0) + shift, 1.0, 0.0
        ).astype(BF)
        for c in range(2):
            high = grad[c].astype(BF)
            low = (grad[c] - high.astype(F32)).astype(BF)
            moved = jnp.dot(high, put, preferred_element_type=F32) + jnp.dot(
                low, put, preferred_element_type=F32
            )
            for b in range(3):
                placed[p * 2 + c, b + 1, RIM : RIM + PATCH, :] = moved[:, b * BLK : (b + 1) * BLK]
        return carry

    lax.fori_loop(0, 2, forward_patch, 0)

    def cells_at(c, row_chunk, lane_block):
        total_cells = None
        for p in range(2):
            u, v = corner(p)
            row = jnp.minimum(jnp.maximum(row_chunk * RIM - u + RIM, 0), PATCH + RIM)
            lane = jnp.minimum(jnp.maximum(lane_block - (v >> 7), -1), 3) + 1
            term = placed[p * 2 + c, lane, pl.ds(row, RIM), :]
            total_cells = term if total_cells is None else total_cells + term
        return total_cells

    rim_chunk = 9 * oy
    rim_block = 5 * ox
    for c in range(2):
        for b in range(4):
            rim_row[c, :, b * BLK : (b + 1) * BLK] = cells_at(c, rim_chunk, b + 1).astype(BF)

    def packed_rim(row_chunk):
        real, imag = (cells_at(c, row_chunk, rim_block) for c in range(2))
        kept, moved = jnp.where(sx == 0, real, imag), jnp.where(sx == 0, imag, real)
        return (kept + swap_halves(moved)).astype(BF)

    rim_cor[...] = packed_rim(rim_chunk)

    def rim_columns(r, carry):
        rim_col[pl.ds(pl.multiple_of(r * RIM, RIM), RIM), :] = packed_rim(r + 1)
        return carry

    lax.fori_loop(0, 8, rim_columns, 0)
    outs = [
        pltpu.make_async_copy(src, dst, out_sem.at[i])
        for i, (src, dst) in enumerate(
            [
                (rim_row, row_out), (rim_col, col_out), (rim_cor, cor_out),
                (og, og_out), (part, part_out), (ramp, ramp_out), (bv, bv_out), (sino, sino_out),
            ]
        )
    ]
    for copy in outs[:3]:
        copy.start()
    for copy in picks:
        copy.wait()
    for copy in outs[5:7]:
        copy.start()

    for c in range(2):
        for b in range(5):
            sino[2 * TILE + c * RIM : 2 * TILE + (c + 1) * RIM, b * BLK : (b + 1) * BLK] = cells_at(
                c, rim_chunk, b + ox
            ).astype(BF)

    def interior(r, carry):
        rows = pl.ds(pl.multiple_of(r * RIM, RIM), RIM)
        for c in range(2):
            for b in range(4):
                og[c, rows, b * BLK : (b + 1) * BLK] = cells_at(c, r + 1, b + 1)
            for b in range(5):
                sino[pl.ds(pl.multiple_of(c * TILE + r * RIM, RIM), RIM), b * BLK : (b + 1) * BLK] = cells_at(
                    c, r + 1, b + ox
                ).astype(BF)
        return carry

    lax.fori_loop(0, 8, interior, 0)
    outs[7].start()
    outs[3].start()

    for m in range(2):
        real, imag = (
            patch[0, 0] * chi[0, m, :, a] + sign * patch[0, 1] * chi[0, m, :, b]
            + patch[1, 0] * chi[1, m, :, a] + sign * patch[1, 1] * chi[1, m, :, b]
            for a, b, sign in ((slice(0, PATCH), slice(PATCH, 512), 1.0), (slice(PATCH, 512), slice(0, PATCH), -1.0))
        )
        for q, terms in ((2 * m, real), (2 * m + 1, imag)):
            part[0, q] = terms[0:BLK].astype(BF)
            part[1, SECOND[q]] = terms[BLK:].astype(BF)
    outs[4].start()
    for copy in outs:
        copy.wait()


def regroup_kernel(
    angles,
    sino_ref, row_ref, col_ref, cor_ref, part_ref, ramp_ref, bv_ref,
    got_row, got_col, got_cor, total_out, inbox_out,
    sino, part, ramp, bv, part_got, part_sum, quarter_send, quarter_got, total,
    lines, over_send, over_got, msgs, inbox,
    load_sem, rim_send, rim_recv, part_ssem, part_rsem, over_ssem, over_rsem,
    word_sem, a2a_send, a2a_recv, own_sem, out_sem,
):
    ang, sy, sx = lax.axis_index("ang"), lax.axis_index("sy"), lax.axis_index("sx")
    oy, ox = 1 - sy, 1 - sx
    group = 2 * angles
    me = ang * 2 + sx

    barrier = pltpu.get_barrier_semaphore()
    line, place = ang >> 4, ang & 15
    spot = line * 2 + sx
    crosswise = []
    for k in range(1, group // 16):
        d = jnp.bitwise_xor(spot, k)
        crosswise.append(((d >> 1) * 16 + place, sy, d & 1))
    lengthwise = [(line * 16 + ((place + k) & 15), sy, sx) for k in range(1, 16)]
    greeted = [(ang, oy, sx), (ang, oy, ox)] + crosswise + lengthwise
    for dev in greeted:
        pl.semaphore_signal(barrier, inc=1, device_id=dev, device_id_type=MESH)
    across, beside = (ang, oy, ox), (ang, sy, ox)
    kind = jnp.bitwise_xor(sy, sx)
    routes = (
        (across, beside, 2 * sy, 2 * oy, sx, ox),
        (beside, across, 2 * kind, 2 * (1 - kind), sy, oy),
    )
    loads = [
        pltpu.make_async_copy(src, dst, load_sem.at[i])
        for i, (src, dst) in enumerate(
            [(sino_ref, sino), (ramp_ref, ramp), (bv_ref, bv)]
            + [(part_ref.at[h, pl.ds(routes[h][2], 2)], part.at[h]) for h in range(2)]
        )
    ]
    for copy in loads:
        copy.start()
    pl.semaphore_wait(barrier, len(greeted))

    for dev in crosswise:
        pl.semaphore_signal(word_sem, inc=1, device_id=dev, device_id_type=MESH)

    def exchange(step, h, src, dst, dev):
        return pltpu.make_async_remote_copy(
            src_ref=src, dst_ref=dst, send_sem=part_ssem.at[step, h], recv_sem=part_rsem.at[step, h],
            device_id=dev, device_id_type=MESH,
        )

    firsts = [
        exchange(0, h, part_ref.at[h, pl.ds(routes[h][3], 2)], part_got.at[h], routes[h][0])
        for h in range(2)
    ]
    for copy in firsts:
        copy.start()
    for copy in loads:
        copy.wait()

    for s in range(2):
        filtered = jnp.dot(sino[...], ramp[s], preferred_element_type=F32).astype(BF)
        lines[s] = jnp.dot(filtered, bv[s], preferred_element_type=F32)
        for c in range(2):
            over_send[s, c] = lines[s, 2 * TILE + c * RIM : 2 * TILE + (c + 1) * RIM, :].astype(BF)
    over = pltpu.make_async_remote_copy(
        src_ref=over_send, dst_ref=over_got, send_sem=over_ssem, recv_sem=over_rsem,
        device_id=(ang, oy, sx), device_id_type=MESH,
    )
    over.start()
    top = lax.broadcasted_iota(jnp.int32, (64, 8, BLK), 1) < 4
    for s in range(2):
        a = lines[s, 0:TILE, :].reshape(64, 8, BLK)
        b = lines[s, TILE : 2 * TILE, :].reshape(64, 8, BLK)
        lanes = slice(s * BLK, (s + 1) * BLK)
        msgs[:, 0, :, lanes] = jnp.where(top, a, pltpu.roll(b, 4, 1)).astype(BF)
        msgs[:, 1, :, lanes] = jnp.where(top, pltpu.roll(a, 4, 1), b).astype(BF)

    def send_to(d):
        @pl.when(d != me)
        def _():
            pltpu.make_async_remote_copy(
                src_ref=msgs.at[d >> 1, d & 1], dst_ref=inbox.at[me],
                send_sem=a2a_send, recv_sem=a2a_recv,
                device_id=(d >> 1, sy, d & 1), device_id_type=MESH,
            ).start()

    inner = group - 16

    def send_inner(k, carry):
        send_to(16 * sy + lax.rem(me + k, inner))
        return carry

    def send_edge(k, carry):
        send_to(inner * oy + ((me + k) & 15))
        return carry

    pl.semaphore_wait(word_sem, len(crosswise))
    lax.fori_loop(0, inner // 2, send_inner, 0)
    seconds = []
    for h, (_, after, _, _, keep, give) in enumerate(routes):
        firsts[h].wait()
        part_sum[h] = part[h].astype(F32) + part_got[h].astype(F32)
        quarter_send[h] = part_sum[h, give].astype(BF)
        seconds.append(exchange(1, h, quarter_send.at[h], quarter_got.at[h], after))
        seconds[h].start()
    lax.fori_loop(inner // 2, inner, send_inner, 0)
    over.wait()
    edge = pl.ds(pl.multiple_of((TILE - RIM) * oy, RIM), RIM)
    edge_low = pl.ds(pl.multiple_of(TILE + (TILE - RIM) * oy, RIM), RIM)
    pairs = pl.ds(56 * oy, 8)
    for s in range(2):
        a = (lines[s, edge, :] + over_got[s, 0].astype(F32)).reshape(8, 8, BLK)
        b = (lines[s, edge_low, :] + over_got[s, 1].astype(F32)).reshape(8, 8, BLK)
        lanes = slice(s * BLK, (s + 1) * BLK)
        msgs[pairs, 0, :, lanes] = jnp.where(top[0:8], a, pltpu.roll(b, 4, 1)).astype(BF)
        msgs[pairs, 1, :, lanes] = jnp.where(top[0:8], pltpu.roll(a, 4, 1), b).astype(BF)
    lax.fori_loop(0, 16, send_edge, 0)
    own = pltpu.make_async_copy(msgs.at[ang, sx], inbox.at[me], own_sem)
    own.start()

    thirds = []
    for h, (_, after, base, _, keep, _) in enumerate(routes):
        seconds[h].wait()
        at = total.at[h, base + keep]
        total[h, base + keep] = (part_sum[h, keep] + quarter_got[h].astype(F32)).astype(BF)
        thirds.append(exchange(2, h, at, at, after))
        thirds[h].start()
    rims = [
        pltpu.make_async_remote_copy(
            src_ref=src, dst_ref=dst, send_sem=rim_send.at[i], recv_sem=rim_recv.at[i],
            device_id=dev, device_id_type=MESH,
        )
        for i, (src, dst, dev) in enumerate(
            [
                (row_ref, got_row, (ang, oy, sx)),
                (col_ref, got_col, beside),
                (cor_ref, got_cor, across),
            ]
        )
    ]
    for copy in rims:
        copy.start()
    fourths = []
    for h, (before, _, base, _, _, _) in enumerate(routes):
        thirds[h].wait()
        at = total.at[h, pl.ds(base, 2)]
        fourths.append(exchange(3, h, at, at, before))
        fourths[h].start()
    own.wait()
    pltpu.make_async_copy(
        inbox.at[pl.ds(0, group - 1)], inbox.at[pl.ds(0, group - 1)], a2a_recv
    ).wait()
    inbox_copy = pltpu.make_async_copy(inbox, inbox_out, out_sem.at[0])
    inbox_copy.start()
    for copy in fourths:
        copy.wait()
    total_copy = pltpu.make_async_copy(total, total_out, out_sem.at[1])
    total_copy.start()
    pltpu.make_async_copy(
        inbox.at[pl.ds(0, group - 1)], inbox.at[pl.ds(0, group - 1)], a2a_send
    ).wait()
    for copy in rims:
        copy.wait()
    inbox_copy.wait()
    total_copy.wait()


def finish_kernel(
    angles, bi_ref, og_ref, row_ref, col_ref, cor_ref, total_ref, inbox_ref, og_out, pg_out, vol_out,
    og, row, col, cor, total, pg, inbox, vol, seen, in_sem, out_sem,
):
    sy, sx = lax.axis_index("sy"), lax.axis_index("sx")
    oy, ox = 1 - sy, 1 - sx
    loads = [
        pltpu.make_async_copy(src, dst, in_sem.at[i])
        for i, (src, dst) in enumerate(
            [
                (og_ref, og), (row_ref, row), (col_ref, col), (cor_ref, cor),
                (total_ref, total), (inbox_ref, inbox),
            ]
        )
    ]
    for copy in loads:
        copy.start()
    summed, arrived = loads[4:]
    for a in range(angles):
        seen[a] = 0
    summed.wait()
    for q in range(4):
        pg[0, q // 2, q % 2, 0:BLK, :] = total[0, q].astype(F32) * (1.0 / math.sqrt(8.0))
        pg[0, q // 2, q % 2, BLK:, :] = total[1, SECOND[q]].astype(F32) * (1.0 / math.sqrt(8.0))
    pg_copy = pltpu.make_async_copy(pg, pg_out, out_sem.at[0])
    pg_copy.start()
    for copy in loads[0:4]:
        copy.wait()
    row_at = pl.ds(pl.multiple_of((TILE - RIM) * oy, RIM), RIM)
    col_at = pl.ds(pl.multiple_of((TILE - BLK) * ox, BLK), BLK)
    for got, at in ((col, pl.ds(0, TILE)), (cor, row_at)):
        wide = got[...].astype(F32)
        turned = swap_halves(wide)
        low = lax.broadcasted_iota(jnp.int32, wide.shape, 1) < RIM
        added = (
            jnp.where(sx == 1, jnp.where(low, wide, 0.0), jnp.where(low, 0.0, turned)),
            jnp.where(sx == 1, jnp.where(low, turned, 0.0), jnp.where(low, 0.0, wide)),
        )
        for c in range(2):
            og[c, at, col_at] = og[c, at, col_at] + added[c]
    for c in range(2):
        og[c, row_at, :] = og[c, row_at, :] + row[c].astype(F32)
    og_copy = pltpu.make_async_copy(og, og_out.at[0], out_sem.at[2])
    og_copy.start()
    arrived.wait()
    for b in range(8):
        line = jnp.zeros((8, BLK), F32)
        for k in range(16):
            source = bi_ref[b, k] >> 3
            slot = seen[source]
            seen[source] = 1
            lane = pl.multiple_of(slot * BLK, BLK)
            for h in range(2):
                line = line + inbox[source * 2 + h, :, pl.ds(lane, BLK)].astype(F32)
        for c in range(2):
            for r in range(4):
                vol[0, r, c, b * BLK : (b + 1) * BLK] = line[c * 4 + r]
    vol_copy = pltpu.make_async_copy(vol, vol_out, out_sem.at[1])
    vol_copy.start()
    og_copy.wait()
    pg_copy.wait()
    vol_copy.wait()


def body(angles, tables, objects, probe, data, positions, block_index, block_values):
    forward, backward, ramp = (jnp.asarray(t) for t in tables)
    group = 2 * angles
    dma = pltpu.SemaphoreType.DMA
    smem = pl.BlockSpec(memory_space=pltpu.SMEM)
    hbm = pl.BlockSpec(memory_space=pltpu.HBM)

    def shape(dims, kind):
        return jax.ShapeDtypeStruct(dims, kind)

    rim_shapes = (shape((2, RIM, TILE), BF), shape((TILE, BLK), BF), shape((RIM, BLK), BF))
    halos = pl.pallas_call(
        strips_kernel,
        out_shape=rim_shapes,
        in_specs=[hbm],
        out_specs=[hbm] * 3,
        scratch_shapes=[
            pltpu.VMEM((2, TILE, BLK), BF), pltpu.VMEM((TILE, BLK), BF), dma, dma((3,)), dma((3,)),
        ],
        compiler_params=pltpu.CompilerParams(
            collective_id=0, has_side_effects=True, vmem_limit_bytes=62 * 1024 * 1024
        ),
    )(objects)
    og_part, row, col, cor, parts, ramp_two, bv_two, sino = pl.pallas_call(
        functools.partial(patch_kernel, angles),
        out_shape=(shape((2, TILE, TILE), F32),) + rim_shapes + (
            shape((2, 4, BLK, PATCH), BF), shape((2, SPAN, BLK), BF), shape((2, BLK, BLK), BF),
            shape((2 * ROWS - 2 * RIM, SPAN), BF),
        ),
        in_specs=[smem] * 2 + [hbm] * 10,
        out_specs=[hbm] * 8,
        scratch_shapes=[
            pltpu.VMEM((2, ROWS, COLS), BF),
            pltpu.VMEM((ROWS, BLK), BF),
            pltpu.VMEM((2, 2, PATCH, PATCH), F32),
            pltpu.VMEM((2, PATCH, PATCH), BF),
            pltpu.VMEM((512, 512), BF),
            pltpu.VMEM((512, 512), BF),
            pltpu.VMEM((2, SPAN, BLK), BF),
            pltpu.VMEM((2, BLK, BLK), BF),
            pltpu.VMEM((2, 2, 272, BLK), F32),
            pltpu.VMEM((2, 2, PATCH, PATCH), F32),
            pltpu.VMEM((2, 512, PATCH), BF),
            pltpu.VMEM((2, PATCH, 512), BF),
            pltpu.VMEM((2, PATCH, 512), F32),
            pltpu.VMEM((2, 2, PATCH, 512), F32),
            pltpu.VMEM((4, 5, 384, BLK), F32),
            pltpu.VMEM((2, TILE, TILE), F32),
            pltpu.VMEM((2, RIM, TILE), BF),
            pltpu.VMEM((TILE, BLK), BF),
            pltpu.VMEM((RIM, BLK), BF),
            pltpu.VMEM((2, 4, BLK, PATCH), BF),
            pltpu.VMEM((2 * ROWS - 2 * RIM, SPAN), BF),
            dma((8,)), dma((4,)), dma((8,)),
        ],
        compiler_params=pltpu.CompilerParams(vmem_limit_bytes=62 * 1024 * 1024),
    )(positions, block_index, objects, *halos, probe, data, forward, backward, ramp, block_values)
    got_row, got_col, got_cor, total, inbox = pl.pallas_call(
        functools.partial(regroup_kernel, angles),
        out_shape=rim_shapes + (shape((2, 4, BLK, PATCH), BF), shape((group, 8, 2 * BLK), BF)),
        in_specs=[hbm] * 7,
        out_specs=[hbm] * 5,
        scratch_shapes=[
            pltpu.VMEM((2 * ROWS - 2 * RIM, SPAN), BF),
            pltpu.VMEM((2, 2, BLK, PATCH), BF),
            pltpu.VMEM((2, SPAN, BLK), BF),
            pltpu.VMEM((2, BLK, BLK), BF),
            pltpu.VMEM((2, 2, BLK, PATCH), BF),
            pltpu.VMEM((2, 2, BLK, PATCH), F32),
            pltpu.VMEM((2, BLK, PATCH), BF),
            pltpu.VMEM((2, BLK, PATCH), BF),
            pltpu.VMEM((2, 4, BLK, PATCH), BF),
            pltpu.VMEM((2, 2 * ROWS - 2 * RIM, BLK), F32),
            pltpu.VMEM((2, 2, RIM, BLK), BF),
            pltpu.VMEM((2, 2, RIM, BLK), BF),
            pltpu.VMEM((group // 2, 2, 8, 2 * BLK), BF),
            pltpu.VMEM((group, 8, 2 * BLK), BF),
            dma((5,)), dma((3,)), dma((3,)), dma((4, 2)), dma((4, 2)), dma, dma,
            pltpu.SemaphoreType.REGULAR, dma, dma, dma, dma((2,)),
        ],
        compiler_params=pltpu.CompilerParams(
            collective_id=1, has_side_effects=True, vmem_limit_bytes=62 * 1024 * 1024
        ),
    )(sino, row, col, cor, parts, ramp_two, bv_two)
    return pl.pallas_call(
        functools.partial(finish_kernel, angles),
        out_shape=(
            shape((1, 2, TILE, TILE), F32), shape((1, 2, 2, PATCH, PATCH), F32), shape((1, 4, 2, 1024), F32),
        ),
        in_specs=[smem] + [hbm] * 6,
        out_specs=[hbm] * 3,
        scratch_shapes=[
            pltpu.VMEM((2, TILE, TILE), F32),
            pltpu.VMEM((2, RIM, TILE), BF),
            pltpu.VMEM((TILE, BLK), BF),
            pltpu.VMEM((RIM, BLK), BF),
            pltpu.VMEM((2, 4, BLK, PATCH), BF),
            pltpu.VMEM((1, 2, 2, PATCH, PATCH), F32),
            pltpu.VMEM((group, 8, 2 * BLK), BF),
            pltpu.VMEM((1, 4, 2, 1024), F32),
            pltpu.SMEM((angles,), jnp.int32),
            dma((6,)), dma((3,)),
        ],
        compiler_params=pltpu.CompilerParams(vmem_limit_bytes=62 * 1024 * 1024),
    )(block_index, og_part, got_row, got_col, got_cor, total, inbox)


def solution(mesh):
    tables = dft_tables() + (ramp_blocks(8),)
    return jax.shard_map(
        functools.partial(body, mesh.shape["ang"], tables),
        mesh=mesh,
        in_specs=(
            P("ang", None, "sy", "sx"),
            P(),
            P("ang", "sy", "sx", None, None, None),
            P("ang", "sy", "sx", None, None),
            P(),
            P(),
        ),
        out_specs=(
            P("ang", None, "sy", "sx"),
            P("ang", None, None, None, None),
            P("sy", ("ang", "sx"), None, None),
        ),
        check_vma=False,
    )
```

```python
import functools
import math

import jax
import jax.numpy as jnp
import numpy as np
from jax import lax
from jax.experimental import pallas as pl
from jax.experimental.pallas import tpu as pltpu
from jax.sharding import PartitionSpec as P

PATCH = 256
RIM = 64
BLK = 128
TILE = 512
ROWS = 640
SPAN = 640
COLS = 768
SECOND = (0, 2, 3, 1)
MESH = pl.DeviceIdType.MESH
BF = jnp.bfloat16
F32 = jnp.float32


def dft_tables():
    ids = np.arange(PATCH)
    phases = (np.outer(ids, ids) % PATCH).astype(np.float64) * (2.0 * math.pi / PATCH)
    factor = 1.0 / math.sqrt(PATCH)
    real = (np.cos(phases) * factor).astype(np.float32)
    imag = (-np.sin(phases) * factor).astype(np.float32)
    forward = np.block([[real, -imag], [imag, real]])
    backward = np.block([[real, imag], [-imag, real]])
    return forward.astype(BF), backward.astype(BF)


def ramp_blocks(line_blocks):
    x = np.arange((2 * line_blocks - 1) * BLK)
    n = np.arange(BLK)[None, :] - (x - (line_blocks - 1) * BLK)[:, None]
    odd = n % 2 != 0
    scaled = n.astype(np.float32) * np.float32(math.pi)
    values = np.where(odd, -1.0 / np.maximum(scaled * scaled, 1.0), 0.0)
    values = np.where(n == 0, 0.25, values).astype(np.float32)
    return values.astype(BF)


def swap_halves(cells):
    return pltpu.roll(cells, BLK // 2, cells.ndim - 1)


def strips_kernel(
    angles, bi_ref, obj_ref, named_out, row_out, col_out, cor_out, block, packed, load_sem, send_sem, recv_sem,
):
    ang, sy, sx = lax.axis_index("ang"), lax.axis_index("sy"), lax.axis_index("sx")
    oy, ox = 1 - sy, 1 - sx
    devices = [(ang, oy, sx), (ang, sy, ox), (ang, oy, ox)]
    rows = pl.ds(pl.multiple_of((TILE - RIM) * oy, RIM), RIM)
    cols = pl.ds(pl.multiple_of((TILE - BLK) * ox, BLK), BLK)
    load = pltpu.make_async_copy(obj_ref.at[0, :, :, cols], block, load_sem)
    load.start()
    barrier = pltpu.get_barrier_semaphore()
    for dev in devices:
        pl.semaphore_signal(barrier, inc=1, device_id=dev, device_id_type=MESH)
    load.wait()
    real, imag = block[0].astype(F32), block[1].astype(F32)
    low = lax.broadcasted_iota(jnp.int32, (TILE, BLK), 1) < RIM
    packed[...] = jnp.where(
        low, jnp.where(sx == 0, swap_halves(real), real), jnp.where(sx == 0, imag, swap_halves(imag))
    ).astype(BF)
    pl.semaphore_wait(barrier, 3)
    sources = [obj_ref.at[0, :, rows, :], packed, packed.at[rows]]
    copies = [
        pltpu.make_async_remote_copy(
            src_ref=src, dst_ref=dst, send_sem=send_sem.at[i], recv_sem=recv_sem.at[i],
            device_id=dev, device_id_type=MESH,
        )
        for i, (src, dst, dev) in enumerate(zip(sources, (row_out, col_out, cor_out), devices))
    ]
    for copy in copies:
        copy.start()
    named = [(jnp.int32(-1), jnp.int32(0)), (jnp.int32(0), jnp.int32(0))]
    for j in range(2 * angles):
        entry = bi_ref[j // 16, j % 16]
        mine = (entry >> 3) == ang
        early = jnp.logical_and(mine, named[0][0] < 0)
        named = [
            (jnp.where(take, j, at), jnp.where(take, entry & 7, column))
            for take, (at, column) in zip((early, mine), named)
        ]
    named[0] = (jnp.maximum(named[0][0], 0), named[0][1])
    for s, (entry, column) in enumerate(named):
        named_out[2 * s] = entry
        named_out[2 * s + 1] = column
    for copy in copies:
        copy.wait()


def patch_kernel(
    angles,
    pos_ref, named_ref,
    obj_ref, halo_row, halo_col, halo_cor, probe_ref, data_ref, fwd_ref, bwd_ref, ramp_ref, bv_ref,
    og_out, row_out, col_out, cor_out, part_out, ramp_out, bv_out, sino_out,
    big, side, probe, data, fwd, bwd, ramp, bv,
    win, patch, exits, half, far, chi, placed, og,
    rim_row, rim_col, rim_cor, part, sino,
    load_sem, pick_sem, out_sem, piece_sem,
):
    ang, sy, sx = lax.axis_index("ang"), lax.axis_index("sy"), lax.axis_index("sx")
    oy, ox = 1 - sy, 1 - sx
    dst_row = pl.ds(pl.multiple_of((ROWS - RIM) * oy, RIM), RIM)
    dst_col = pl.ds(pl.multiple_of((COLS - BLK) * ox, BLK), BLK)
    loads = [
        pltpu.make_async_copy(src, dst, load_sem.at[i])
        for i, (src, dst) in enumerate(
            [
                (obj_ref.at[0], big.at[:, pl.ds(RIM, TILE), pl.ds(BLK, TILE)]),
                (halo_row, big.at[:, dst_row, pl.ds(BLK, TILE)]),
                (halo_col, side.at[pl.ds(RIM, TILE)]),
                (halo_cor, side.at[dst_row]),
                (probe_ref, probe),
                (fwd_ref, fwd),
                (bwd_ref, bwd),
                (data_ref.at[0, 0, 0], data),
            ]
        )
    ]
    for copy in loads:
        copy.start()

    big[:, pl.ds(pl.multiple_of((ROWS - RIM) * sy, RIM), RIM), :] = jnp.zeros((2, RIM, COLS), BF)
    big[:, :, pl.ds(pl.multiple_of((COLS - BLK) * sx, BLK), BLK)] = jnp.zeros((2, ROWS, BLK), BF)
    for q in range(4):
        placed[q, :, 0:RIM, :] = jnp.zeros((5, RIM, BLK), F32)
        placed[q, :, RIM + PATCH :, :] = jnp.zeros((5, RIM, BLK), F32)
        placed[q, 0, RIM : RIM + PATCH, :] = jnp.zeros((PATCH, BLK), F32)
        placed[q, 4, RIM : RIM + PATCH, :] = jnp.zeros((PATCH, BLK), F32)

    named = [(named_ref[0], named_ref[1]), (named_ref[2], named_ref[3])]
    picks = []
    for s, (entry, column) in enumerate(named):
        at = pl.multiple_of((7 - column + 3 * sx) * BLK, BLK)
        picks.append(
            pltpu.make_async_copy(ramp_ref.at[pl.ds(at, SPAN), :], ramp.at[s], pick_sem.at[2 * s])
        )
        picks.append(
            pltpu.make_async_copy(bv_ref.at[entry >> 4, entry & 15], bv.at[s], pick_sem.at[2 * s + 1])
        )
    for copy in picks:
        copy.start()
    side[pl.ds(pl.multiple_of((ROWS - RIM) * sy, RIM), RIM), :] = jnp.zeros((RIM, BLK), BF)
    for copy in loads[0:4]:
        copy.wait()
    wide = side[...].astype(F32)
    turned = swap_halves(wide)
    big[0, :, dst_col] = jnp.where(sx == 1, turned, wide).astype(BF)
    big[1, :, dst_col] = jnp.where(sx == 1, wide, turned).astype(BF)

    def corner(p):
        return pos_ref[0, 0, 0, p, 0], pos_ref[0, 0, 0, p, 1] + RIM

    def forward_patch(p, carry):
        u, v = corner(p)
        base = jnp.minimum(u >> 4, 23) * 16
        lead = u - base
        block, shift = v >> 7, v & (BLK - 1)
        across = lax.broadcasted_iota(jnp.int32, (384, PATCH), 0)
        pick = jnp.where(
            across == lax.broadcasted_iota(jnp.int32, (384, PATCH), 1) + shift, 1.0, 0.0
        ).astype(BF)
        for c in range(2):
            cells = big[
                c, pl.ds(pl.multiple_of(base, 16), 272), pl.ds(pl.multiple_of(block * BLK, BLK), 384)
            ]
            cells = jnp.dot(cells, pick, preferred_element_type=F32)
            for b in range(2):
                win[c, b] = cells[:, b * BLK : (b + 1) * BLK]
        for c in range(2):
            for b in range(2):
                patch[p, c, :, b * BLK : (b + 1) * BLK] = win[c, b, pl.ds(lead, PATCH), :]
        @pl.when(p == 0)
        def _():
            loads[4].wait()

        for m in range(2):
            exits[m, 0:PATCH] = (probe[m, 0] * patch[p, 0] - probe[m, 1] * patch[p, 1]).astype(BF)
            exits[m, PATCH:] = (probe[m, 0] * patch[p, 1] + probe[m, 1] * patch[p, 0]).astype(BF)
        @pl.when(p == 0)
        def _():
            loads[5].wait()

        for m in range(2):
            done = jnp.dot(fwd[...], exits[m], preferred_element_type=F32)
            half[m, :, 0:PATCH] = done[0:PATCH].astype(BF)
            half[m, :, PATCH:] = done[PATCH:].astype(BF)
        @pl.when(p == 0)
        def _():
            loads[6].wait()

        @pl.when(p == 0)
        def _():
            loads[7].wait()

        for m in range(2):
            far[m] = jnp.dot(half[m], bwd[...], preferred_element_type=F32)
        misfit = (
            far[0, :, 0:PATCH] * far[0, :, 0:PATCH]
            + far[0, :, PATCH:] * far[0, :, PATCH:]
            + far[1, :, 0:PATCH] * far[1, :, 0:PATCH]
            + far[1, :, PATCH:] * far[1, :, PATCH:]
            - data[p].astype(F32)
        )
        for m in range(2):
            exits[m, 0:PATCH] = (misfit * far[m, :, 0:PATCH]).astype(BF)
            exits[m, PATCH:] = (misfit * far[m, :, PATCH:]).astype(BF)
        for m in range(2):
            done = jnp.dot(bwd[...], exits[m], preferred_element_type=F32)
            half[m, :, 0:PATCH] = done[0:PATCH].astype(BF)
            half[m, :, PATCH:] = done[PATCH:].astype(BF)
        for m in range(2):
            chi[p, m] = jnp.dot(half[m], fwd[...], preferred_element_type=F32)
        cr = [chi[p, m, :, 0:PATCH] for m in range(2)]
        ci = [chi[p, m, :, PATCH:] for m in range(2)]
        grad = [
            probe[0, 0] * cr[0] + probe[0, 1] * ci[0] + probe[1, 0] * cr[1] + probe[1, 1] * ci[1],
            probe[0, 0] * ci[0] - probe[0, 1] * cr[0] + probe[1, 0] * ci[1] - probe[1, 1] * cr[1],
        ]
        spots = lax.broadcasted_iota(jnp.int32, (PATCH, 384), 1)
        put = jnp.where(
            spots == lax.broadcasted_iota(jnp.int32, (PATCH, 384), 0) + shift, 1.0, 0.0
        ).astype(BF)
        for c in range(2):
            high = grad[c].astype(BF)
            low = (grad[c] - high.astype(F32)).astype(BF)
            moved = jnp.dot(high, put, preferred_element_type=F32) + jnp.dot(
                low, put, preferred_element_type=F32
            )
            for b in range(3):
                placed[p * 2 + c, b + 1, RIM : RIM + PATCH, :] = moved[:, b * BLK : (b + 1) * BLK]
        return carry

    lax.fori_loop(0, 2, forward_patch, 0)

    def cells_at(c, row_chunk, lane_block):
        total_cells = None
        for p in range(2):
            u, v = corner(p)
            row = jnp.minimum(jnp.maximum(row_chunk * RIM - u + RIM, 0), PATCH + RIM)
            lane = jnp.minimum(jnp.maximum(lane_block - (v >> 7), -1), 3) + 1
            term = placed[p * 2 + c, lane, pl.ds(row, RIM), :]
            total_cells = term if total_cells is None else total_cells + term
        return total_cells

    rim_chunk = 9 * oy
    rim_block = 5 * ox
    for c in range(2):
        for b in range(4):
            rim_row[c, :, b * BLK : (b + 1) * BLK] = cells_at(c, rim_chunk, b + 1).astype(BF)

    def packed_rim(row_chunk):
        real, imag = (cells_at(c, row_chunk, rim_block) for c in range(2))
        kept, moved = jnp.where(sx == 0, real, imag), jnp.where(sx == 0, imag, real)
        return (kept + swap_halves(moved)).astype(BF)

    rim_cor[...] = packed_rim(rim_chunk)

    def rim_columns(r, carry):
        rim_col[pl.ds(pl.multiple_of(r * RIM, RIM), RIM), :] = packed_rim(r + 1)
        return carry

    lax.fori_loop(0, 8, rim_columns, 0)
    outs = [
        pltpu.make_async_copy(src, dst, out_sem.at[i])
        for i, (src, dst) in enumerate(
            [
                (rim_row, row_out), (rim_col, col_out), (rim_cor, cor_out),
                (part, part_out), (ramp, ramp_out), (bv, bv_out),
            ]
        )
    ]
    for copy in outs[:3]:
        copy.start()
    for copy in picks:
        copy.wait()
    for copy in outs[4:6]:
        copy.start()

    for c in range(2):
        for b in range(5):
            sino[2 * TILE + c * RIM : 2 * TILE + (c + 1) * RIM, b * BLK : (b + 1) * BLK] = cells_at(
                c, rim_chunk, b + ox
            ).astype(BF)

    over_rows = pl.ds(2 * TILE, 2 * RIM)
    over_copy = pltpu.make_async_copy(sino.at[over_rows], sino_out.at[over_rows], out_sem.at[6])
    over_copy.start()

    def finished(r):
        rows = pl.ds(pl.multiple_of(r * RIM, RIM), RIM)
        spans = [pl.ds(pl.multiple_of(c * TILE + r * RIM, RIM), RIM) for c in range(2)]
        return [pltpu.make_async_copy(og.at[:, rows], og_out.at[0, :, rows], piece_sem.at[r, 2])] + [
            pltpu.make_async_copy(sino.at[spans[c]], sino_out.at[spans[c]], piece_sem.at[r, c])
            for c in range(2)
        ]

    def interior(r, carry):
        rows = pl.ds(pl.multiple_of(r * RIM, RIM), RIM)
        for c in range(2):
            for b in range(4):
                og[c, rows, b * BLK : (b + 1) * BLK] = cells_at(c, r + 1, b + 1)
            for b in range(5):
                sino[pl.ds(pl.multiple_of(c * TILE + r * RIM, RIM), RIM), b * BLK : (b + 1) * BLK] = cells_at(
                    c, r + 1, b + ox
                ).astype(BF)
        for copy in finished(r):
            copy.start()
        return carry

    lax.fori_loop(0, 8, interior, 0)

    for m in range(2):
        real, imag = (
            patch[0, 0] * chi[0, m, :, a] + sign * patch[0, 1] * chi[0, m, :, b]
            + patch[1, 0] * chi[1, m, :, a] + sign * patch[1, 1] * chi[1, m, :, b]
            for a, b, sign in ((slice(0, PATCH), slice(PATCH, 512), 1.0), (slice(PATCH, 512), slice(0, PATCH), -1.0))
        )
        for q, terms in ((2 * m, real), (2 * m + 1, imag)):
            part[0, q] = terms[0:BLK].astype(BF)
            part[1, SECOND[q]] = terms[BLK:].astype(BF)
    outs[3].start()

    def settle(r, carry):
        for copy in finished(r):
            copy.wait()
        return carry

    lax.fori_loop(0, 8, settle, 0)
    for copy in outs:
        copy.wait()
    over_copy.wait()


def regroup_kernel(
    angles,
    sino_ref, row_ref, col_ref, cor_ref, part_ref, ramp_ref, bv_ref,
    got_row, got_col, got_cor, total_out, inbox_out,
    sino, part, ramp, bv, part_got, part_sum, quarter_send, quarter_got, total,
    lines, over_send, over_got, msgs, inbox,
    load_sem, rim_send, rim_recv, part_ssem, part_rsem, over_ssem, over_rsem,
    word_sem, a2a_send, a2a_recv, own_sem, out_sem,
):
    ang, sy, sx = lax.axis_index("ang"), lax.axis_index("sy"), lax.axis_index("sx")
    oy, ox = 1 - sy, 1 - sx
    group = 2 * angles
    me = ang * 2 + sx

    barrier = pltpu.get_barrier_semaphore()
    line, place = ang >> 4, ang & 15
    spot = line * 2 + sx
    crosswise = []
    for k in range(1, group // 16):
        d = jnp.bitwise_xor(spot, k)
        crosswise.append(((d >> 1) * 16 + place, sy, d & 1))
    lengthwise = [(line * 16 + ((place + k) & 15), sy, sx) for k in range(1, 16)]
    greeted = [(ang, oy, sx), (ang, oy, ox)] + crosswise + lengthwise
    for dev in greeted:
        pl.semaphore_signal(barrier, inc=1, device_id=dev, device_id_type=MESH)
    across, beside = (ang, oy, ox), (ang, sy, ox)
    kind = jnp.bitwise_xor(sy, sx)
    routes = (
        (across, beside, 2 * sy, 2 * oy, sx, ox),
        (beside, across, 2 * kind, 2 * (1 - kind), sy, oy),
    )
    loads = [
        pltpu.make_async_copy(src, dst, load_sem.at[i])
        for i, (src, dst) in enumerate(
            [(sino_ref, sino), (ramp_ref, ramp), (bv_ref, bv)]
            + [(part_ref.at[h, pl.ds(routes[h][2], 2)], part.at[h]) for h in range(2)]
        )
    ]
    for copy in loads:
        copy.start()
    pl.semaphore_wait(barrier, len(greeted))

    for dev in crosswise:
        pl.semaphore_signal(word_sem, inc=1, device_id=dev, device_id_type=MESH)

    def exchange(step, h, src, dst, dev):
        return pltpu.make_async_remote_copy(
            src_ref=src, dst_ref=dst, send_sem=part_ssem.at[step, h], recv_sem=part_rsem.at[step, h],
            device_id=dev, device_id_type=MESH,
        )

    firsts = [
        exchange(0, h, part_ref.at[h, pl.ds(routes[h][3], 2)], part_got.at[h], routes[h][0])
        for h in range(2)
    ]
    for copy in firsts:
        copy.start()
    for copy in loads:
        copy.wait()

    for s in range(2):
        filtered = jnp.dot(sino[...], ramp[s], preferred_element_type=F32).astype(BF)
        lines[s] = jnp.dot(filtered, bv[s], preferred_element_type=F32)
        for c in range(2):
            over_send[s, c] = lines[s, 2 * TILE + c * RIM : 2 * TILE + (c + 1) * RIM, :].astype(BF)
    over = pltpu.make_async_remote_copy(
        src_ref=over_send, dst_ref=over_got, send_sem=over_ssem, recv_sem=over_rsem,
        device_id=(ang, oy, sx), device_id_type=MESH,
    )
    over.start()
    top = lax.broadcasted_iota(jnp.int32, (64, 8, BLK), 1) < 4
    for s in range(2):
        a = lines[s, 0:TILE, :].reshape(64, 8, BLK)
        b = lines[s, TILE : 2 * TILE, :].reshape(64, 8, BLK)
        lanes = slice(s * BLK, (s + 1) * BLK)
        msgs[:, 0, :, lanes] = jnp.where(top, a, pltpu.roll(b, 4, 1)).astype(BF)
        msgs[:, 1, :, lanes] = jnp.where(top, pltpu.roll(a, 4, 1), b).astype(BF)

    def send_to(d):
        @pl.when(d != me)
        def _():
            pltpu.make_async_remote_copy(
                src_ref=msgs.at[d >> 1, d & 1], dst_ref=inbox.at[me],
                send_sem=a2a_send, recv_sem=a2a_recv,
                device_id=(d >> 1, sy, d & 1), device_id_type=MESH,
            ).start()

    inner = group - 16

    def send_inner(k, carry):
        send_to(16 * sy + lax.rem(me + k, inner))
        return carry

    def send_edge(k, carry):
        send_to(inner * oy + ((me + k) & 15))
        return carry

    pl.semaphore_wait(word_sem, len(crosswise))
    lax.fori_loop(0, inner // 2, send_inner, 0)
    seconds = []
    for h, (_, after, _, _, keep, give) in enumerate(routes):
        firsts[h].wait()
        part_sum[h] = part[h].astype(F32) + part_got[h].astype(F32)
        quarter_send[h] = part_sum[h, give].astype(BF)
        seconds.append(exchange(1, h, quarter_send.at[h], quarter_got.at[h], after))
        seconds[h].start()
    lax.fori_loop(inner // 2, inner, send_inner, 0)
    over.wait()
    edge = pl.ds(pl.multiple_of((TILE - RIM) * oy, RIM), RIM)
    edge_low = pl.ds(pl.multiple_of(TILE + (TILE - RIM) * oy, RIM), RIM)
    pairs = pl.ds(56 * oy, 8)
    for s in range(2):
        a = (lines[s, edge, :] + over_got[s, 0].astype(F32)).reshape(8, 8, BLK)
        b = (lines[s, edge_low, :] + over_got[s, 1].astype(F32)).reshape(8, 8, BLK)
        lanes = slice(s * BLK, (s + 1) * BLK)
        msgs[pairs, 0, :, lanes] = jnp.where(top[0:8], a, pltpu.roll(b, 4, 1)).astype(BF)
        msgs[pairs, 1, :, lanes] = jnp.where(top[0:8], pltpu.roll(a, 4, 1), b).astype(BF)
    lax.fori_loop(0, 16, send_edge, 0)
    own = pltpu.make_async_copy(msgs.at[ang, sx], inbox.at[me], own_sem)
    own.start()

    thirds = []
    for h, (_, after, base, _, keep, _) in enumerate(routes):
        seconds[h].wait()
        at = total.at[h, base + keep]
        total[h, base + keep] = (part_sum[h, keep] + quarter_got[h].astype(F32)).astype(BF)
        thirds.append(exchange(2, h, at, at, after))
        thirds[h].start()
    rims = [
        pltpu.make_async_remote_copy(
            src_ref=src, dst_ref=dst, send_sem=rim_send.at[i], recv_sem=rim_recv.at[i],
            device_id=dev, device_id_type=MESH,
        )
        for i, (src, dst, dev) in enumerate(
            [
                (row_ref, got_row, (ang, oy, sx)),
                (col_ref, got_col, beside),
                (cor_ref, got_cor, across),
            ]
        )
    ]
    for copy in rims:
        copy.start()
    fourths = []
    for h, (before, _, base, _, _, _) in enumerate(routes):
        thirds[h].wait()
        at = total.at[h, pl.ds(base, 2)]
        fourths.append(exchange(3, h, at, at, before))
        fourths[h].start()
    own.wait()
    pltpu.make_async_copy(
        inbox.at[pl.ds(0, group - 1)], inbox.at[pl.ds(0, group - 1)], a2a_recv
    ).wait()
    inbox_copy = pltpu.make_async_copy(inbox, inbox_out, out_sem.at[0])
    inbox_copy.start()
    for copy in fourths:
        copy.wait()
    total_copy = pltpu.make_async_copy(total, total_out, out_sem.at[1])
    total_copy.start()
    pltpu.make_async_copy(
        inbox.at[pl.ds(0, group - 1)], inbox.at[pl.ds(0, group - 1)], a2a_send
    ).wait()
    for copy in rims:
        copy.wait()
    inbox_copy.wait()
    total_copy.wait()


def finish_kernel(
    angles, bi_ref, og_ref, row_ref, col_ref, cor_ref, total_ref, inbox_ref, og_out, pg_out, vol_out,
    og_row, og_col, row, col, cor, total, pg, inbox, vol, seen, in_sem, out_sem,
):
    sy, sx = lax.axis_index("sy"), lax.axis_index("sx")
    oy, ox = 1 - sy, 1 - sx
    row_at = pl.ds(pl.multiple_of((TILE - RIM) * oy, RIM), RIM)
    col_at = pl.ds(pl.multiple_of((TILE - BLK) * ox, BLK), BLK)
    rest_at = pl.ds(pl.multiple_of(BLK * sx, BLK), TILE - BLK)
    loads = [
        pltpu.make_async_copy(src, dst, in_sem.at[i])
        for i, (src, dst) in enumerate(
            [
                (og_ref.at[0, :, row_at, rest_at], og_row), (og_ref.at[0, :, :, col_at], og_col),
                (row_ref, row), (col_ref, col), (cor_ref, cor), (total_ref, total), (inbox_ref, inbox),
            ]
        )
    ]
    for copy in loads:
        copy.start()
    summed, arrived = loads[5:]
    for a in range(angles):
        seen[a] = 0
    summed.wait()
    for q in range(4):
        pg[0, q // 2, q % 2, 0:BLK, :] = total[0, q].astype(F32) * (1.0 / math.sqrt(8.0))
        pg[0, q // 2, q % 2, BLK:, :] = total[1, SECOND[q]].astype(F32) * (1.0 / math.sqrt(8.0))
    pg_copy = pltpu.make_async_copy(pg, pg_out, out_sem.at[0])
    pg_copy.start()
    for copy in loads[0:5]:
        copy.wait()
    for got, at in ((col, pl.ds(0, TILE)), (cor, row_at)):
        wide = got[...].astype(F32)
        turned = swap_halves(wide)
        low = lax.broadcasted_iota(jnp.int32, wide.shape, 1) < RIM
        added = (
            jnp.where(sx == 1, jnp.where(low, wide, 0.0), jnp.where(low, 0.0, turned)),
            jnp.where(sx == 1, jnp.where(low, turned, 0.0), jnp.where(low, 0.0, wide)),
        )
        for c in range(2):
            og_col[c, at, :] = og_col[c, at, :] + added[c]
    for c in range(2):
        og_row[c] = og_row[c] + row[c, :, rest_at].astype(F32)
        og_col[c, row_at, :] = og_col[c, row_at, :] + row[c, :, col_at].astype(F32)
    og_copies = [
        pltpu.make_async_copy(og_row, og_out.at[0, :, row_at, rest_at], out_sem.at[2]),
        pltpu.make_async_copy(og_col, og_out.at[0, :, :, col_at], out_sem.at[3]),
    ]
    for copy in og_copies:
        copy.start()
    arrived.wait()
    for b in range(8):
        line = jnp.zeros((8, BLK), F32)
        for k in range(16):
            source = bi_ref[b, k] >> 3
            slot = seen[source]
            seen[source] = 1
            lane = pl.multiple_of(slot * BLK, BLK)
            for h in range(2):
                line = line + inbox[source * 2 + h, :, pl.ds(lane, BLK)].astype(F32)
        for c in range(2):
            for r in range(4):
                vol[0, r, c, b * BLK : (b + 1) * BLK] = line[c * 4 + r]
    vol_copy = pltpu.make_async_copy(vol, vol_out, out_sem.at[1])
    vol_copy.start()
    for copy in og_copies:
        copy.wait()
    pg_copy.wait()
    vol_copy.wait()


def body(angles, tables, objects, probe, data, positions, block_index, block_values):
    forward, backward, ramp = (jnp.asarray(t) for t in tables)
    group = 2 * angles
    dma = pltpu.SemaphoreType.DMA
    smem = pl.BlockSpec(memory_space=pltpu.SMEM)
    hbm = pl.BlockSpec(memory_space=pltpu.HBM)

    def shape(dims, kind):
        return jax.ShapeDtypeStruct(dims, kind)

    rim_shapes = (shape((2, RIM, TILE), BF), shape((TILE, BLK), BF), shape((RIM, BLK), BF))
    named, *halos = pl.pallas_call(
        functools.partial(strips_kernel, angles),
        out_shape=(shape((4,), jnp.int32),) + rim_shapes,
        in_specs=[smem, hbm],
        out_specs=[smem] + [hbm] * 3,
        scratch_shapes=[
            pltpu.VMEM((2, TILE, BLK), BF), pltpu.VMEM((TILE, BLK), BF), dma, dma((3,)), dma((3,)),
        ],
        compiler_params=pltpu.CompilerParams(
            collective_id=0, has_side_effects=True, vmem_limit_bytes=62 * 1024 * 1024
        ),
    )(block_index, objects)
    og_part, row, col, cor, parts, ramp_two, bv_two, sino = pl.pallas_call(
        functools.partial(patch_kernel, angles),
        out_shape=(shape((1, 2, TILE, TILE), F32),) + rim_shapes + (
            shape((2, 4, BLK, PATCH), BF), shape((2, SPAN, BLK), BF), shape((2, BLK, BLK), BF),
            shape((2 * ROWS - 2 * RIM, SPAN), BF),
        ),
        in_specs=[smem] * 2 + [hbm] * 10,
        out_specs=[hbm] * 8,
        scratch_shapes=[
            pltpu.VMEM((2, ROWS, COLS), BF),
            pltpu.VMEM((ROWS, BLK), BF),
            pltpu.VMEM((2, 2, PATCH, PATCH), F32),
            pltpu.VMEM((2, PATCH, PATCH), BF),
            pltpu.VMEM((512, 512), BF),
            pltpu.VMEM((512, 512), BF),
            pltpu.VMEM((2, SPAN, BLK), BF),
            pltpu.VMEM((2, BLK, BLK), BF),
            pltpu.VMEM((2, 2, 272, BLK), F32),
            pltpu.VMEM((2, 2, PATCH, PATCH), F32),
            pltpu.VMEM((2, 512, PATCH), BF),
            pltpu.VMEM((2, PATCH, 512), BF),
            pltpu.VMEM((2, PATCH, 512), F32),
            pltpu.VMEM((2, 2, PATCH, 512), F32),
            pltpu.VMEM((4, 5, 384, BLK), F32),
            pltpu.VMEM((2, TILE, TILE), F32),
            pltpu.VMEM((2, RIM, TILE), BF),
            pltpu.VMEM((TILE, BLK), BF),
            pltpu.VMEM((RIM, BLK), BF),
            pltpu.VMEM((2, 4, BLK, PATCH), BF),
            pltpu.VMEM((2 * ROWS - 2 * RIM, SPAN), BF),
            dma((8,)), dma((4,)), dma((7,)), dma((8, 3)),
        ],
        compiler_params=pltpu.CompilerParams(vmem_limit_bytes=62 * 1024 * 1024),
    )(positions, named, objects, *halos, probe, data, forward, backward, ramp, block_values)
    got_row, got_col, got_cor, total, inbox = pl.pallas_call(
        functools.partial(regroup_kernel, angles),
        out_shape=rim_shapes + (shape((2, 4, BLK, PATCH), BF), shape((group, 8, 2 * BLK), BF)),
        in_specs=[hbm] * 7,
        out_specs=[hbm] * 5,
        scratch_shapes=[
            pltpu.VMEM((2 * ROWS - 2 * RIM, SPAN), BF),
            pltpu.VMEM((2, 2, BLK, PATCH), BF),
            pltpu.VMEM((2, SPAN, BLK), BF),
            pltpu.VMEM((2, BLK, BLK), BF),
            pltpu.VMEM((2, 2, BLK, PATCH), BF),
            pltpu.VMEM((2, 2, BLK, PATCH), F32),
            pltpu.VMEM((2, BLK, PATCH), BF),
            pltpu.VMEM((2, BLK, PATCH), BF),
            pltpu.VMEM((2, 4, BLK, PATCH), BF),
            pltpu.VMEM((2, 2 * ROWS - 2 * RIM, BLK), F32),
            pltpu.VMEM((2, 2, RIM, BLK), BF),
            pltpu.VMEM((2, 2, RIM, BLK), BF),
            pltpu.VMEM((group // 2, 2, 8, 2 * BLK), BF),
            pltpu.VMEM((group, 8, 2 * BLK), BF),
            dma((5,)), dma((3,)), dma((3,)), dma((4, 2)), dma((4, 2)), dma, dma,
            pltpu.SemaphoreType.REGULAR, dma, dma, dma, dma((2,)),
        ],
        compiler_params=pltpu.CompilerParams(
            collective_id=1, has_side_effects=True, vmem_limit_bytes=62 * 1024 * 1024
        ),
    )(sino, row, col, cor, parts, ramp_two, bv_two)
    return pl.pallas_call(
        functools.partial(finish_kernel, angles),
        out_shape=(
            shape((1, 2, TILE, TILE), F32), shape((1, 2, 2, PATCH, PATCH), F32), shape((1, 4, 2, 1024), F32),
        ),
        in_specs=[smem] + [hbm] * 6,
        out_specs=[hbm] * 3,
        scratch_shapes=[
            pltpu.VMEM((2, RIM, TILE - BLK), F32),
            pltpu.VMEM((2, TILE, BLK), F32),
            pltpu.VMEM((2, RIM, TILE), BF),
            pltpu.VMEM((TILE, BLK), BF),
            pltpu.VMEM((RIM, BLK), BF),
            pltpu.VMEM((2, 4, BLK, PATCH), BF),
            pltpu.VMEM((1, 2, 2, PATCH, PATCH), F32),
            pltpu.VMEM((group, 8, 2 * BLK), BF),
            pltpu.VMEM((1, 4, 2, 1024), F32),
            pltpu.SMEM((angles,), jnp.int32),
            dma((7,)), dma((4,)),
        ],
        input_output_aliases={1: 0},
        compiler_params=pltpu.CompilerParams(vmem_limit_bytes=62 * 1024 * 1024),
    )(block_index, og_part, got_row, got_col, got_cor, total, inbox)


def solution(mesh):
    tables = dft_tables() + (ramp_blocks(8),)
    return jax.shard_map(
        functools.partial(body, mesh.shape["ang"], tables),
        mesh=mesh,
        in_specs=(
            P("ang", None, "sy", "sx"),
            P(),
            P("ang", "sy", "sx", None, None, None),
            P("ang", "sy", "sx", None, None),
            P(),
            P(),
        ),
        out_specs=(
            P("ang", None, "sy", "sx"),
            P("ang", None, None, None, None),
            P("sy", ("ang", "sx"), None, None),
        ),
        check_vma=False,
    )
```

```python
import functools
import math

import jax
import jax.numpy as jnp
import numpy as np
from jax import lax
from jax.experimental import pallas as pl
from jax.experimental.pallas import tpu as pltpu
from jax.sharding import PartitionSpec as P

PATCH = 256
RIM = 64
BLK = 128
TILE = 512
ROWS = 640
SPAN = 640
COLS = 768
SECOND = (0, 2, 3, 1)
MESH = pl.DeviceIdType.MESH
BF = jnp.bfloat16
F32 = jnp.float32


def dft_tables():
    ids = np.arange(PATCH)
    phases = (np.outer(ids, ids) % PATCH).astype(np.float64) * (2.0 * math.pi / PATCH)
    factor = 1.0 / math.sqrt(PATCH)
    real = (np.cos(phases) * factor).astype(np.float32)
    imag = (-np.sin(phases) * factor).astype(np.float32)
    forward = np.block([[real, -imag], [imag, real]])
    backward = np.block([[real, imag], [-imag, real]])
    return forward.astype(BF), backward.astype(BF)


def ramp_blocks(line_blocks):
    x = np.arange((2 * line_blocks - 1) * BLK)
    n = np.arange(BLK)[None, :] - (x - (line_blocks - 1) * BLK)[:, None]
    odd = n % 2 != 0
    scaled = n.astype(np.float32) * np.float32(math.pi)
    values = np.where(odd, -1.0 / np.maximum(scaled * scaled, 1.0), 0.0)
    values = np.where(n == 0, 0.25, values).astype(np.float32)
    return values.astype(BF)


def swap_halves(cells):
    return pltpu.roll(cells, BLK // 2, cells.ndim - 1)


def strips_kernel(
    obj_ref, row_out, col_out, cor_out, block, packed, load_sem, send_sem, recv_sem,
):
    ang, sy, sx = lax.axis_index("ang"), lax.axis_index("sy"), lax.axis_index("sx")
    oy, ox = 1 - sy, 1 - sx
    devices = [(ang, oy, sx), (ang, sy, ox), (ang, oy, ox)]
    rows = pl.ds(pl.multiple_of((TILE - RIM) * oy, RIM), RIM)
    cols = pl.ds(pl.multiple_of((TILE - BLK) * ox, BLK), BLK)
    load = pltpu.make_async_copy(obj_ref.at[0, :, :, cols], block, load_sem)
    load.start()
    barrier = pltpu.get_barrier_semaphore()
    for dev in devices:
        pl.semaphore_signal(barrier, inc=1, device_id=dev, device_id_type=MESH)
    load.wait()
    real, imag = block[0].astype(F32), block[1].astype(F32)
    low = lax.broadcasted_iota(jnp.int32, (TILE, BLK), 1) < RIM
    packed[...] = jnp.where(
        low, jnp.where(sx == 0, swap_halves(real), real), jnp.where(sx == 0, imag, swap_halves(imag))
    ).astype(BF)
    pl.semaphore_wait(barrier, 3)
    sources = [obj_ref.at[0, :, rows, :], packed, packed.at[rows]]
    copies = [
        pltpu.make_async_remote_copy(
            src_ref=src, dst_ref=dst, send_sem=send_sem.at[i], recv_sem=recv_sem.at[i],
            device_id=dev, device_id_type=MESH,
        )
        for i, (src, dst, dev) in enumerate(zip(sources, (row_out, col_out, cor_out), devices))
    ]
    for copy in copies:
        copy.start()
    for copy in copies:
        copy.wait()


def patch_kernel(
    angles,
    pos_ref, bi_ref,
    obj_ref, halo_row, halo_col, halo_cor, probe_ref, data_ref, fwd_ref, bwd_ref, ramp_ref, bv_ref,
    og_out, row_out, col_out, cor_out, part_out, msgs_out, over_out, edge_out,
    big, side, probe, data, fwd, bwd, ramp, bv,
    win, patch, exits, half, far, chi, placed, og,
    rim_row, rim_col, rim_cor, part, sino, lines, over_send, edge_send, msgs,
    load_sem, pick_sem, out_sem, piece_sem,
):
    ang, sy, sx = lax.axis_index("ang"), lax.axis_index("sy"), lax.axis_index("sx")
    oy, ox = 1 - sy, 1 - sx
    dst_row = pl.ds(pl.multiple_of((ROWS - RIM) * oy, RIM), RIM)
    dst_col = pl.ds(pl.multiple_of((COLS - BLK) * ox, BLK), BLK)
    loads = [
        pltpu.make_async_copy(src, dst, load_sem.at[i])
        for i, (src, dst) in enumerate(
            [
                (obj_ref.at[0], big.at[:, pl.ds(RIM, TILE), pl.ds(BLK, TILE)]),
                (halo_row, big.at[:, dst_row, pl.ds(BLK, TILE)]),
                (halo_col, side.at[pl.ds(RIM, TILE)]),
                (halo_cor, side.at[dst_row]),
                (probe_ref, probe),
                (fwd_ref, fwd),
                (bwd_ref, bwd),
                (data_ref.at[0, 0, 0], data),
            ]
        )
    ]
    for copy in loads:
        copy.start()

    big[:, pl.ds(pl.multiple_of((ROWS - RIM) * sy, RIM), RIM), :] = jnp.zeros((2, RIM, COLS), BF)
    big[:, :, pl.ds(pl.multiple_of((COLS - BLK) * sx, BLK), BLK)] = jnp.zeros((2, ROWS, BLK), BF)
    for q in range(4):
        placed[q, :, 0:RIM, :] = jnp.zeros((5, RIM, BLK), F32)
        placed[q, :, RIM + PATCH :, :] = jnp.zeros((5, RIM, BLK), F32)
        placed[q, 0, RIM : RIM + PATCH, :] = jnp.zeros((PATCH, BLK), F32)
        placed[q, 4, RIM : RIM + PATCH, :] = jnp.zeros((PATCH, BLK), F32)

    named = [(jnp.int32(-1), jnp.int32(0)), (jnp.int32(0), jnp.int32(0))]
    for j in range(2 * angles):
        entry = bi_ref[j // 16, j % 16]
        mine = (entry >> 3) == ang
        early = jnp.logical_and(mine, named[0][0] < 0)
        named = [
            (jnp.where(take, j, at), jnp.where(take, entry & 7, column))
            for take, (at, column) in zip((early, mine), named)
        ]
    named[0] = (jnp.maximum(named[0][0], 0), named[0][1])
    picks = []
    for s, (entry, column) in enumerate(named):
        at = pl.multiple_of((7 - column + 3 * sx) * BLK, BLK)
        picks.append(
            pltpu.make_async_copy(ramp_ref.at[pl.ds(at, SPAN), :], ramp.at[s], pick_sem.at[2 * s])
        )
        picks.append(
            pltpu.make_async_copy(bv_ref.at[entry >> 4, entry & 15], bv.at[s], pick_sem.at[2 * s + 1])
        )
    for copy in picks:
        copy.start()
    side[pl.ds(pl.multiple_of((ROWS - RIM) * sy, RIM), RIM), :] = jnp.zeros((RIM, BLK), BF)
    for copy in loads[0:4]:
        copy.wait()
    wide = side[...].astype(F32)
    turned = swap_halves(wide)
    big[0, :, dst_col] = jnp.where(sx == 1, turned, wide).astype(BF)
    big[1, :, dst_col] = jnp.where(sx == 1, wide, turned).astype(BF)

    def corner(p):
        return pos_ref[0, 0, 0, p, 0], pos_ref[0, 0, 0, p, 1] + RIM

    def forward_patch(p, carry):
        u, v = corner(p)
        base = jnp.minimum(u >> 4, 23) * 16
        lead = u - base
        block, shift = v >> 7, v & (BLK - 1)
        across = lax.broadcasted_iota(jnp.int32, (384, PATCH), 0)
        pick = jnp.where(
            across == lax.broadcasted_iota(jnp.int32, (384, PATCH), 1) + shift, 1.0, 0.0
        ).astype(BF)
        for c in range(2):
            cells = big[
                c, pl.ds(pl.multiple_of(base, 16), 272), pl.ds(pl.multiple_of(block * BLK, BLK), 384)
            ]
            cells = jnp.dot(cells, pick, preferred_element_type=F32)
            for b in range(2):
                win[c, b] = cells[:, b * BLK : (b + 1) * BLK]
        for c in range(2):
            for b in range(2):
                patch[p, c, :, b * BLK : (b + 1) * BLK] = win[c, b, pl.ds(lead, PATCH), :]
        @pl.when(p == 0)
        def _():
            loads[4].wait()

        for m in range(2):
            exits[m, 0:PATCH] = (probe[m, 0] * patch[p, 0] - probe[m, 1] * patch[p, 1]).astype(BF)
            exits[m, PATCH:] = (probe[m, 0] * patch[p, 1] + probe[m, 1] * patch[p, 0]).astype(BF)
        @pl.when(p == 0)
        def _():
            loads[5].wait()

        for m in range(2):
            done = jnp.dot(fwd[...], exits[m], preferred_element_type=F32)
            half[m, :, 0:PATCH] = done[0:PATCH].astype(BF)
            half[m, :, PATCH:] = done[PATCH:].astype(BF)
        @pl.when(p == 0)
        def _():
            loads[6].wait()

        @pl.when(p == 0)
        def _():
            loads[7].wait()

        for m in range(2):
            far[m] = jnp.dot(half[m], bwd[...], preferred_element_type=F32)
        misfit = (
            far[0, :, 0:PATCH] * far[0, :, 0:PATCH]
            + far[0, :, PATCH:] * far[0, :, PATCH:]
            + far[1, :, 0:PATCH] * far[1, :, 0:PATCH]
            + far[1, :, PATCH:] * far[1, :, PATCH:]
            - data[p].astype(F32)
        )
        for m in range(2):
            exits[m, 0:PATCH] = (misfit * far[m, :, 0:PATCH]).astype(BF)
            exits[m, PATCH:] = (misfit * far[m, :, PATCH:]).astype(BF)
        for m in range(2):
            done = jnp.dot(bwd[...], exits[m], preferred_element_type=F32)
            half[m, :, 0:PATCH] = done[0:PATCH].astype(BF)
            half[m, :, PATCH:] = done[PATCH:].astype(BF)
        for m in range(2):
            chi[p, m] = jnp.dot(half[m], fwd[...], preferred_element_type=F32)
        cr = [chi[p, m, :, 0:PATCH] for m in range(2)]
        ci = [chi[p, m, :, PATCH:] for m in range(2)]
        grad = [
            probe[0, 0] * cr[0] + probe[0, 1] * ci[0] + probe[1, 0] * cr[1] + probe[1, 1] * ci[1],
            probe[0, 0] * ci[0] - probe[0, 1] * cr[0] + probe[1, 0] * ci[1] - probe[1, 1] * cr[1],
        ]
        spots = lax.broadcasted_iota(jnp.int32, (PATCH, 384), 1)
        put = jnp.where(
            spots == lax.broadcasted_iota(jnp.int32, (PATCH, 384), 0) + shift, 1.0, 0.0
        ).astype(BF)
        for c in range(2):
            high = grad[c].astype(BF)
            low = (grad[c] - high.astype(F32)).astype(BF)
            moved = jnp.dot(high, put, preferred_element_type=F32) + jnp.dot(
                low, put, preferred_element_type=F32
            )
            for b in range(3):
                placed[p * 2 + c, b + 1, RIM : RIM + PATCH, :] = moved[:, b * BLK : (b + 1) * BLK]
        return carry

    lax.fori_loop(0, 2, forward_patch, 0)

    def cells_at(c, row_chunk, lane_block):
        total_cells = None
        for p in range(2):
            u, v = corner(p)
            row = jnp.minimum(jnp.maximum(row_chunk * RIM - u + RIM, 0), PATCH + RIM)
            lane = jnp.minimum(jnp.maximum(lane_block - (v >> 7), -1), 3) + 1
            term = placed[p * 2 + c, lane, pl.ds(row, RIM), :]
            total_cells = term if total_cells is None else total_cells + term
        return total_cells

    rim_chunk = 9 * oy
    rim_block = 5 * ox
    for c in range(2):
        for b in range(4):
            rim_row[c, :, b * BLK : (b + 1) * BLK] = cells_at(c, rim_chunk, b + 1).astype(BF)

    def packed_rim(row_chunk):
        real, imag = (cells_at(c, row_chunk, rim_block) for c in range(2))
        kept, moved = jnp.where(sx == 0, real, imag), jnp.where(sx == 0, imag, real)
        return (kept + swap_halves(moved)).astype(BF)

    rim_cor[...] = packed_rim(rim_chunk)

    def rim_columns(r, carry):
        rim_col[pl.ds(pl.multiple_of(r * RIM, RIM), RIM), :] = packed_rim(r + 1)
        return carry

    lax.fori_loop(0, 8, rim_columns, 0)
    outs = [
        pltpu.make_async_copy(src, dst, out_sem.at[i])
        for i, (src, dst) in enumerate(
            [
                (rim_row, row_out), (rim_col, col_out), (rim_cor, cor_out),
                (part, part_out), (msgs, msgs_out), (over_send, over_out), (edge_send, edge_out),
            ]
        )
    ]
    for copy in outs[:3]:
        copy.start()
    for copy in picks:
        copy.wait()

    for c in range(2):
        for b in range(5):
            sino[2 * TILE + c * RIM : 2 * TILE + (c + 1) * RIM, b * BLK : (b + 1) * BLK] = cells_at(
                c, rim_chunk, b + ox
            ).astype(BF)

    def finished(r):
        rows = pl.ds(pl.multiple_of(r * RIM, RIM), RIM)
        return pltpu.make_async_copy(og.at[:, rows], og_out.at[0, :, rows], piece_sem.at[r])

    def interior(r, carry):
        rows = pl.ds(pl.multiple_of(r * RIM, RIM), RIM)
        for c in range(2):
            for b in range(4):
                og[c, rows, b * BLK : (b + 1) * BLK] = cells_at(c, r + 1, b + 1)
            for b in range(5):
                sino[pl.ds(pl.multiple_of(c * TILE + r * RIM, RIM), RIM), b * BLK : (b + 1) * BLK] = cells_at(
                    c, r + 1, b + ox
                ).astype(BF)
        finished(r).start()
        return carry

    lax.fori_loop(0, 8, interior, 0)

    for m in range(2):
        real, imag = (
            patch[0, 0] * chi[0, m, :, a] + sign * patch[0, 1] * chi[0, m, :, b]
            + patch[1, 0] * chi[1, m, :, a] + sign * patch[1, 1] * chi[1, m, :, b]
            for a, b, sign in ((slice(0, PATCH), slice(PATCH, 512), 1.0), (slice(PATCH, 512), slice(0, PATCH), -1.0))
        )
        for q, terms in ((2 * m, real), (2 * m + 1, imag)):
            part[0, q] = terms[0:BLK].astype(BF)
            part[1, SECOND[q]] = terms[BLK:].astype(BF)
    outs[3].start()
    for s in range(2):
        filtered = jnp.dot(sino[...], ramp[s], preferred_element_type=F32).astype(BF)
        lines[s] = jnp.dot(filtered, bv[s], preferred_element_type=F32)
        for c in range(2):
            over_send[s, c] = lines[s, 2 * TILE + c * RIM : 2 * TILE + (c + 1) * RIM, :].astype(BF)
            edge_send[s, c] = lines[s, pl.ds(pl.multiple_of(c * TILE + (TILE - RIM) * oy, RIM), RIM), :]
    top = lax.broadcasted_iota(jnp.int32, (64, 8, BLK), 1) < 4
    for s in range(2):
        a = lines[s, 0:TILE, :].reshape(64, 8, BLK)
        b = lines[s, TILE : 2 * TILE, :].reshape(64, 8, BLK)
        lanes = slice(s * BLK, (s + 1) * BLK)
        msgs[:, 0, :, lanes] = jnp.where(top, a, pltpu.roll(b, 4, 1)).astype(BF)
        msgs[:, 1, :, lanes] = jnp.where(top, pltpu.roll(a, 4, 1), b).astype(BF)
    for copy in outs[4:]:
        copy.start()

    def settle(r, carry):
        finished(r).wait()
        return carry

    lax.fori_loop(0, 8, settle, 0)
    for copy in outs:
        copy.wait()


def regroup_kernel(
    angles,
    msgs_ref, over_ref, edge_ref, row_ref, col_ref, cor_ref, part_ref,
    got_row, got_col, got_cor, total_out, inbox_out,
    part, part_got, part_sum, quarter_send, quarter_got, total,
    edges, over_got, last_msgs, inbox,
    load_sem, rim_send, rim_recv, part_ssem, part_rsem, over_ssem, over_rsem,
    word_sem, a2a_send, a2a_recv, own_sem, out_sem,
):
    ang, sy, sx = lax.axis_index("ang"), lax.axis_index("sy"), lax.axis_index("sx")
    oy, ox = 1 - sy, 1 - sx
    group = 2 * angles
    me = ang * 2 + sx

    barrier = pltpu.get_barrier_semaphore()
    line, place = ang >> 4, ang & 15
    spot = line * 2 + sx
    crosswise = []
    for k in range(1, group // 16):
        d = jnp.bitwise_xor(spot, k)
        crosswise.append(((d >> 1) * 16 + place, sy, d & 1))
    lengthwise = [(line * 16 + ((place + k) & 15), sy, sx) for k in range(1, 16)]
    greeted = [(ang, oy, sx), (ang, oy, ox)] + crosswise + lengthwise
    for dev in greeted:
        pl.semaphore_signal(barrier, inc=1, device_id=dev, device_id_type=MESH)
    across, beside = (ang, oy, ox), (ang, sy, ox)
    kind = jnp.bitwise_xor(sy, sx)
    routes = (
        (across, beside, 2 * sy, 2 * oy, sx, ox),
        (beside, across, 2 * kind, 2 * (1 - kind), sy, oy),
    )
    loads = [
        pltpu.make_async_copy(src, dst, load_sem.at[i])
        for i, (src, dst) in enumerate(
            [(edge_ref, edges)]
            + [(part_ref.at[h, pl.ds(routes[h][2], 2)], part.at[h]) for h in range(2)]
        )
    ]
    for copy in loads:
        copy.start()
    pl.semaphore_wait(barrier, len(greeted))

    for dev in crosswise:
        pl.semaphore_signal(word_sem, inc=1, device_id=dev, device_id_type=MESH)

    def exchange(step, h, src, dst, dev):
        return pltpu.make_async_remote_copy(
            src_ref=src, dst_ref=dst, send_sem=part_ssem.at[step, h], recv_sem=part_rsem.at[step, h],
            device_id=dev, device_id_type=MESH,
        )

    firsts = [
        exchange(0, h, part_ref.at[h, pl.ds(routes[h][3], 2)], part_got.at[h], routes[h][0])
        for h in range(2)
    ]
    over = pltpu.make_async_remote_copy(
        src_ref=over_ref, dst_ref=over_got, send_sem=over_ssem, recv_sem=over_rsem,
        device_id=(ang, oy, sx), device_id_type=MESH,
    )
    over.start()
    for copy in firsts:
        copy.start()
    top = lax.broadcasted_iota(jnp.int32, (8, 8, BLK), 1) < 4

    def send_to(src, d):
        @pl.when(d != me)
        def _():
            pltpu.make_async_remote_copy(
                src_ref=src, dst_ref=inbox.at[me], send_sem=a2a_send, recv_sem=a2a_recv,
                device_id=(d >> 1, sy, d & 1), device_id_type=MESH,
            ).start()

    inner = group - 16

    def send_inner(k, carry):
        d = 16 * sy + lax.rem(me + k, inner)
        send_to(msgs_ref.at[d >> 1, d & 1], d)
        return carry

    def send_edge(k, carry):
        e = (me + k) & 15
        send_to(last_msgs.at[e >> 1, e & 1], inner * oy + e)
        return carry

    pl.semaphore_wait(word_sem, len(crosswise))
    lax.fori_loop(0, inner // 2, send_inner, 0)
    for copy in loads:
        copy.wait()
    seconds = []
    for h, (_, after, _, _, keep, give) in enumerate(routes):
        firsts[h].wait()
        part_sum[h] = part[h].astype(F32) + part_got[h].astype(F32)
        quarter_send[h] = part_sum[h, give].astype(BF)
        seconds.append(exchange(1, h, quarter_send.at[h], quarter_got.at[h], after))
        seconds[h].start()
    lax.fori_loop(inner // 2, inner, send_inner, 0)
    over.wait()
    for s in range(2):
        a = (edges[s, 0] + over_got[s, 0].astype(F32)).reshape(8, 8, BLK)
        b = (edges[s, 1] + over_got[s, 1].astype(F32)).reshape(8, 8, BLK)
        lanes = slice(s * BLK, (s + 1) * BLK)
        last_msgs[:, 0, :, lanes] = jnp.where(top, a, pltpu.roll(b, 4, 1)).astype(BF)
        last_msgs[:, 1, :, lanes] = jnp.where(top, pltpu.roll(a, 4, 1), b).astype(BF)
    lax.fori_loop(0, 16, send_edge, 0)
    own = pltpu.make_async_copy(msgs_ref.at[ang, sx], inbox.at[me], own_sem)
    own_last = pltpu.make_async_copy(last_msgs.at[(me & 15) >> 1, sx], inbox.at[me], own_sem)
    at_edge = jnp.logical_and(me >= inner * oy, me < inner * oy + 16)

    @pl.when(at_edge)
    def _():
        own_last.start()

    @pl.when(jnp.logical_not(at_edge))
    def _():
        own.start()


    thirds = []
    for h, (_, after, base, _, keep, _) in enumerate(routes):
        seconds[h].wait()
        at = total.at[h, base + keep]
        total[h, base + keep] = (part_sum[h, keep] + quarter_got[h].astype(F32)).astype(BF)
        thirds.append(exchange(2, h, at, at, after))
        thirds[h].start()
    rims = [
        pltpu.make_async_remote_copy(
            src_ref=src, dst_ref=dst, send_sem=rim_send.at[i], recv_sem=rim_recv.at[i],
            device_id=dev, device_id_type=MESH,
        )
        for i, (src, dst, dev) in enumerate(
            [
                (row_ref, got_row, (ang, oy, sx)),
                (col_ref, got_col, beside),
                (cor_ref, got_cor, across),
            ]
        )
    ]
    for copy in rims:
        copy.start()
    fourths = []
    for h, (before, _, base, _, _, _) in enumerate(routes):
        thirds[h].wait()
        at = total.at[h, pl.ds(base, 2)]
        fourths.append(exchange(3, h, at, at, before))
        fourths[h].start()
    own.wait()
    pltpu.make_async_copy(
        inbox.at[pl.ds(0, group - 1)], inbox.at[pl.ds(0, group - 1)], a2a_recv
    ).wait()
    inbox_copy = pltpu.make_async_copy(inbox, inbox_out, out_sem.at[0])
    inbox_copy.start()
    for copy in fourths:
        copy.wait()
    total_copy = pltpu.make_async_copy(total, total_out, out_sem.at[1])
    total_copy.start()
    pltpu.make_async_copy(
        inbox.at[pl.ds(0, group - 1)], inbox.at[pl.ds(0, group - 1)], a2a_send
    ).wait()
    for copy in rims:
        copy.wait()
    inbox_copy.wait()
    total_copy.wait()


def finish_kernel(
    angles, bi_ref, og_ref, row_ref, col_ref, cor_ref, total_ref, inbox_ref, og_out, pg_out, vol_out,
    og_row, og_col, row, col, cor, total, pg, inbox, vol, seen, in_sem, out_sem,
):
    sy, sx = lax.axis_index("sy"), lax.axis_index("sx")
    oy, ox = 1 - sy, 1 - sx
    row_at = pl.ds(pl.multiple_of((TILE - RIM) * oy, RIM), RIM)
    col_at = pl.ds(pl.multiple_of((TILE - BLK) * ox, BLK), BLK)
    rest_at = pl.ds(pl.multiple_of(BLK * sx, BLK), TILE - BLK)
    loads = [
        pltpu.make_async_copy(src, dst, in_sem.at[i])
        for i, (src, dst) in enumerate(
            [
                (og_ref.at[0, :, row_at, rest_at], og_row), (og_ref.at[0, :, :, col_at], og_col),
                (row_ref, row), (col_ref, col), (cor_ref, cor), (total_ref, total), (inbox_ref, inbox),
            ]
        )
    ]
    for copy in loads:
        copy.start()
    summed, arrived = loads[5:]
    for a in range(angles):
        seen[a] = 0
    summed.wait()
    for q in range(4):
        pg[0, q // 2, q % 2, 0:BLK, :] = total[0, q].astype(F32) * (1.0 / math.sqrt(8.0))
        pg[0, q // 2, q % 2, BLK:, :] = total[1, SECOND[q]].astype(F32) * (1.0 / math.sqrt(8.0))
    pg_copy = pltpu.make_async_copy(pg, pg_out, out_sem.at[0])
    pg_copy.start()
    for copy in loads[0:5]:
        copy.wait()
    for got, at in ((col, pl.ds(0, TILE)), (cor, row_at)):
        wide = got[...].astype(F32)
        turned = swap_halves(wide)
        low = lax.broadcasted_iota(jnp.int32, wide.shape, 1) < RIM
        added = (
            jnp.where(sx == 1, jnp.where(low, wide, 0.0), jnp.where(low, 0.0, turned)),
            jnp.where(sx == 1, jnp.where(low, turned, 0.0), jnp.where(low, 0.0, wide)),
        )
        for c in range(2):
            og_col[c, at, :] = og_col[c, at, :] + added[c]
    for c in range(2):
        og_row[c] = og_row[c] + row[c, :, rest_at].astype(F32)
        og_col[c, row_at, :] = og_col[c, row_at, :] + row[c, :, col_at].astype(F32)
    og_copies = [
        pltpu.make_async_copy(og_row, og_out.at[0, :, row_at, rest_at], out_sem.at[2]),
        pltpu.make_async_copy(og_col, og_out.at[0, :, :, col_at], out_sem.at[3]),
    ]
    for copy in og_copies:
        copy.start()
    arrived.wait()
    for b in range(8):
        line = jnp.zeros((8, BLK), F32)
        for k in range(16):
            source = bi_ref[b, k] >> 3
            slot = seen[source]
            seen[source] = 1
            lane = pl.multiple_of(slot * BLK, BLK)
            for h in range(2):
                line = line + inbox[source * 2 + h, :, pl.ds(lane, BLK)].astype(F32)
        for c in range(2):
            for r in range(4):
                vol[0, r, c, b * BLK : (b + 1) * BLK] = line[c * 4 + r]
    vol_copy = pltpu.make_async_copy(vol, vol_out, out_sem.at[1])
    vol_copy.start()
    for copy in og_copies:
        copy.wait()
    pg_copy.wait()
    vol_copy.wait()


def body(angles, tables, objects, probe, data, positions, block_index, block_values):
    forward, backward, ramp = (jnp.asarray(t) for t in tables)
    group = 2 * angles
    dma = pltpu.SemaphoreType.DMA
    smem = pl.BlockSpec(memory_space=pltpu.SMEM)
    hbm = pl.BlockSpec(memory_space=pltpu.HBM)

    def shape(dims, kind):
        return jax.ShapeDtypeStruct(dims, kind)

    rim_shapes = (shape((2, RIM, TILE), BF), shape((TILE, BLK), BF), shape((RIM, BLK), BF))
    halos = pl.pallas_call(
        strips_kernel,
        out_shape=rim_shapes,
        in_specs=[hbm],
        out_specs=[hbm] * 3,
        scratch_shapes=[
            pltpu.VMEM((2, TILE, BLK), BF), pltpu.VMEM((TILE, BLK), BF), dma, dma((3,)), dma((3,)),
        ],
        compiler_params=pltpu.CompilerParams(
            collective_id=0, has_side_effects=True, vmem_limit_bytes=62 * 1024 * 1024
        ),
    )(objects)
    og_part, row, col, cor, parts, messages, over, edges = pl.pallas_call(
        functools.partial(patch_kernel, angles),
        out_shape=(shape((1, 2, TILE, TILE), F32),) + rim_shapes + (
            shape((2, 4, BLK, PATCH), BF), shape((group // 2, 2, 8, 2 * BLK), BF),
            shape((2, 2, RIM, BLK), BF), shape((2, 2, RIM, BLK), F32),
        ),
        in_specs=[smem] * 2 + [hbm] * 10,
        out_specs=[hbm] * 8,
        scratch_shapes=[
            pltpu.VMEM((2, ROWS, COLS), BF),
            pltpu.VMEM((ROWS, BLK), BF),
            pltpu.VMEM((2, 2, PATCH, PATCH), F32),
            pltpu.VMEM((2, PATCH, PATCH), BF),
            pltpu.VMEM((512, 512), BF),
            pltpu.VMEM((512, 512), BF),
            pltpu.VMEM((2, SPAN, BLK), BF),
            pltpu.VMEM((2, BLK, BLK), BF),
            pltpu.VMEM((2, 2, 272, BLK), F32),
            pltpu.VMEM((2, 2, PATCH, PATCH), F32),
            pltpu.VMEM((2, 512, PATCH), BF),
            pltpu.VMEM((2, PATCH, 512), BF),
            pltpu.VMEM((2, PATCH, 512), F32),
            pltpu.VMEM((2, 2, PATCH, 512), F32),
            pltpu.VMEM((4, 5, 384, BLK), F32),
            pltpu.VMEM((2, TILE, TILE), F32),
            pltpu.VMEM((2, RIM, TILE), BF),
            pltpu.VMEM((TILE, BLK), BF),
            pltpu.VMEM((RIM, BLK), BF),
            pltpu.VMEM((2, 4, BLK, PATCH), BF),
            pltpu.VMEM((2 * ROWS - 2 * RIM, SPAN), BF),
            pltpu.VMEM((2, 2 * ROWS - 2 * RIM, BLK), F32),
            pltpu.VMEM((2, 2, RIM, BLK), BF),
            pltpu.VMEM((2, 2, RIM, BLK), F32),
            pltpu.VMEM((group // 2, 2, 8, 2 * BLK), BF),
            dma((8,)), dma((4,)), dma((7,)), dma((8,)),
        ],
        compiler_params=pltpu.CompilerParams(vmem_limit_bytes=62 * 1024 * 1024),
    )(positions, block_index, objects, *halos, probe, data, forward, backward, ramp, block_values)
    got_row, got_col, got_cor, total, inbox = pl.pallas_call(
        functools.partial(regroup_kernel, angles),
        out_shape=rim_shapes + (shape((2, 4, BLK, PATCH), BF), shape((group, 8, 2 * BLK), BF)),
        in_specs=[hbm] * 7,
        out_specs=[hbm] * 5,
        scratch_shapes=[
            pltpu.VMEM((2, 2, BLK, PATCH), BF),
            pltpu.VMEM((2, 2, BLK, PATCH), BF),
            pltpu.VMEM((2, 2, BLK, PATCH), F32),
            pltpu.VMEM((2, BLK, PATCH), BF),
            pltpu.VMEM((2, BLK, PATCH), BF),
            pltpu.VMEM((2, 4, BLK, PATCH), BF),
            pltpu.VMEM((2, 2, RIM, BLK), F32),
            pltpu.VMEM((2, 2, RIM, BLK), BF),
            pltpu.VMEM((8, 2, 8, 2 * BLK), BF),
            pltpu.VMEM((group, 8, 2 * BLK), BF),
            dma((3,)), dma((3,)), dma((3,)), dma((4, 2)), dma((4, 2)), dma, dma,
            pltpu.SemaphoreType.REGULAR, dma, dma, dma, dma((2,)),
        ],
        compiler_params=pltpu.CompilerParams(
            collective_id=1, has_side_effects=True, vmem_limit_bytes=62 * 1024 * 1024
        ),
    )(messages, over, edges, row, col, cor, parts)
    return pl.pallas_call(
        functools.partial(finish_kernel, angles),
        out_shape=(
            shape((1, 2, TILE, TILE), F32), shape((1, 2, 2, PATCH, PATCH), F32), shape((1, 4, 2, 1024), F32),
        ),
        in_specs=[smem] + [hbm] * 6,
        out_specs=[hbm] * 3,
        scratch_shapes=[
            pltpu.VMEM((2, RIM, TILE - BLK), F32),
            pltpu.VMEM((2, TILE, BLK), F32),
            pltpu.VMEM((2, RIM, TILE), BF),
            pltpu.VMEM((TILE, BLK), BF),
            pltpu.VMEM((RIM, BLK), BF),
            pltpu.VMEM((2, 4, BLK, PATCH), BF),
            pltpu.VMEM((1, 2, 2, PATCH, PATCH), F32),
            pltpu.VMEM((group, 8, 2 * BLK), BF),
            pltpu.VMEM((1, 4, 2, 1024), F32),
            pltpu.SMEM((angles,), jnp.int32),
            dma((7,)), dma((4,)),
        ],
        input_output_aliases={1: 0},
        compiler_params=pltpu.CompilerParams(vmem_limit_bytes=62 * 1024 * 1024),
    )(block_index, og_part, got_row, got_col, got_cor, total, inbox)


def solution(mesh):
    tables = dft_tables() + (ramp_blocks(8),)
    return jax.shard_map(
        functools.partial(body, mesh.shape["ang"], tables),
        mesh=mesh,
        in_specs=(
            P("ang", None, "sy", "sx"),
            P(),
            P("ang", "sy", "sx", None, None, None),
            P("ang", "sy", "sx", None, None),
            P(),
            P(),
        ),
        out_specs=(
            P("ang", None, "sy", "sx"),
            P("ang", None, None, None, None),
            P("sy", ("ang", "sx"), None, None),
        ),
        check_vma=False,
    )
```

```python
import functools
import math

import jax
import jax.numpy as jnp
import numpy as np
from jax import lax
from jax.experimental import pallas as pl
from jax.experimental.pallas import tpu as pltpu
from jax.sharding import PartitionSpec as P

PATCH = 256
RIM = 64
BLK = 128
TILE = 512
ROWS = 640
SPAN = 640
COLS = 768
SECOND = (0, 2, 3, 1)
MESH = pl.DeviceIdType.MESH
BF = jnp.bfloat16
F32 = jnp.float32


def dft_tables():
    ids = np.arange(PATCH)
    phases = (np.outer(ids, ids) % PATCH).astype(np.float64) * (2.0 * math.pi / PATCH)
    factor = 1.0 / math.sqrt(PATCH)
    real = (np.cos(phases) * factor).astype(np.float32)
    imag = (-np.sin(phases) * factor).astype(np.float32)
    forward = np.block([[real, -imag], [imag, real]])
    backward = np.block([[real, imag], [-imag, real]])
    return forward.astype(BF), backward.astype(BF)


def ramp_blocks(line_blocks):
    x = np.arange((2 * line_blocks - 1) * BLK)
    n = np.arange(BLK)[None, :] - (x - (line_blocks - 1) * BLK)[:, None]
    odd = n % 2 != 0
    scaled = n.astype(np.float32) * np.float32(math.pi)
    values = np.where(odd, -1.0 / np.maximum(scaled * scaled, 1.0), 0.0)
    values = np.where(n == 0, 0.25, values).astype(np.float32)
    return values.astype(BF)


def swap_halves(cells):
    return pltpu.roll(cells, BLK // 2, cells.ndim - 1)


def strips_kernel(
    obj_ref, row_out, col_out, cor_out, block, packed, load_sem, send_sem, recv_sem,
):
    ang, sy, sx = lax.axis_index("ang"), lax.axis_index("sy"), lax.axis_index("sx")
    oy, ox = 1 - sy, 1 - sx
    devices = [(ang, oy, sx), (ang, sy, ox), (ang, oy, ox)]
    rows = pl.ds(pl.multiple_of((TILE - RIM) * oy, RIM), RIM)
    cols = pl.ds(pl.multiple_of((TILE - BLK) * ox, BLK), BLK)
    load = pltpu.make_async_copy(obj_ref.at[0, :, :, cols], block, load_sem)
    load.start()
    barrier = pltpu.get_barrier_semaphore()
    for dev in devices:
        pl.semaphore_signal(barrier, inc=1, device_id=dev, device_id_type=MESH)
    load.wait()
    real, imag = block[0].astype(F32), block[1].astype(F32)
    low = lax.broadcasted_iota(jnp.int32, (TILE, BLK), 1) < RIM
    packed[...] = jnp.where(
        low, jnp.where(sx == 0, swap_halves(real), real), jnp.where(sx == 0, imag, swap_halves(imag))
    ).astype(BF)
    pl.semaphore_wait(barrier, 3)
    sources = [obj_ref.at[0, :, rows, :], packed, packed.at[rows]]
    copies = [
        pltpu.make_async_remote_copy(
            src_ref=src, dst_ref=dst, send_sem=send_sem.at[i], recv_sem=recv_sem.at[i],
            device_id=dev, device_id_type=MESH,
        )
        for i, (src, dst, dev) in enumerate(zip(sources, (row_out, col_out, cor_out), devices))
    ]
    for copy in copies:
        copy.start()
    for copy in copies:
        copy.wait()


def patch_kernel(
    angles,
    pos_ref, bi_ref,
    obj_ref, halo_row, halo_col, halo_cor, probe_ref, data_ref, fwd_ref, bwd_ref, ramp_ref, bv_ref,
    og_out, row_out, col_out, cor_out, part_out, ramp_out, bv_out, sino_out,
    big, side, probe, data, fwd, bwd, ramp, bv,
    win, patch, exits, half, far, chi, placed, og,
    rim_row, rim_col, rim_cor, part, sino,
    load_sem, pick_sem, out_sem, piece_sem,
):
    ang, sy, sx = lax.axis_index("ang"), lax.axis_index("sy"), lax.axis_index("sx")
    oy, ox = 1 - sy, 1 - sx
    dst_row = pl.ds(pl.multiple_of((ROWS - RIM) * oy, RIM), RIM)
    dst_col = pl.ds(pl.multiple_of((COLS - BLK) * ox, BLK), BLK)
    loads = [
        pltpu.make_async_copy(src, dst, load_sem.at[i])
        for i, (src, dst) in enumerate(
            [
                (obj_ref.at[0], big.at[:, pl.ds(RIM, TILE), pl.ds(BLK, TILE)]),
                (halo_row, big.at[:, dst_row, pl.ds(BLK, TILE)]),
                (halo_col, side.at[pl.ds(RIM, TILE)]),
                (halo_cor, side.at[dst_row]),
                (probe_ref, probe),
                (fwd_ref, fwd),
                (bwd_ref, bwd),
                (data_ref.at[0, 0, 0], data),
            ]
        )
    ]
    for copy in loads:
        copy.start()

    big[:, pl.ds(pl.multiple_of((ROWS - RIM) * sy, RIM), RIM), :] = jnp.zeros((2, RIM, COLS), BF)
    big[:, :, pl.ds(pl.multiple_of((COLS - BLK) * sx, BLK), BLK)] = jnp.zeros((2, ROWS, BLK), BF)
    for q in range(4):
        placed[q, :, 0:RIM, :] = jnp.zeros((5, RIM, BLK), F32)
        placed[q, :, RIM + PATCH :, :] = jnp.zeros((5, RIM, BLK), F32)
        placed[q, 0, RIM : RIM + PATCH, :] = jnp.zeros((PATCH, BLK), F32)
        placed[q, 4, RIM : RIM + PATCH, :] = jnp.zeros((PATCH, BLK), F32)

    named = [(jnp.int32(-1), jnp.int32(0)), (jnp.int32(0), jnp.int32(0))]
    for j in range(2 * angles):
        entry = bi_ref[j // 16, j % 16]
        mine = (entry >> 3) == ang
        early = jnp.logical_and(mine, named[0][0] < 0)
        named = [
            (jnp.where(take, j, at), jnp.where(take, entry & 7, column))
            for take, (at, column) in zip((early, mine), named)
        ]
    named[0] = (jnp.maximum(named[0][0], 0), named[0][1])
    picks = []
    for s, (entry, column) in enumerate(named):
        at = pl.multiple_of((7 - column + 3 * sx) * BLK, BLK)
        picks.append(
            pltpu.make_async_copy(ramp_ref.at[pl.ds(at, SPAN), :], ramp.at[s], pick_sem.at[2 * s])
        )
        picks.append(
            pltpu.make_async_copy(bv_ref.at[entry >> 4, entry & 15], bv.at[s], pick_sem.at[2 * s + 1])
        )
    for copy in picks:
        copy.start()
    side[pl.ds(pl.multiple_of((ROWS - RIM) * sy, RIM), RIM), :] = jnp.zeros((RIM, BLK), BF)
    for copy in loads[0:4]:
        copy.wait()
    wide = side[...].astype(F32)
    turned = swap_halves(wide)
    big[0, :, dst_col] = jnp.where(sx == 1, turned, wide).astype(BF)
    big[1, :, dst_col] = jnp.where(sx == 1, wide, turned).astype(BF)

    def corner(p):
        return pos_ref[0, 0, 0, p, 0], pos_ref[0, 0, 0, p, 1] + RIM

    def forward_patch(p, carry):
        u, v = corner(p)
        base = jnp.minimum(u >> 4, 23) * 16
        lead = u - base
        block, shift = v >> 7, v & (BLK - 1)
        across = lax.broadcasted_iota(jnp.int32, (384, PATCH), 0)
        pick = jnp.where(
            across == lax.broadcasted_iota(jnp.int32, (384, PATCH), 1) + shift, 1.0, 0.0
        ).astype(BF)
        for c in range(2):
            cells = big[
                c, pl.ds(pl.multiple_of(base, 16), 272), pl.ds(pl.multiple_of(block * BLK, BLK), 384)
            ]
            cells = jnp.dot(cells, pick, preferred_element_type=F32)
            for b in range(2):
                win[c, b] = cells[:, b * BLK : (b + 1) * BLK]
        for c in range(2):
            for b in range(2):
                patch[p, c, :, b * BLK : (b + 1) * BLK] = win[c, b, pl.ds(lead, PATCH), :]
        @pl.when(p == 0)
        def _():
            loads[4].wait()

        for m in range(2):
            exits[m, 0:PATCH] = (probe[m, 0] * patch[p, 0] - probe[m, 1] * patch[p, 1]).astype(BF)
            exits[m, PATCH:] = (probe[m, 0] * patch[p, 1] + probe[m, 1] * patch[p, 0]).astype(BF)
        @pl.when(p == 0)
        def _():
            loads[5].wait()

        for m in range(2):
            done = jnp.dot(fwd[...], exits[m], preferred_element_type=F32)
            half[m, :, 0:PATCH] = done[0:PATCH].astype(BF)
            half[m, :, PATCH:] = done[PATCH:].astype(BF)
        @pl.when(p == 0)
        def _():
            loads[6].wait()

        @pl.when(p == 0)
        def _():
            loads[7].wait()

        for m in range(2):
            far[m] = jnp.dot(half[m], bwd[...], preferred_element_type=F32)
        misfit = (
            far[0, :, 0:PATCH] * far[0, :, 0:PATCH]
            + far[0, :, PATCH:] * far[0, :, PATCH:]
            + far[1, :, 0:PATCH] * far[1, :, 0:PATCH]
            + far[1, :, PATCH:] * far[1, :, PATCH:]
            - data[p].astype(F32)
        )
        for m in range(2):
            exits[m, 0:PATCH] = (misfit * far[m, :, 0:PATCH]).astype(BF)
            exits[m, PATCH:] = (misfit * far[m, :, PATCH:]).astype(BF)
        for m in range(2):
            done = jnp.dot(bwd[...], exits[m], preferred_element_type=F32)
            half[m, :, 0:PATCH] = done[0:PATCH].astype(BF)
            half[m, :, PATCH:] = done[PATCH:].astype(BF)
        for m in range(2):
            chi[p, m] = jnp.dot(half[m], fwd[...], preferred_element_type=F32)
        cr = [chi[p, m, :, 0:PATCH] for m in range(2)]
        ci = [chi[p, m, :, PATCH:] for m in range(2)]
        grad = [
            probe[0, 0] * cr[0] + probe[0, 1] * ci[0] + probe[1, 0] * cr[1] + probe[1, 1] * ci[1],
            probe[0, 0] * ci[0] - probe[0, 1] * cr[0] + probe[1, 0] * ci[1] - probe[1, 1] * cr[1],
        ]
        spots = lax.broadcasted_iota(jnp.int32, (PATCH, 384), 1)
        put = jnp.where(
            spots == lax.broadcasted_iota(jnp.int32, (PATCH, 384), 0) + shift, 1.0, 0.0
        ).astype(BF)
        for c in range(2):
            high = grad[c].astype(BF)
            low = (grad[c] - high.astype(F32)).astype(BF)
            moved = jnp.dot(high, put, preferred_element_type=F32) + jnp.dot(
                low, put, preferred_element_type=F32
            )
            for b in range(3):
                placed[p * 2 + c, b + 1, RIM : RIM + PATCH, :] = moved[:, b * BLK : (b + 1) * BLK]
        return carry

    lax.fori_loop(0, 2, forward_patch, 0)

    def cells_at(c, row_chunk, lane_block):
        total_cells = None
        for p in range(2):
            u, v = corner(p)
            row = jnp.minimum(jnp.maximum(row_chunk * RIM - u + RIM, 0), PATCH + RIM)
            lane = jnp.minimum(jnp.maximum(lane_block - (v >> 7), -1), 3) + 1
            term = placed[p * 2 + c, lane, pl.ds(row, RIM), :]
            total_cells = term if total_cells is None else total_cells + term
        return total_cells

    rim_chunk = 9 * oy
    rim_block = 5 * ox
    for c in range(2):
        for b in range(4):
            rim_row[c, :, b * BLK : (b + 1) * BLK] = cells_at(c, rim_chunk, b + 1).astype(BF)

    def packed_rim(row_chunk):
        real, imag = (cells_at(c, row_chunk, rim_block) for c in range(2))
        kept, moved = jnp.where(sx == 0, real, imag), jnp.where(sx == 0, imag, real)
        return (kept + swap_halves(moved)).astype(BF)

    rim_cor[...] = packed_rim(rim_chunk)

    def rim_columns(r, carry):
        rim_col[pl.ds(pl.multiple_of(r * RIM, RIM), RIM), :] = packed_rim(r + 1)
        return carry

    lax.fori_loop(0, 8, rim_columns, 0)
    outs = [
        pltpu.make_async_copy(src, dst, out_sem.at[i])
        for i, (src, dst) in enumerate(
            [
                (rim_row, row_out), (rim_col, col_out), (rim_cor, cor_out),
                (part, part_out), (ramp, ramp_out), (bv, bv_out),
            ]
        )
    ]
    for copy in outs[:3]:
        copy.start()
    for copy in picks:
        copy.wait()
    for copy in outs[4:6]:
        copy.start()

    for c in range(2):
        for b in range(5):
            sino[2 * TILE + c * RIM : 2 * TILE + (c + 1) * RIM, b * BLK : (b + 1) * BLK] = cells_at(
                c, rim_chunk, b + ox
            ).astype(BF)

    over_rows = pl.ds(2 * TILE, 2 * RIM)
    over_copy = pltpu.make_async_copy(sino.at[over_rows], sino_out.at[over_rows], out_sem.at[6])
    over_copy.start()

    def finished(r):
        rows = pl.ds(pl.multiple_of(r * RIM, RIM), RIM)
        spans = [pl.ds(pl.multiple_of(c * TILE + r * RIM, RIM), RIM) for c in range(2)]
        return [pltpu.make_async_copy(og.at[:, rows], og_out.at[0, :, rows], piece_sem.at[r, 2])] + [
            pltpu.make_async_copy(sino.at[spans[c]], sino_out.at[spans[c]], piece_sem.at[r, c])
            for c in range(2)
        ]

    def interior(r, carry):
        rows = pl.ds(pl.multiple_of(r * RIM, RIM), RIM)
        for c in range(2):
            for b in range(4):
                og[c, rows, b * BLK : (b + 1) * BLK] = cells_at(c, r + 1, b + 1)
            for b in range(5):
                sino[pl.ds(pl.multiple_of(c * TILE + r * RIM, RIM), RIM), b * BLK : (b + 1) * BLK] = cells_at(
                    c, r + 1, b + ox
                ).astype(BF)
        for copy in finished(r):
            copy.start()
        return carry

    lax.fori_loop(0, 8, interior, 0)

    for m in range(2):
        real, imag = (
            patch[0, 0] * chi[0, m, :, a] + sign * patch[0, 1] * chi[0, m, :, b]
            + patch[1, 0] * chi[1, m, :, a] + sign * patch[1, 1] * chi[1, m, :, b]
            for a, b, sign in ((slice(0, PATCH), slice(PATCH, 512), 1.0), (slice(PATCH, 512), slice(0, PATCH), -1.0))
        )
        for q, terms in ((2 * m, real), (2 * m + 1, imag)):
            part[0, q] = terms[0:BLK].astype(BF)
            part[1, SECOND[q]] = terms[BLK:].astype(BF)
    outs[3].start()

    def settle(r, carry):
        for copy in finished(r):
            copy.wait()
        return carry

    lax.fori_loop(0, 8, settle, 0)
    for copy in outs:
        copy.wait()
    over_copy.wait()


def regroup_kernel(
    angles,
    sino_ref, row_ref, col_ref, cor_ref, part_ref, ramp_ref, bv_ref,
    got_row, got_col, got_cor, total_out, inbox_out,
    sino, part, ramp, bv, part_got, part_sum, quarter_send, quarter_got, total,
    lines, over_send, over_got, msgs, inbox,
    load_sem, rim_send, rim_recv, part_ssem, part_rsem, over_ssem, over_rsem,
    word_sem, a2a_send, a2a_recv, own_sem, out_sem,
):
    ang, sy, sx = lax.axis_index("ang"), lax.axis_index("sy"), lax.axis_index("sx")
    oy, ox = 1 - sy, 1 - sx
    group = 2 * angles
    me = ang * 2 + sx

    barrier = pltpu.get_barrier_semaphore()
    line, place = ang >> 4, ang & 15
    spot = line * 2 + sx
    crosswise = []
    for k in range(1, group // 16):
        d = jnp.bitwise_xor(spot, k)
        crosswise.append(((d >> 1) * 16 + place, sy, d & 1))
    lengthwise = [(line * 16 + ((place + k) & 15), sy, sx) for k in range(1, 16)]
    greeted = [(ang, oy, sx), (ang, oy, ox)] + crosswise + lengthwise
    for dev in greeted:
        pl.semaphore_signal(barrier, inc=1, device_id=dev, device_id_type=MESH)
    across, beside = (ang, oy, ox), (ang, sy, ox)
    kind = jnp.bitwise_xor(sy, sx)
    routes = (
        (across, beside, 2 * sy, 2 * oy, sx, ox),
        (beside, across, 2 * kind, 2 * (1 - kind), sy, oy),
    )
    loads = [
        pltpu.make_async_copy(src, dst, load_sem.at[i])
        for i, (src, dst) in enumerate(
            [(sino_ref, sino), (ramp_ref, ramp), (bv_ref, bv)]
            + [(part_ref.at[h, pl.ds(routes[h][2], 2)], part.at[h]) for h in range(2)]
        )
    ]
    for copy in loads:
        copy.start()
    pl.semaphore_wait(barrier, len(greeted))

    for dev in crosswise:
        pl.semaphore_signal(word_sem, inc=1, device_id=dev, device_id_type=MESH)

    def exchange(step, h, src, dst, dev):
        return pltpu.make_async_remote_copy(
            src_ref=src, dst_ref=dst, send_sem=part_ssem.at[step, h], recv_sem=part_rsem.at[step, h],
            device_id=dev, device_id_type=MESH,
        )

    firsts = [
        exchange(0, h, part_ref.at[h, pl.ds(routes[h][3], 2)], part_got.at[h], routes[h][0])
        for h in range(2)
    ]
    for copy in firsts:
        copy.start()
    for copy in loads:
        copy.wait()

    for s in range(2):
        filtered = jnp.dot(sino[...], ramp[s], preferred_element_type=F32).astype(BF)
        lines[s] = jnp.dot(filtered, bv[s], preferred_element_type=F32)
        for c in range(2):
            over_send[s, c] = lines[s, 2 * TILE + c * RIM : 2 * TILE + (c + 1) * RIM, :].astype(BF)
    over = pltpu.make_async_remote_copy(
        src_ref=over_send, dst_ref=over_got, send_sem=over_ssem, recv_sem=over_rsem,
        device_id=(ang, oy, sx), device_id_type=MESH,
    )
    over.start()
    top = lax.broadcasted_iota(jnp.int32, (64, 8, BLK), 1) < 4
    for s in range(2):
        a = lines[s, 0:TILE, :].reshape(64, 8, BLK)
        b = lines[s, TILE : 2 * TILE, :].reshape(64, 8, BLK)
        lanes = slice(s * BLK, (s + 1) * BLK)
        msgs[:, 0, :, lanes] = jnp.where(top, a, pltpu.roll(b, 4, 1)).astype(BF)
        msgs[:, 1, :, lanes] = jnp.where(top, pltpu.roll(a, 4, 1), b).astype(BF)

    def send_to(d):
        @pl.when(d != me)
        def _():
            pltpu.make_async_remote_copy(
                src_ref=msgs.at[d >> 1, d & 1], dst_ref=inbox.at[me],
                send_sem=a2a_send, recv_sem=a2a_recv,
                device_id=(d >> 1, sy, d & 1), device_id_type=MESH,
            ).start()

    inner = group - 16

    def send_inner(k, carry):
        send_to(16 * sy + lax.rem(me + k, inner))
        return carry

    def send_edge(k, carry):
        send_to(inner * oy + ((me + k) & 15))
        return carry

    pl.semaphore_wait(word_sem, len(crosswise))
    lax.fori_loop(0, inner // 2, send_inner, 0)
    seconds = []
    for h, (_, after, _, _, keep, give) in enumerate(routes):
        firsts[h].wait()
        part_sum[h] = part[h].astype(F32) + part_got[h].astype(F32)
        quarter_send[h] = part_sum[h, give].astype(BF)
        seconds.append(exchange(1, h, quarter_send.at[h], quarter_got.at[h], after))
        seconds[h].start()
    lax.fori_loop(inner // 2, inner, send_inner, 0)
    rims = [
        pltpu.make_async_remote_copy(
            src_ref=src, dst_ref=dst, send_sem=rim_send.at[i], recv_sem=rim_recv.at[i],
            device_id=dev, device_id_type=MESH,
        )
        for i, (src, dst, dev) in enumerate(
            [
                (row_ref, got_row, (ang, oy, sx)),
                (col_ref, got_col, beside),
                (cor_ref, got_cor, across),
            ]
        )
    ]
    rims[0].start()
    over.wait()
    edge = pl.ds(pl.multiple_of((TILE - RIM) * oy, RIM), RIM)
    edge_low = pl.ds(pl.multiple_of(TILE + (TILE - RIM) * oy, RIM), RIM)
    pairs = pl.ds(56 * oy, 8)
    for s in range(2):
        a = (lines[s, edge, :] + over_got[s, 0].astype(F32)).reshape(8, 8, BLK)
        b = (lines[s, edge_low, :] + over_got[s, 1].astype(F32)).reshape(8, 8, BLK)
        lanes = slice(s * BLK, (s + 1) * BLK)
        msgs[pairs, 0, :, lanes] = jnp.where(top[0:8], a, pltpu.roll(b, 4, 1)).astype(BF)
        msgs[pairs, 1, :, lanes] = jnp.where(top[0:8], pltpu.roll(a, 4, 1), b).astype(BF)
    lax.fori_loop(0, 16, send_edge, 0)
    own = pltpu.make_async_copy(msgs.at[ang, sx], inbox.at[me], own_sem)
    own.start()

    thirds = []
    for h, (_, after, base, _, keep, _) in enumerate(routes):
        seconds[h].wait()
        at = total.at[h, base + keep]
        total[h, base + keep] = (part_sum[h, keep] + quarter_got[h].astype(F32)).astype(BF)
        thirds.append(exchange(2, h, at, at, after))
        thirds[h].start()
    rims[1].start()
    rims[2].start()
    fourths = []
    for h, (before, _, base, _, _, _) in enumerate(routes):
        thirds[h].wait()
        at = total.at[h, pl.ds(base, 2)]
        fourths.append(exchange(3, h, at, at, before))
        fourths[h].start()
    own.wait()
    pltpu.make_async_copy(
        inbox.at[pl.ds(0, group - 1)], inbox.at[pl.ds(0, group - 1)], a2a_recv
    ).wait()
    inbox_copy = pltpu.make_async_copy(inbox, inbox_out, out_sem.at[0])
    inbox_copy.start()
    for copy in fourths:
        copy.wait()
    total_copy = pltpu.make_async_copy(total, total_out, out_sem.at[1])
    total_copy.start()
    pltpu.make_async_copy(
        inbox.at[pl.ds(0, group - 1)], inbox.at[pl.ds(0, group - 1)], a2a_send
    ).wait()
    for copy in rims:
        copy.wait()
    inbox_copy.wait()
    total_copy.wait()


def finish_kernel(
    angles, bi_ref, og_ref, row_ref, col_ref, cor_ref, total_ref, inbox_ref, og_out, pg_out, vol_out,
    og_row, og_col, row, col, cor, total, pg, inbox, vol, seen, in_sem, out_sem,
):
    sy, sx = lax.axis_index("sy"), lax.axis_index("sx")
    oy, ox = 1 - sy, 1 - sx
    row_at = pl.ds(pl.multiple_of((TILE - RIM) * oy, RIM), RIM)
    col_at = pl.ds(pl.multiple_of((TILE - BLK) * ox, BLK), BLK)
    rest_at = pl.ds(pl.multiple_of(BLK * sx, BLK), TILE - BLK)
    loads = [
        pltpu.make_async_copy(src, dst, in_sem.at[i])
        for i, (src, dst) in enumerate(
            [
                (og_ref.at[0, :, row_at, rest_at], og_row), (og_ref.at[0, :, :, col_at], og_col),
                (row_ref, row), (col_ref, col), (cor_ref, cor), (total_ref, total), (inbox_ref, inbox),
            ]
        )
    ]
    for copy in loads:
        copy.start()
    summed, arrived = loads[5:]
    for a in range(angles):
        seen[a] = 0
    summed.wait()
    for q in range(4):
        pg[0, q // 2, q % 2, 0:BLK, :] = total[0, q].astype(F32) * (1.0 / math.sqrt(8.0))
        pg[0, q // 2, q % 2, BLK:, :] = total[1, SECOND[q]].astype(F32) * (1.0 / math.sqrt(8.0))
    pg_copy = pltpu.make_async_copy(pg, pg_out, out_sem.at[0])
    pg_copy.start()
    for copy in loads[0:5]:
        copy.wait()
    for got, at in ((col, pl.ds(0, TILE)), (cor, row_at)):
        wide = got[...].astype(F32)
        turned = swap_halves(wide)
        low = lax.broadcasted_iota(jnp.int32, wide.shape, 1) < RIM
        added = (
            jnp.where(sx == 1, jnp.where(low, wide, 0.0), jnp.where(low, 0.0, turned)),
            jnp.where(sx == 1, jnp.where(low, turned, 0.0), jnp.where(low, 0.0, wide)),
        )
        for c in range(2):
            og_col[c, at, :] = og_col[c, at, :] + added[c]
    for c in range(2):
        og_row[c] = og_row[c] + row[c, :, rest_at].astype(F32)
        og_col[c, row_at, :] = og_col[c, row_at, :] + row[c, :, col_at].astype(F32)
    og_copies = [
        pltpu.make_async_copy(og_row, og_out.at[0, :, row_at, rest_at], out_sem.at[2]),
        pltpu.make_async_copy(og_col, og_out.at[0, :, :, col_at], out_sem.at[3]),
    ]
    for copy in og_copies:
        copy.start()
    arrived.wait()
    for b in range(8):
        line = jnp.zeros((8, BLK), F32)
        for k in range(16):
            source = bi_ref[b, k] >> 3
            slot = seen[source]
            seen[source] = 1
            lane = pl.multiple_of(slot * BLK, BLK)
            for h in range(2):
                line = line + inbox[source * 2 + h, :, pl.ds(lane, BLK)].astype(F32)
        for c in range(2):
            for r in range(4):
                vol[0, r, c, b * BLK : (b + 1) * BLK] = line[c * 4 + r]
    vol_copy = pltpu.make_async_copy(vol, vol_out, out_sem.at[1])
    vol_copy.start()
    for copy in og_copies:
        copy.wait()
    pg_copy.wait()
    vol_copy.wait()


def body(angles, tables, objects, probe, data, positions, block_index, block_values):
    forward, backward, ramp = (jnp.asarray(t) for t in tables)
    group = 2 * angles
    dma = pltpu.SemaphoreType.DMA
    smem = pl.BlockSpec(memory_space=pltpu.SMEM)
    hbm = pl.BlockSpec(memory_space=pltpu.HBM)

    def shape(dims, kind):
        return jax.ShapeDtypeStruct(dims, kind)

    rim_shapes = (shape((2, RIM, TILE), BF), shape((TILE, BLK), BF), shape((RIM, BLK), BF))
    halos = pl.pallas_call(
        strips_kernel,
        out_shape=rim_shapes,
        in_specs=[hbm],
        out_specs=[hbm] * 3,
        scratch_shapes=[
            pltpu.VMEM((2, TILE, BLK), BF), pltpu.VMEM((TILE, BLK), BF), dma, dma((3,)), dma((3,)),
        ],
        compiler_params=pltpu.CompilerParams(
            collective_id=0, has_side_effects=True, vmem_limit_bytes=62 * 1024 * 1024
        ),
    )(objects)
    og_part, row, col, cor, parts, ramp_two, bv_two, sino = pl.pallas_call(
        functools.partial(patch_kernel, angles),
        out_shape=(shape((1, 2, TILE, TILE), F32),) + rim_shapes + (
            shape((2, 4, BLK, PATCH), BF), shape((2, SPAN, BLK), BF), shape((2, BLK, BLK), BF),
            shape((2 * ROWS - 2 * RIM, SPAN), BF),
        ),
        in_specs=[smem] * 2 + [hbm] * 10,
        out_specs=[hbm] * 8,
        scratch_shapes=[
            pltpu.VMEM((2, ROWS, COLS), BF),
            pltpu.VMEM((ROWS, BLK), BF),
            pltpu.VMEM((2, 2, PATCH, PATCH), F32),
            pltpu.VMEM((2, PATCH, PATCH), BF),
            pltpu.VMEM((512, 512), BF),
            pltpu.VMEM((512, 512), BF),
            pltpu.VMEM((2, SPAN, BLK), BF),
            pltpu.VMEM((2, BLK, BLK), BF),
            pltpu.VMEM((2, 2, 272, BLK), F32),
            pltpu.VMEM((2, 2, PATCH, PATCH), F32),
            pltpu.VMEM((2, 512, PATCH), BF),
            pltpu.VMEM((2, PATCH, 512), BF),
            pltpu.VMEM((2, PATCH, 512), F32),
            pltpu.VMEM((2, 2, PATCH, 512), F32),
            pltpu.VMEM((4, 5, 384, BLK), F32),
            pltpu.VMEM((2, TILE, TILE), F32),
            pltpu.VMEM((2, RIM, TILE), BF),
            pltpu.VMEM((TILE, BLK), BF),
            pltpu.VMEM((RIM, BLK), BF),
            pltpu.VMEM((2, 4, BLK, PATCH), BF),
            pltpu.VMEM((2 * ROWS - 2 * RIM, SPAN), BF),
            dma((8,)), dma((4,)), dma((7,)), dma((8, 3)),
        ],
        compiler_params=pltpu.CompilerParams(vmem_limit_bytes=62 * 1024 * 1024),
    )(positions, block_index, objects, *halos, probe, data, forward, backward, ramp, block_values)
    got_row, got_col, got_cor, total, inbox = pl.pallas_call(
        functools.partial(regroup_kernel, angles),
        out_shape=rim_shapes + (shape((2, 4, BLK, PATCH), BF), shape((group, 8, 2 * BLK), BF)),
        in_specs=[hbm] * 7,
        out_specs=[hbm] * 5,
        scratch_shapes=[
            pltpu.VMEM((2 * ROWS - 2 * RIM, SPAN), BF),
            pltpu.VMEM((2, 2, BLK, PATCH), BF),
            pltpu.VMEM((2, SPAN, BLK), BF),
            pltpu.VMEM((2, BLK, BLK), BF),
            pltpu.VMEM((2, 2, BLK, PATCH), BF),
            pltpu.VMEM((2, 2, BLK, PATCH), F32),
            pltpu.VMEM((2, BLK, PATCH), BF),
            pltpu.VMEM((2, BLK, PATCH), BF),
            pltpu.VMEM((2, 4, BLK, PATCH), BF),
            pltpu.VMEM((2, 2 * ROWS - 2 * RIM, BLK), F32),
            pltpu.VMEM((2, 2, RIM, BLK), BF),
            pltpu.VMEM((2, 2, RIM, BLK), BF),
            pltpu.VMEM((group // 2, 2, 8, 2 * BLK), BF),
            pltpu.VMEM((group, 8, 2 * BLK), BF),
            dma((5,)), dma((3,)), dma((3,)), dma((4, 2)), dma((4, 2)), dma, dma,
            pltpu.SemaphoreType.REGULAR, dma, dma, dma, dma((2,)),
        ],
        compiler_params=pltpu.CompilerParams(
            collective_id=1, has_side_effects=True, vmem_limit_bytes=62 * 1024 * 1024
        ),
    )(sino, row, col, cor, parts, ramp_two, bv_two)
    return pl.pallas_call(
        functools.partial(finish_kernel, angles),
        out_shape=(
            shape((1, 2, TILE, TILE), F32), shape((1, 2, 2, PATCH, PATCH), F32), shape((1, 4, 2, 1024), F32),
        ),
        in_specs=[smem] + [hbm] * 6,
        out_specs=[hbm] * 3,
        scratch_shapes=[
            pltpu.VMEM((2, RIM, TILE - BLK), F32),
            pltpu.VMEM((2, TILE, BLK), F32),
            pltpu.VMEM((2, RIM, TILE), BF),
            pltpu.VMEM((TILE, BLK), BF),
            pltpu.VMEM((RIM, BLK), BF),
            pltpu.VMEM((2, 4, BLK, PATCH), BF),
            pltpu.VMEM((1, 2, 2, PATCH, PATCH), F32),
            pltpu.VMEM((group, 8, 2 * BLK), BF),
            pltpu.VMEM((1, 4, 2, 1024), F32),
            pltpu.SMEM((angles,), jnp.int32),
            dma((7,)), dma((4,)),
        ],
        input_output_aliases={1: 0},
        compiler_params=pltpu.CompilerParams(vmem_limit_bytes=62 * 1024 * 1024),
    )(block_index, og_part, got_row, got_col, got_cor, total, inbox)


def solution(mesh):
    tables = dft_tables() + (ramp_blocks(8),)
    return jax.shard_map(
        functools.partial(body, mesh.shape["ang"], tables),
        mesh=mesh,
        in_specs=(
            P("ang", None, "sy", "sx"),
            P(),
            P("ang", "sy", "sx", None, None, None),
            P("ang", "sy", "sx", None, None),
            P(),
            P(),
        ),
        out_specs=(
            P("ang", None, "sy", "sx"),
            P("ang", None, None, None, None),
            P("sy", ("ang", "sx"), None, None),
        ),
        check_vma=False,
    )
```

```python
import functools
import math

import jax
import jax.numpy as jnp
import numpy as np
from jax import lax
from jax.experimental import pallas as pl
from jax.experimental.pallas import tpu as pltpu
from jax.sharding import PartitionSpec as P

PATCH = 256
RIM = 64
BLK = 128
TILE = 512
ROWS = 640
SPAN = 640
COLS = 768
SECOND = (0, 2, 3, 1)
MESH = pl.DeviceIdType.MESH
BF = jnp.bfloat16
F32 = jnp.float32


def dft_tables():
    ids = np.arange(PATCH)
    phases = (np.outer(ids, ids) % PATCH).astype(np.float64) * (2.0 * math.pi / PATCH)
    factor = 1.0 / math.sqrt(PATCH)
    real = (np.cos(phases) * factor).astype(np.float32)
    imag = (-np.sin(phases) * factor).astype(np.float32)
    forward = np.block([[real, -imag], [imag, real]])
    backward = np.block([[real, imag], [-imag, real]])
    return forward.astype(BF), backward.astype(BF)


def ramp_blocks(line_blocks):
    x = np.arange((2 * line_blocks - 1) * BLK)
    n = np.arange(BLK)[None, :] - (x - (line_blocks - 1) * BLK)[:, None]
    odd = n % 2 != 0
    scaled = n.astype(np.float32) * np.float32(math.pi)
    values = np.where(odd, -1.0 / np.maximum(scaled * scaled, 1.0), 0.0)
    values = np.where(n == 0, 0.25, values).astype(np.float32)
    return values.astype(BF)


def swap_halves(cells):
    return pltpu.roll(cells, BLK // 2, cells.ndim - 1)


def strips_kernel(
    obj_ref, row_out, col_out, cor_out, block, packed, load_sem, send_sem, recv_sem,
):
    ang, sy, sx = lax.axis_index("ang"), lax.axis_index("sy"), lax.axis_index("sx")
    oy, ox = 1 - sy, 1 - sx
    devices = [(ang, oy, sx), (ang, sy, ox), (ang, oy, ox)]
    rows = pl.ds(pl.multiple_of((TILE - RIM) * oy, RIM), RIM)
    cols = pl.ds(pl.multiple_of((TILE - BLK) * ox, BLK), BLK)
    load = pltpu.make_async_copy(obj_ref.at[0, :, :, cols], block, load_sem)
    load.start()
    barrier = pltpu.get_barrier_semaphore()
    for dev in devices:
        pl.semaphore_signal(barrier, inc=1, device_id=dev, device_id_type=MESH)
    load.wait()
    real, imag = block[0].astype(F32), block[1].astype(F32)
    low = lax.broadcasted_iota(jnp.int32, (TILE, BLK), 1) < RIM
    packed[...] = jnp.where(
        low, jnp.where(sx == 0, swap_halves(real), real), jnp.where(sx == 0, imag, swap_halves(imag))
    ).astype(BF)
    pl.semaphore_wait(barrier, 3)
    sources = [obj_ref.at[0, :, rows, :], packed, packed.at[rows]]
    copies = [
        pltpu.make_async_remote_copy(
            src_ref=src, dst_ref=dst, send_sem=send_sem.at[i], recv_sem=recv_sem.at[i],
            device_id=dev, device_id_type=MESH,
        )
        for i, (src, dst, dev) in enumerate(zip(sources, (row_out, col_out, cor_out), devices))
    ]
    for copy in copies:
        copy.start()
    for copy in copies:
        copy.wait()


def patch_kernel(
    angles,
    pos_ref, bi_ref,
    obj_ref, halo_row, halo_col, halo_cor, probe_ref, data_ref, fwd_ref, bwd_ref, ramp_ref, bv_ref,
    og_out, row_out, col_out, cor_out, part_out, ramp_out, bv_out, sino_out,
    big, side, probe, data, fwd, bwd, ramp, bv,
    win, patch, exits, half, far, chi, placed, og,
    rim_row, rim_col, rim_cor, part, sino,
    load_sem, pick_sem, out_sem, piece_sem,
):
    ang, sy, sx = lax.axis_index("ang"), lax.axis_index("sy"), lax.axis_index("sx")
    oy, ox = 1 - sy, 1 - sx
    dst_row = pl.ds(pl.multiple_of((ROWS - RIM) * oy, RIM), RIM)
    dst_col = pl.ds(pl.multiple_of((COLS - BLK) * ox, BLK), BLK)
    loads = [
        pltpu.make_async_copy(src, dst, load_sem.at[i])
        for i, (src, dst) in enumerate(
            [
                (obj_ref.at[0], big.at[:, pl.ds(RIM, TILE), pl.ds(BLK, TILE)]),
                (halo_row, big.at[:, dst_row, pl.ds(BLK, TILE)]),
                (halo_col, side.at[pl.ds(RIM, TILE)]),
                (halo_cor, side.at[dst_row]),
                (probe_ref, probe),
                (fwd_ref, fwd),
                (bwd_ref, bwd),
                (data_ref.at[0, 0, 0], data),
            ]
        )
    ]
    for copy in loads:
        copy.start()

    big[:, pl.ds(pl.multiple_of((ROWS - RIM) * sy, RIM), RIM), :] = jnp.zeros((2, RIM, COLS), BF)
    big[:, :, pl.ds(pl.multiple_of((COLS - BLK) * sx, BLK), BLK)] = jnp.zeros((2, ROWS, BLK), BF)
    for q in range(4):
        placed[q, :, 0:RIM, :] = jnp.zeros((5, RIM, BLK), F32)
        placed[q, :, RIM + PATCH :, :] = jnp.zeros((5, RIM, BLK), F32)
        placed[q, 0, RIM : RIM + PATCH, :] = jnp.zeros((PATCH, BLK), F32)
        placed[q, 4, RIM : RIM + PATCH, :] = jnp.zeros((PATCH, BLK), F32)

    named = [(jnp.int32(-1), jnp.int32(0)), (jnp.int32(0), jnp.int32(0))]
    for j in range(2 * angles):
        entry = bi_ref[j // 16, j % 16]
        mine = (entry >> 3) == ang
        early = jnp.logical_and(mine, named[0][0] < 0)
        named = [
            (jnp.where(take, j, at), jnp.where(take, entry & 7, column))
            for take, (at, column) in zip((early, mine), named)
        ]
    named[0] = (jnp.maximum(named[0][0], 0), named[0][1])
    picks = []
    for s, (entry, column) in enumerate(named):
        at = pl.multiple_of((7 - column + 3 * sx) * BLK, BLK)
        picks.append(
            pltpu.make_async_copy(ramp_ref.at[pl.ds(at, SPAN), :], ramp.at[s], pick_sem.at[2 * s])
        )
        picks.append(
            pltpu.make_async_copy(bv_ref.at[entry >> 4, entry & 15], bv.at[s], pick_sem.at[2 * s + 1])
        )
    for copy in picks:
        copy.start()
    side[pl.ds(pl.multiple_of((ROWS - RIM) * sy, RIM), RIM), :] = jnp.zeros((RIM, BLK), BF)
    for copy in loads[0:4]:
        copy.wait()
    wide = side[...].astype(F32)
    turned = swap_halves(wide)
    big[0, :, dst_col] = jnp.where(sx == 1, turned, wide).astype(BF)
    big[1, :, dst_col] = jnp.where(sx == 1, wide, turned).astype(BF)

    def corner(p):
        return pos_ref[0, 0, 0, p, 0], pos_ref[0, 0, 0, p, 1] + RIM

    def forward_patch(p, carry):
        u, v = corner(p)
        base = jnp.minimum(u >> 4, 23) * 16
        lead = u - base
        block, shift = v >> 7, v & (BLK - 1)
        across = lax.broadcasted_iota(jnp.int32, (384, PATCH), 0)
        pick = jnp.where(
            across == lax.broadcasted_iota(jnp.int32, (384, PATCH), 1) + shift, 1.0, 0.0
        ).astype(BF)
        for c in range(2):
            cells = big[
                c, pl.ds(pl.multiple_of(base, 16), 272), pl.ds(pl.multiple_of(block * BLK, BLK), 384)
            ]
            cells = jnp.dot(cells, pick, preferred_element_type=F32)
            for b in range(2):
                win[c, b] = cells[:, b * BLK : (b + 1) * BLK]
        for c in range(2):
            for b in range(2):
                patch[p, c, :, b * BLK : (b + 1) * BLK] = win[c, b, pl.ds(lead, PATCH), :]
        @pl.when(p == 0)
        def _():
            loads[4].wait()

        for m in range(2):
            exits[m, 0:PATCH] = (probe[m, 0] * patch[p, 0] - probe[m, 1] * patch[p, 1]).astype(BF)
            exits[m, PATCH:] = (probe[m, 0] * patch[p, 1] + probe[m, 1] * patch[p, 0]).astype(BF)
        @pl.when(p == 0)
        def _():
            loads[5].wait()

        for m in range(2):
            done = jnp.dot(fwd[...], exits[m], preferred_element_type=F32)
            half[m, :, 0:PATCH] = done[0:PATCH].astype(BF)
            half[m, :, PATCH:] = done[PATCH:].astype(BF)
        @pl.when(p == 0)
        def _():
            loads[6].wait()

        @pl.when(p == 0)
        def _():
            loads[7].wait()

        for m in range(2):
            far[m] = jnp.dot(half[m], bwd[...], preferred_element_type=F32)
        misfit = (
            far[0, :, 0:PATCH] * far[0, :, 0:PATCH]
            + far[0, :, PATCH:] * far[0, :, PATCH:]
            + far[1, :, 0:PATCH] * far[1, :, 0:PATCH]
            + far[1, :, PATCH:] * far[1, :, PATCH:]
            - data[p].astype(F32)
        )
        for m in range(2):
            exits[m, 0:PATCH] = (misfit * far[m, :, 0:PATCH]).astype(BF)
            exits[m, PATCH:] = (misfit * far[m, :, PATCH:]).astype(BF)
        for m in range(2):
            done = jnp.dot(bwd[...], exits[m], preferred_element_type=F32)
            half[m, :, 0:PATCH] = done[0:PATCH].astype(BF)
            half[m, :, PATCH:] = done[PATCH:].astype(BF)
        for m in range(2):
            chi[p, m] = jnp.dot(half[m], fwd[...], preferred_element_type=F32)
        cr = [chi[p, m, :, 0:PATCH] for m in range(2)]
        ci = [chi[p, m, :, PATCH:] for m in range(2)]
        grad = [
            probe[0, 0] * cr[0] + probe[0, 1] * ci[0] + probe[1, 0] * cr[1] + probe[1, 1] * ci[1],
            probe[0, 0] * ci[0] - probe[0, 1] * cr[0] + probe[1, 0] * ci[1] - probe[1, 1] * cr[1],
        ]
        spots = lax.broadcasted_iota(jnp.int32, (PATCH, 384), 1)
        put = jnp.where(
            spots == lax.broadcasted_iota(jnp.int32, (PATCH, 384), 0) + shift, 1.0, 0.0
        ).astype(BF)
        for c in range(2):
            high = grad[c].astype(BF)
            low = (grad[c] - high.astype(F32)).astype(BF)
            moved = jnp.dot(high, put, preferred_element_type=F32) + jnp.dot(
                low, put, preferred_element_type=F32
            )
            for b in range(3):
                placed[p * 2 + c, b + 1, RIM : RIM + PATCH, :] = moved[:, b * BLK : (b + 1) * BLK]
        return carry

    lax.fori_loop(0, 2, forward_patch, 0)

    def cells_at(c, row_chunk, lane_block):
        total_cells = None
        for p in range(2):
            u, v = corner(p)
            row = jnp.minimum(jnp.maximum(row_chunk * RIM - u + RIM, 0), PATCH + RIM)
            lane = jnp.minimum(jnp.maximum(lane_block - (v >> 7), -1), 3) + 1
            term = placed[p * 2 + c, lane, pl.ds(row, RIM), :]
            total_cells = term if total_cells is None else total_cells + term
        return total_cells

    rim_chunk = 9 * oy
    rim_block = 5 * ox
    for c in range(2):
        for b in range(4):
            rim_row[c, :, b * BLK : (b + 1) * BLK] = cells_at(c, rim_chunk, b + 1).astype(BF)

    def packed_rim(row_chunk):
        real, imag = (cells_at(c, row_chunk, rim_block) for c in range(2))
        kept, moved = jnp.where(sx == 0, real, imag), jnp.where(sx == 0, imag, real)
        return (kept + swap_halves(moved)).astype(BF)

    rim_cor[...] = packed_rim(rim_chunk)

    def rim_columns(r, carry):
        rim_col[pl.ds(pl.multiple_of(r * RIM, RIM), RIM), :] = packed_rim(r + 1)
        return carry

    lax.fori_loop(0, 8, rim_columns, 0)
    outs = [
        pltpu.make_async_copy(src, dst, out_sem.at[i])
        for i, (src, dst) in enumerate(
            [
                (rim_row, row_out), (rim_col, col_out), (rim_cor, cor_out),
                (part, part_out), (ramp, ramp_out), (bv, bv_out),
            ]
        )
    ]
    for copy in outs[:3]:
        copy.start()
    for copy in picks:
        copy.wait()
    for copy in outs[4:6]:
        copy.start()

    for c in range(2):
        for b in range(5):
            sino[2 * TILE + c * RIM : 2 * TILE + (c + 1) * RIM, b * BLK : (b + 1) * BLK] = cells_at(
                c, rim_chunk, b + ox
            ).astype(BF)

    over_rows = pl.ds(2 * TILE, 2 * RIM)
    over_copy = pltpu.make_async_copy(sino.at[over_rows], sino_out.at[over_rows], out_sem.at[6])
    over_copy.start()

    def finished(r):
        rows = pl.ds(pl.multiple_of(r * RIM, RIM), RIM)
        spans = [pl.ds(pl.multiple_of(c * TILE + r * RIM, RIM), RIM) for c in range(2)]
        return [pltpu.make_async_copy(og.at[:, rows], og_out.at[0, :, rows], piece_sem.at[r, 2])] + [
            pltpu.make_async_copy(sino.at[spans[c]], sino_out.at[spans[c]], piece_sem.at[r, c])
            for c in range(2)
        ]

    def interior(r, carry):
        rows = pl.ds(pl.multiple_of(r * RIM, RIM), RIM)
        for c in range(2):
            for b in range(4):
                og[c, rows, b * BLK : (b + 1) * BLK] = cells_at(c, r + 1, b + 1)
            for b in range(5):
                sino[pl.ds(pl.multiple_of(c * TILE + r * RIM, RIM), RIM), b * BLK : (b + 1) * BLK] = cells_at(
                    c, r + 1, b + ox
                ).astype(BF)
        for copy in finished(r):
            copy.start()
        return carry

    lax.fori_loop(0, 8, interior, 0)

    for m in range(2):
        real, imag = (
            patch[0, 0] * chi[0, m, :, a] + sign * patch[0, 1] * chi[0, m, :, b]
            + patch[1, 0] * chi[1, m, :, a] + sign * patch[1, 1] * chi[1, m, :, b]
            for a, b, sign in ((slice(0, PATCH), slice(PATCH, 512), 1.0), (slice(PATCH, 512), slice(0, PATCH), -1.0))
        )
        for q, terms in ((2 * m, real), (2 * m + 1, imag)):
            part[0, q] = terms[0:BLK].astype(BF)
            part[1, SECOND[q]] = terms[BLK:].astype(BF)
    outs[3].start()

    def settle(r, carry):
        for copy in finished(r):
            copy.wait()
        return carry

    lax.fori_loop(0, 8, settle, 0)
    for copy in outs:
        copy.wait()
    over_copy.wait()


def regroup_kernel(
    angles,
    sino_ref, row_ref, col_ref, cor_ref, part_ref, ramp_ref, bv_ref,
    got_row, got_col, got_cor, total_out, inbox_out,
    sino, part, ramp, bv, part_got, part_sum, quarter_send, quarter_got, total,
    lines, over_send, over_got, msgs,
    load_sem, rim_send, rim_recv, part_ssem, part_rsem, over_ssem, over_rsem,
    word_sem, a2a_send, a2a_recv, own_sem, out_sem,
):
    ang, sy, sx = lax.axis_index("ang"), lax.axis_index("sy"), lax.axis_index("sx")
    oy, ox = 1 - sy, 1 - sx
    group = 2 * angles
    me = ang * 2 + sx

    barrier = pltpu.get_barrier_semaphore()
    line, place = ang >> 4, ang & 15
    spot = line * 2 + sx
    crosswise = []
    for k in range(1, group // 16):
        d = jnp.bitwise_xor(spot, k)
        crosswise.append(((d >> 1) * 16 + place, sy, d & 1))
    lengthwise = [(line * 16 + ((place + k) & 15), sy, sx) for k in range(1, 16)]
    greeted = [(ang, oy, sx), (ang, oy, ox)] + crosswise + lengthwise
    for dev in greeted:
        pl.semaphore_signal(barrier, inc=1, device_id=dev, device_id_type=MESH)
    across, beside = (ang, oy, ox), (ang, sy, ox)
    kind = jnp.bitwise_xor(sy, sx)
    routes = (
        (across, beside, 2 * sy, 2 * oy, sx, ox),
        (beside, across, 2 * kind, 2 * (1 - kind), sy, oy),
    )
    loads = [
        pltpu.make_async_copy(src, dst, load_sem.at[i])
        for i, (src, dst) in enumerate(
            [(sino_ref, sino), (ramp_ref, ramp), (bv_ref, bv)]
            + [(part_ref.at[h, pl.ds(routes[h][2], 2)], part.at[h]) for h in range(2)]
        )
    ]
    for copy in loads:
        copy.start()
    pl.semaphore_wait(barrier, len(greeted))

    for dev in crosswise:
        pl.semaphore_signal(word_sem, inc=1, device_id=dev, device_id_type=MESH)

    def exchange(step, h, src, dst, dev):
        return pltpu.make_async_remote_copy(
            src_ref=src, dst_ref=dst, send_sem=part_ssem.at[step, h], recv_sem=part_rsem.at[step, h],
            device_id=dev, device_id_type=MESH,
        )

    firsts = [
        exchange(0, h, part_ref.at[h, pl.ds(routes[h][3], 2)], part_got.at[h], routes[h][0])
        for h in range(2)
    ]
    for copy in firsts:
        copy.start()
    for copy in loads:
        copy.wait()

    for s in range(2):
        filtered = jnp.dot(sino[...], ramp[s], preferred_element_type=F32).astype(BF)
        lines[s] = jnp.dot(filtered, bv[s], preferred_element_type=F32)
        for c in range(2):
            over_send[s, c] = lines[s, 2 * TILE + c * RIM : 2 * TILE + (c + 1) * RIM, :].astype(BF)
    over = pltpu.make_async_remote_copy(
        src_ref=over_send, dst_ref=over_got, send_sem=over_ssem, recv_sem=over_rsem,
        device_id=(ang, oy, sx), device_id_type=MESH,
    )
    over.start()
    top = lax.broadcasted_iota(jnp.int32, (64, 8, BLK), 1) < 4
    for s in range(2):
        a = lines[s, 0:TILE, :].reshape(64, 8, BLK)
        b = lines[s, TILE : 2 * TILE, :].reshape(64, 8, BLK)
        lanes = slice(s * BLK, (s + 1) * BLK)
        msgs[:, 0, :, lanes] = jnp.where(top, a, pltpu.roll(b, 4, 1)).astype(BF)
        msgs[:, 1, :, lanes] = jnp.where(top, pltpu.roll(a, 4, 1), b).astype(BF)

    def send_to(d):
        @pl.when(d != me)
        def _():
            pltpu.make_async_remote_copy(
                src_ref=msgs.at[d >> 1, d & 1], dst_ref=inbox_out.at[me],
                send_sem=a2a_send, recv_sem=a2a_recv,
                device_id=(d >> 1, sy, d & 1), device_id_type=MESH,
            ).start()

    inner = group - 16

    def send_inner(k, carry):
        send_to(16 * sy + lax.rem(me + k, inner))
        return carry

    def send_edge(k, carry):
        send_to(inner * oy + ((me + k) & 15))
        return carry

    pl.semaphore_wait(word_sem, len(crosswise))
    lax.fori_loop(0, inner // 2, send_inner, 0)
    seconds = []
    for h, (_, after, _, _, keep, give) in enumerate(routes):
        firsts[h].wait()
        part_sum[h] = part[h].astype(F32) + part_got[h].astype(F32)
        quarter_send[h] = part_sum[h, give].astype(BF)
        seconds.append(exchange(1, h, quarter_send.at[h], quarter_got.at[h], after))
        seconds[h].start()
    lax.fori_loop(inner // 2, inner, send_inner, 0)
    rims = [
        pltpu.make_async_remote_copy(
            src_ref=src, dst_ref=dst, send_sem=rim_send.at[i], recv_sem=rim_recv.at[i],
            device_id=dev, device_id_type=MESH,
        )
        for i, (src, dst, dev) in enumerate(
            [
                (row_ref, got_row, (ang, oy, sx)),
                (col_ref, got_col, beside),
                (cor_ref, got_cor, across),
            ]
        )
    ]
    rims[0].start()
    over.wait()
    edge = pl.ds(pl.multiple_of((TILE - RIM) * oy, RIM), RIM)
    edge_low = pl.ds(pl.multiple_of(TILE + (TILE - RIM) * oy, RIM), RIM)
    pairs = pl.ds(56 * oy, 8)
    for s in range(2):
        a = (lines[s, edge, :] + over_got[s, 0].astype(F32)).reshape(8, 8, BLK)
        b = (lines[s, edge_low, :] + over_got[s, 1].astype(F32)).reshape(8, 8, BLK)
        lanes = slice(s * BLK, (s + 1) * BLK)
        msgs[pairs, 0, :, lanes] = jnp.where(top[0:8], a, pltpu.roll(b, 4, 1)).astype(BF)
        msgs[pairs, 1, :, lanes] = jnp.where(top[0:8], pltpu.roll(a, 4, 1), b).astype(BF)
    lax.fori_loop(0, 16, send_edge, 0)
    own = pltpu.make_async_copy(msgs.at[ang, sx], inbox_out.at[me], own_sem)
    own.start()

    thirds = []
    for h, (_, after, base, _, keep, _) in enumerate(routes):
        seconds[h].wait()
        at = total.at[h, base + keep]
        total[h, base + keep] = (part_sum[h, keep] + quarter_got[h].astype(F32)).astype(BF)
        thirds.append(exchange(2, h, at, at, after))
        thirds[h].start()
    rims[1].start()
    rims[2].start()
    fourths, kept = [], []
    for h, (before, _, base, _, _, _) in enumerate(routes):
        thirds[h].wait()
        at = pl.ds(base, 2)
        fourths.append(exchange(3, h, total.at[h, at], total_out.at[h, at], before))
        fourths[h].start()
        kept.append(pltpu.make_async_copy(total.at[h, at], total_out.at[h, at], out_sem.at[h]))
        kept[h].start()
    own.wait()
    pltpu.make_async_copy(
        inbox_out.at[pl.ds(0, group - 1)], inbox_out.at[pl.ds(0, group - 1)], a2a_recv
    ).wait()
    for copy in fourths:
        copy.wait()
    pltpu.make_async_copy(
        inbox_out.at[pl.ds(0, group - 1)], inbox_out.at[pl.ds(0, group - 1)], a2a_send
    ).wait()
    for copy in rims:
        copy.wait()
    for copy in kept:
        copy.wait()


def finish_kernel(
    angles, bi_ref, og_ref, row_ref, col_ref, cor_ref, total_ref, inbox_ref, og_out, pg_out, vol_out,
    og_row, og_col, row, col, cor, total, pg, inbox, vol, seen, in_sem, out_sem,
):
    sy, sx = lax.axis_index("sy"), lax.axis_index("sx")
    oy, ox = 1 - sy, 1 - sx
    row_at = pl.ds(pl.multiple_of((TILE - RIM) * oy, RIM), RIM)
    col_at = pl.ds(pl.multiple_of((TILE - BLK) * ox, BLK), BLK)
    rest_at = pl.ds(pl.multiple_of(BLK * sx, BLK), TILE - BLK)
    loads = [
        pltpu.make_async_copy(src, dst, in_sem.at[i])
        for i, (src, dst) in enumerate(
            [
                (og_ref.at[0, :, row_at, rest_at], og_row), (og_ref.at[0, :, :, col_at], og_col),
                (row_ref, row), (col_ref, col), (cor_ref, cor), (total_ref, total), (inbox_ref, inbox),
            ]
        )
    ]
    for copy in loads:
        copy.start()
    summed, arrived = loads[5:]
    for a in range(angles):
        seen[a] = 0
    summed.wait()
    for q in range(4):
        pg[0, q // 2, q % 2, 0:BLK, :] = total[0, q].astype(F32) * (1.0 / math.sqrt(8.0))
        pg[0, q // 2, q % 2, BLK:, :] = total[1, SECOND[q]].astype(F32) * (1.0 / math.sqrt(8.0))
    pg_copy = pltpu.make_async_copy(pg, pg_out, out_sem.at[0])
    pg_copy.start()
    for copy in loads[0:5]:
        copy.wait()
    for got, at in ((col, pl.ds(0, TILE)), (cor, row_at)):
        wide = got[...].astype(F32)
        turned = swap_halves(wide)
        low = lax.broadcasted_iota(jnp.int32, wide.shape, 1) < RIM
        added = (
            jnp.where(sx == 1, jnp.where(low, wide, 0.0), jnp.where(low, 0.0, turned)),
            jnp.where(sx == 1, jnp.where(low, turned, 0.0), jnp.where(low, 0.0, wide)),
        )
        for c in range(2):
            og_col[c, at, :] = og_col[c, at, :] + added[c]
    for c in range(2):
        og_row[c] = og_row[c] + row[c, :, rest_at].astype(F32)
        og_col[c, row_at, :] = og_col[c, row_at, :] + row[c, :, col_at].astype(F32)
    og_copies = [
        pltpu.make_async_copy(og_row, og_out.at[0, :, row_at, rest_at], out_sem.at[2]),
        pltpu.make_async_copy(og_col, og_out.at[0, :, :, col_at], out_sem.at[3]),
    ]
    for copy in og_copies:
        copy.start()
    arrived.wait()
    for b in range(8):
        line = jnp.zeros((8, BLK), F32)
        for k in range(16):
            source = bi_ref[b, k] >> 3
            slot = seen[source]
            seen[source] = 1
            lane = pl.multiple_of(slot * BLK, BLK)
            for h in range(2):
                line = line + inbox[source * 2 + h, :, pl.ds(lane, BLK)].astype(F32)
        for c in range(2):
            for r in range(4):
                vol[0, r, c, b * BLK : (b + 1) * BLK] = line[c * 4 + r]
    vol_copy = pltpu.make_async_copy(vol, vol_out, out_sem.at[1])
    vol_copy.start()
    for copy in og_copies:
        copy.wait()
    pg_copy.wait()
    vol_copy.wait()


def body(angles, tables, objects, probe, data, positions, block_index, block_values):
    forward, backward, ramp = (jnp.asarray(t) for t in tables)
    group = 2 * angles
    dma = pltpu.SemaphoreType.DMA
    smem = pl.BlockSpec(memory_space=pltpu.SMEM)
    hbm = pl.BlockSpec(memory_space=pltpu.HBM)

    def shape(dims, kind):
        return jax.ShapeDtypeStruct(dims, kind)

    rim_shapes = (shape((2, RIM, TILE), BF), shape((TILE, BLK), BF), shape((RIM, BLK), BF))
    halos = pl.pallas_call(
        strips_kernel,
        out_shape=rim_shapes,
        in_specs=[hbm],
        out_specs=[hbm] * 3,
        scratch_shapes=[
            pltpu.VMEM((2, TILE, BLK), BF), pltpu.VMEM((TILE, BLK), BF), dma, dma((3,)), dma((3,)),
        ],
        compiler_params=pltpu.CompilerParams(
            collective_id=0, has_side_effects=True, vmem_limit_bytes=62 * 1024 * 1024
        ),
    )(objects)
    og_part, row, col, cor, parts, ramp_two, bv_two, sino = pl.pallas_call(
        functools.partial(patch_kernel, angles),
        out_shape=(shape((1, 2, TILE, TILE), F32),) + rim_shapes + (
            shape((2, 4, BLK, PATCH), BF), shape((2, SPAN, BLK), BF), shape((2, BLK, BLK), BF),
            shape((2 * ROWS - 2 * RIM, SPAN), BF),
        ),
        in_specs=[smem] * 2 + [hbm] * 10,
        out_specs=[hbm] * 8,
        scratch_shapes=[
            pltpu.VMEM((2, ROWS, COLS), BF),
            pltpu.VMEM((ROWS, BLK), BF),
            pltpu.VMEM((2, 2, PATCH, PATCH), F32),
            pltpu.VMEM((2, PATCH, PATCH), BF),
            pltpu.VMEM((512, 512), BF),
            pltpu.VMEM((512, 512), BF),
            pltpu.VMEM((2, SPAN, BLK), BF),
            pltpu.VMEM((2, BLK, BLK), BF),
            pltpu.VMEM((2, 2, 272, BLK), F32),
            pltpu.VMEM((2, 2, PATCH, PATCH), F32),
            pltpu.VMEM((2, 512, PATCH), BF),
            pltpu.VMEM((2, PATCH, 512), BF),
            pltpu.VMEM((2, PATCH, 512), F32),
            pltpu.VMEM((2, 2, PATCH, 512), F32),
            pltpu.VMEM((4, 5, 384, BLK), F32),
            pltpu.VMEM((2, TILE, TILE), F32),
            pltpu.VMEM((2, RIM, TILE), BF),
            pltpu.VMEM((TILE, BLK), BF),
            pltpu.VMEM((RIM, BLK), BF),
            pltpu.VMEM((2, 4, BLK, PATCH), BF),
            pltpu.VMEM((2 * ROWS - 2 * RIM, SPAN), BF),
            dma((8,)), dma((4,)), dma((7,)), dma((8, 3)),
        ],
        compiler_params=pltpu.CompilerParams(vmem_limit_bytes=62 * 1024 * 1024),
    )(positions, block_index, objects, *halos, probe, data, forward, backward, ramp, block_values)
    got_row, got_col, got_cor, total, inbox = pl.pallas_call(
        functools.partial(regroup_kernel, angles),
        out_shape=rim_shapes + (shape((2, 4, BLK, PATCH), BF), shape((group, 8, 2 * BLK), BF)),
        in_specs=[hbm] * 7,
        out_specs=[hbm] * 5,
        scratch_shapes=[
            pltpu.VMEM((2 * ROWS - 2 * RIM, SPAN), BF),
            pltpu.VMEM((2, 2, BLK, PATCH), BF),
            pltpu.VMEM((2, SPAN, BLK), BF),
            pltpu.VMEM((2, BLK, BLK), BF),
            pltpu.VMEM((2, 2, BLK, PATCH), BF),
            pltpu.VMEM((2, 2, BLK, PATCH), F32),
            pltpu.VMEM((2, BLK, PATCH), BF),
            pltpu.VMEM((2, BLK, PATCH), BF),
            pltpu.VMEM((2, 4, BLK, PATCH), BF),
            pltpu.VMEM((2, 2 * ROWS - 2 * RIM, BLK), F32),
            pltpu.VMEM((2, 2, RIM, BLK), BF),
            pltpu.VMEM((2, 2, RIM, BLK), BF),
            pltpu.VMEM((group // 2, 2, 8, 2 * BLK), BF),
            dma((5,)), dma((3,)), dma((3,)), dma((4, 2)), dma((4, 2)), dma, dma,
            pltpu.SemaphoreType.REGULAR, dma, dma, dma, dma((2,)),
        ],
        compiler_params=pltpu.CompilerParams(
            collective_id=1, has_side_effects=True, vmem_limit_bytes=62 * 1024 * 1024
        ),
    )(sino, row, col, cor, parts, ramp_two, bv_two)
    return pl.pallas_call(
        functools.partial(finish_kernel, angles),
        out_shape=(
            shape((1, 2, TILE, TILE), F32), shape((1, 2, 2, PATCH, PATCH), F32), shape((1, 4, 2, 1024), F32),
        ),
        in_specs=[smem] + [hbm] * 6,
        out_specs=[hbm] * 3,
        scratch_shapes=[
            pltpu.VMEM((2, RIM, TILE - BLK), F32),
            pltpu.VMEM((2, TILE, BLK), F32),
            pltpu.VMEM((2, RIM, TILE), BF),
            pltpu.VMEM((TILE, BLK), BF),
            pltpu.VMEM((RIM, BLK), BF),
            pltpu.VMEM((2, 4, BLK, PATCH), BF),
            pltpu.VMEM((1, 2, 2, PATCH, PATCH), F32),
            pltpu.VMEM((group, 8, 2 * BLK), BF),
            pltpu.VMEM((1, 4, 2, 1024), F32),
            pltpu.SMEM((angles,), jnp.int32),
            dma((7,)), dma((4,)),
        ],
        input_output_aliases={1: 0},
        compiler_params=pltpu.CompilerParams(vmem_limit_bytes=62 * 1024 * 1024),
    )(block_index, og_part, got_row, got_col, got_cor, total, inbox)


def solution(mesh):
    tables = dft_tables() + (ramp_blocks(8),)
    return jax.shard_map(
        functools.partial(body, mesh.shape["ang"], tables),
        mesh=mesh,
        in_specs=(
            P("ang", None, "sy", "sx"),
            P(),
            P("ang", "sy", "sx", None, None, None),
            P("ang", "sy", "sx", None, None),
            P(),
            P(),
        ),
        out_specs=(
            P("ang", None, "sy", "sx"),
            P("ang", None, None, None, None),
            P("sy", ("ang", "sx"), None, None),
        ),
        check_vma=False,
    )
```

```python
import functools
import math

import jax
import jax.numpy as jnp
import numpy as np
from jax import lax
from jax.experimental import pallas as pl
from jax.experimental.pallas import tpu as pltpu
from jax.sharding import PartitionSpec as P

PATCH = 256
RIM = 64
BLK = 128
TILE = 512
ROWS = 640
SPAN = 640
COLS = 768
SECOND = (0, 2, 3, 1)
MESH = pl.DeviceIdType.MESH
BF = jnp.bfloat16
F32 = jnp.float32


def dft_tables():
    ids = np.arange(PATCH)
    phases = (np.outer(ids, ids) % PATCH).astype(np.float64) * (2.0 * math.pi / PATCH)
    factor = 1.0 / math.sqrt(PATCH)
    real = (np.cos(phases) * factor).astype(np.float32)
    imag = (-np.sin(phases) * factor).astype(np.float32)
    forward = np.block([[real, -imag], [imag, real]])
    backward = np.block([[real, imag], [-imag, real]])
    return forward.astype(BF), backward.astype(BF)


def ramp_blocks(line_blocks):
    x = np.arange((2 * line_blocks - 1) * BLK)
    n = np.arange(BLK)[None, :] - (x - (line_blocks - 1) * BLK)[:, None]
    odd = n % 2 != 0
    scaled = n.astype(np.float32) * np.float32(math.pi)
    values = np.where(odd, -1.0 / np.maximum(scaled * scaled, 1.0), 0.0)
    values = np.where(n == 0, 0.25, values).astype(np.float32)
    return values.astype(BF)


def swap_halves(cells):
    return pltpu.roll(cells, BLK // 2, cells.ndim - 1)


def strips_kernel(
    obj_ref, row_out, col_out, cor_out, block, packed, load_sem, send_sem, recv_sem,
):
    ang, sy, sx = lax.axis_index("ang"), lax.axis_index("sy"), lax.axis_index("sx")
    oy, ox = 1 - sy, 1 - sx
    devices = [(ang, oy, sx), (ang, sy, ox), (ang, oy, ox)]
    rows = pl.ds(pl.multiple_of((TILE - RIM) * oy, RIM), RIM)
    cols = pl.ds(pl.multiple_of((TILE - BLK) * ox, BLK), BLK)
    load = pltpu.make_async_copy(obj_ref.at[0, :, :, cols], block, load_sem)
    load.start()
    barrier = pltpu.get_barrier_semaphore()
    for dev in devices:
        pl.semaphore_signal(barrier, inc=1, device_id=dev, device_id_type=MESH)
    pl.semaphore_wait(barrier, 3)
    sources = [obj_ref.at[0, :, rows, :], packed, packed.at[rows]]
    copies = [
        pltpu.make_async_remote_copy(
            src_ref=src, dst_ref=dst, send_sem=send_sem.at[i], recv_sem=recv_sem.at[i],
            device_id=dev, device_id_type=MESH,
        )
        for i, (src, dst, dev) in enumerate(zip(sources, (row_out, col_out, cor_out), devices))
    ]
    copies[0].start()
    load.wait()
    real, imag = block[0].astype(F32), block[1].astype(F32)
    low = lax.broadcasted_iota(jnp.int32, (TILE, BLK), 1) < RIM
    packed[...] = jnp.where(
        low, jnp.where(sx == 0, swap_halves(real), real), jnp.where(sx == 0, imag, swap_halves(imag))
    ).astype(BF)
    for copy in copies[1:]:
        copy.start()
    for copy in copies:
        copy.wait()


def patch_kernel(
    angles,
    pos_ref, bi_ref,
    obj_ref, halo_row, halo_col, halo_cor, probe_ref, data_ref, fwd_ref, bwd_ref, ramp_ref, bv_ref,
    og_out, row_out, col_out, cor_out, part_out, ramp_out, bv_out, sino_out,
    big, side, probe, data, fwd, bwd, ramp, bv,
    win, patch, exits, half, far, chi, placed, og,
    rim_row, rim_col, rim_cor, part, sino,
    load_sem, pick_sem, out_sem, piece_sem,
):
    ang, sy, sx = lax.axis_index("ang"), lax.axis_index("sy"), lax.axis_index("sx")
    oy, ox = 1 - sy, 1 - sx
    dst_row = pl.ds(pl.multiple_of((ROWS - RIM) * oy, RIM), RIM)
    dst_col = pl.ds(pl.multiple_of((COLS - BLK) * ox, BLK), BLK)
    loads = [
        pltpu.make_async_copy(src, dst, load_sem.at[i])
        for i, (src, dst) in enumerate(
            [
                (obj_ref.at[0], big.at[:, pl.ds(RIM, TILE), pl.ds(BLK, TILE)]),
                (halo_row, big.at[:, dst_row, pl.ds(BLK, TILE)]),
                (halo_col, side.at[pl.ds(RIM, TILE)]),
                (halo_cor, side.at[dst_row]),
                (probe_ref, probe),
                (fwd_ref, fwd),
                (bwd_ref, bwd),
                (data_ref.at[0, 0, 0], data),
            ]
        )
    ]
    for copy in loads:
        copy.start()

    big[:, pl.ds(pl.multiple_of((ROWS - RIM) * sy, RIM), RIM), :] = jnp.zeros((2, RIM, COLS), BF)
    big[:, :, pl.ds(pl.multiple_of((COLS - BLK) * sx, BLK), BLK)] = jnp.zeros((2, ROWS, BLK), BF)
    for q in range(4):
        placed[q, :, 0:RIM, :] = jnp.zeros((5, RIM, BLK), F32)
        placed[q, :, RIM + PATCH :, :] = jnp.zeros((5, RIM, BLK), F32)
        placed[q, 0, RIM : RIM + PATCH, :] = jnp.zeros((PATCH, BLK), F32)
        placed[q, 4, RIM : RIM + PATCH, :] = jnp.zeros((PATCH, BLK), F32)

    named = [(jnp.int32(-1), jnp.int32(0)), (jnp.int32(0), jnp.int32(0))]
    for j in range(2 * angles):
        entry = bi_ref[j // 16, j % 16]
        mine = (entry >> 3) == ang
        early = jnp.logical_and(mine, named[0][0] < 0)
        named = [
            (jnp.where(take, j, at), jnp.where(take, entry & 7, column))
            for take, (at, column) in zip((early, mine), named)
        ]
    named[0] = (jnp.maximum(named[0][0], 0), named[0][1])
    picks = []
    for s, (entry, column) in enumerate(named):
        at = pl.multiple_of((7 - column + 3 * sx) * BLK, BLK)
        picks.append(
            pltpu.make_async_copy(ramp_ref.at[pl.ds(at, SPAN), :], ramp.at[s], pick_sem.at[2 * s])
        )
        picks.append(
            pltpu.make_async_copy(bv_ref.at[entry >> 4, entry & 15], bv.at[s], pick_sem.at[2 * s + 1])
        )
    for copy in picks:
        copy.start()
    side[pl.ds(pl.multiple_of((ROWS - RIM) * sy, RIM), RIM), :] = jnp.zeros((RIM, BLK), BF)
    for copy in loads[0:4]:
        copy.wait()
    wide = side[...].astype(F32)
    turned = swap_halves(wide)
    big[0, :, dst_col] = jnp.where(sx == 1, turned, wide).astype(BF)
    big[1, :, dst_col] = jnp.where(sx == 1, wide, turned).astype(BF)

    def corner(p):
        return pos_ref[0, 0, 0, p, 0], pos_ref[0, 0, 0, p, 1] + RIM

    def forward_patch(p, carry):
        u, v = corner(p)
        base = jnp.minimum(u >> 4, 23) * 16
        lead = u - base
        block, shift = v >> 7, v & (BLK - 1)
        across = lax.broadcasted_iota(jnp.int32, (384, PATCH), 0)
        pick = jnp.where(
            across == lax.broadcasted_iota(jnp.int32, (384, PATCH), 1) + shift, 1.0, 0.0
        ).astype(BF)
        for c in range(2):
            cells = big[
                c, pl.ds(pl.multiple_of(base, 16), 272), pl.ds(pl.multiple_of(block * BLK, BLK), 384)
            ]
            cells = jnp.dot(cells, pick, preferred_element_type=F32)
            for b in range(2):
                win[c, b] = cells[:, b * BLK : (b + 1) * BLK]
        for c in range(2):
            for b in range(2):
                patch[p, c, :, b * BLK : (b + 1) * BLK] = win[c, b, pl.ds(lead, PATCH), :]
        @pl.when(p == 0)
        def _():
            loads[4].wait()

        for m in range(2):
            exits[m, 0:PATCH] = (probe[m, 0] * patch[p, 0] - probe[m, 1] * patch[p, 1]).astype(BF)
            exits[m, PATCH:] = (probe[m, 0] * patch[p, 1] + probe[m, 1] * patch[p, 0]).astype(BF)
        @pl.when(p == 0)
        def _():
            loads[5].wait()

        for m in range(2):
            done = jnp.dot(fwd[...], exits[m], preferred_element_type=F32)
            half[m, :, 0:PATCH] = done[0:PATCH].astype(BF)
            half[m, :, PATCH:] = done[PATCH:].astype(BF)
        @pl.when(p == 0)
        def _():
            loads[6].wait()

        @pl.when(p == 0)
        def _():
            loads[7].wait()

        for m in range(2):
            far[m] = jnp.dot(half[m], bwd[...], preferred_element_type=F32)
        misfit = (
            far[0, :, 0:PATCH] * far[0, :, 0:PATCH]
            + far[0, :, PATCH:] * far[0, :, PATCH:]
            + far[1, :, 0:PATCH] * far[1, :, 0:PATCH]
            + far[1, :, PATCH:] * far[1, :, PATCH:]
            - data[p].astype(F32)
        )
        for m in range(2):
            exits[m, 0:PATCH] = (misfit * far[m, :, 0:PATCH]).astype(BF)
            exits[m, PATCH:] = (misfit * far[m, :, PATCH:]).astype(BF)
        for m in range(2):
            done = jnp.dot(bwd[...], exits[m], preferred_element_type=F32)
            half[m, :, 0:PATCH] = done[0:PATCH].astype(BF)
            half[m, :, PATCH:] = done[PATCH:].astype(BF)
        for m in range(2):
            chi[p, m] = jnp.dot(half[m], fwd[...], preferred_element_type=F32)
        cr = [chi[p, m, :, 0:PATCH] for m in range(2)]
        ci = [chi[p, m, :, PATCH:] for m in range(2)]
        grad = [
            probe[0, 0] * cr[0] + probe[0, 1] * ci[0] + probe[1, 0] * cr[1] + probe[1, 1] * ci[1],
            probe[0, 0] * ci[0] - probe[0, 1] * cr[0] + probe[1, 0] * ci[1] - probe[1, 1] * cr[1],
        ]
        spots = lax.broadcasted_iota(jnp.int32, (PATCH, 384), 1)
        put = jnp.where(
            spots == lax.broadcasted_iota(jnp.int32, (PATCH, 384), 0) + shift, 1.0, 0.0
        ).astype(BF)
        for c in range(2):
            high = grad[c].astype(BF)
            low = (grad[c] - high.astype(F32)).astype(BF)
            moved = jnp.dot(high, put, preferred_element_type=F32) + jnp.dot(
                low, put, preferred_element_type=F32
            )
            for b in range(3):
                placed[p * 2 + c, b + 1, RIM : RIM + PATCH, :] = moved[:, b * BLK : (b + 1) * BLK]
        return carry

    lax.fori_loop(0, 2, forward_patch, 0)

    def cells_at(c, row_chunk, lane_block):
        total_cells = None
        for p in range(2):
            u, v = corner(p)
            row = jnp.minimum(jnp.maximum(row_chunk * RIM - u + RIM, 0), PATCH + RIM)
            lane = jnp.minimum(jnp.maximum(lane_block - (v >> 7), -1), 3) + 1
            term = placed[p * 2 + c, lane, pl.ds(row, RIM), :]
            total_cells = term if total_cells is None else total_cells + term
        return total_cells

    rim_chunk = 9 * oy
    rim_block = 5 * ox
    for c in range(2):
        for b in range(4):
            rim_row[c, :, b * BLK : (b + 1) * BLK] = cells_at(c, rim_chunk, b + 1).astype(BF)

    def packed_rim(row_chunk):
        real, imag = (cells_at(c, row_chunk, rim_block) for c in range(2))
        kept, moved = jnp.where(sx == 0, real, imag), jnp.where(sx == 0, imag, real)
        return (kept + swap_halves(moved)).astype(BF)

    rim_cor[...] = packed_rim(rim_chunk)

    def rim_columns(r, carry):
        rim_col[pl.ds(pl.multiple_of(r * RIM, RIM), RIM), :] = packed_rim(r + 1)
        return carry

    lax.fori_loop(0, 8, rim_columns, 0)
    outs = [
        pltpu.make_async_copy(src, dst, out_sem.at[i])
        for i, (src, dst) in enumerate(
            [
                (rim_row, row_out), (rim_col, col_out), (rim_cor, cor_out),
                (part, part_out), (ramp, ramp_out), (bv, bv_out),
            ]
        )
    ]
    for copy in outs[:3]:
        copy.start()
    for copy in picks:
        copy.wait()
    for copy in outs[4:6]:
        copy.start()

    for c in range(2):
        for b in range(5):
            sino[2 * TILE + c * RIM : 2 * TILE + (c + 1) * RIM, b * BLK : (b + 1) * BLK] = cells_at(
                c, rim_chunk, b + ox
            ).astype(BF)

    over_rows = pl.ds(2 * TILE, 2 * RIM)
    over_copy = pltpu.make_async_copy(sino.at[over_rows], sino_out.at[over_rows], out_sem.at[6])
    over_copy.start()

    def finished(r):
        rows = pl.ds(pl.multiple_of(r * RIM, RIM), RIM)
        spans = [pl.ds(pl.multiple_of(c * TILE + r * RIM, RIM), RIM) for c in range(2)]
        return [pltpu.make_async_copy(og.at[:, rows], og_out.at[0, :, rows], piece_sem.at[r, 2])] + [
            pltpu.make_async_copy(sino.at[spans[c]], sino_out.at[spans[c]], piece_sem.at[r, c])
            for c in range(2)
        ]

    def interior(r, carry):
        rows = pl.ds(pl.multiple_of(r * RIM, RIM), RIM)
        for c in range(2):
            for b in range(4):
                og[c, rows, b * BLK : (b + 1) * BLK] = cells_at(c, r + 1, b + 1)
            for b in range(5):
                sino[pl.ds(pl.multiple_of(c * TILE + r * RIM, RIM), RIM), b * BLK : (b + 1) * BLK] = cells_at(
                    c, r + 1, b + ox
                ).astype(BF)
        for copy in finished(r):
            copy.start()
        return carry

    lax.fori_loop(0, 8, interior, 0)

    for m in range(2):
        real, imag = (
            patch[0, 0] * chi[0, m, :, a] + sign * patch[0, 1] * chi[0, m, :, b]
            + patch[1, 0] * chi[1, m, :, a] + sign * patch[1, 1] * chi[1, m, :, b]
            for a, b, sign in ((slice(0, PATCH), slice(PATCH, 512), 1.0), (slice(PATCH, 512), slice(0, PATCH), -1.0))
        )
        for q, terms in ((2 * m, real), (2 * m + 1, imag)):
            part[0, q] = terms[0:BLK].astype(BF)
            part[1, SECOND[q]] = terms[BLK:].astype(BF)
    outs[3].start()

    def settle(r, carry):
        for copy in finished(r):
            copy.wait()
        return carry

    lax.fori_loop(0, 8, settle, 0)
    for copy in outs:
        copy.wait()
    over_copy.wait()


def regroup_kernel(
    angles,
    sino_ref, row_ref, col_ref, cor_ref, part_ref, ramp_ref, bv_ref,
    got_row, got_col, got_cor, total_out, inbox_out,
    sino, part, ramp, bv, part_got, part_sum, quarter_send, quarter_got, total,
    lines, over_send, over_got, msgs,
    load_sem, rim_send, rim_recv, part_ssem, part_rsem, over_ssem, over_rsem,
    word_sem, a2a_send, a2a_recv, own_sem, out_sem,
):
    ang, sy, sx = lax.axis_index("ang"), lax.axis_index("sy"), lax.axis_index("sx")
    oy, ox = 1 - sy, 1 - sx
    group = 2 * angles
    me = ang * 2 + sx

    barrier = pltpu.get_barrier_semaphore()
    line, place = ang >> 4, ang & 15
    spot = line * 2 + sx
    crosswise = []
    for k in range(1, group // 16):
        d = jnp.bitwise_xor(spot, k)
        crosswise.append(((d >> 1) * 16 + place, sy, d & 1))
    lengthwise = [(line * 16 + ((place + k) & 15), sy, sx) for k in range(1, 16)]
    greeted = [(ang, oy, sx), (ang, oy, ox)] + crosswise + lengthwise
    for dev in greeted:
        pl.semaphore_signal(barrier, inc=1, device_id=dev, device_id_type=MESH)
    across, beside = (ang, oy, ox), (ang, sy, ox)
    kind = jnp.bitwise_xor(sy, sx)
    routes = (
        (across, beside, 2 * sy, 2 * oy, sx, ox),
        (beside, across, 2 * kind, 2 * (1 - kind), sy, oy),
    )
    loads = [
        pltpu.make_async_copy(src, dst, load_sem.at[i])
        for i, (src, dst) in enumerate(
            [(sino_ref, sino), (ramp_ref, ramp), (bv_ref, bv)]
            + [(part_ref.at[h, pl.ds(routes[h][2], 2)], part.at[h]) for h in range(2)]
        )
    ]
    for copy in loads:
        copy.start()
    pl.semaphore_wait(barrier, len(greeted))

    for dev in crosswise:
        pl.semaphore_signal(word_sem, inc=1, device_id=dev, device_id_type=MESH)

    def exchange(step, h, src, dst, dev):
        return pltpu.make_async_remote_copy(
            src_ref=src, dst_ref=dst, send_sem=part_ssem.at[step, h], recv_sem=part_rsem.at[step, h],
            device_id=dev, device_id_type=MESH,
        )

    firsts = [
        exchange(0, h, part_ref.at[h, pl.ds(routes[h][3], 2)], part_got.at[h], routes[h][0])
        for h in range(2)
    ]
    for copy in firsts:
        copy.start()
    for copy in loads:
        copy.wait()

    for s in range(2):
        filtered = jnp.dot(sino[...], ramp[s], preferred_element_type=F32).astype(BF)
        lines[s] = jnp.dot(filtered, bv[s], preferred_element_type=F32)
        for c in range(2):
            over_send[s, c] = lines[s, 2 * TILE + c * RIM : 2 * TILE + (c + 1) * RIM, :].astype(BF)
    over = pltpu.make_async_remote_copy(
        src_ref=over_send, dst_ref=over_got, send_sem=over_ssem, recv_sem=over_rsem,
        device_id=(ang, oy, sx), device_id_type=MESH,
    )
    over.start()
    top = lax.broadcasted_iota(jnp.int32, (64, 8, BLK), 1) < 4
    for s in range(2):
        a = lines[s, 0:TILE, :].reshape(64, 8, BLK)
        b = lines[s, TILE : 2 * TILE, :].reshape(64, 8, BLK)
        lanes = slice(s * BLK, (s + 1) * BLK)
        msgs[:, 0, :, lanes] = jnp.where(top, a, pltpu.roll(b, 4, 1)).astype(BF)
        msgs[:, 1, :, lanes] = jnp.where(top, pltpu.roll(a, 4, 1), b).astype(BF)

    def send_to(d):
        @pl.when(d != me)
        def _():
            pltpu.make_async_remote_copy(
                src_ref=msgs.at[d >> 1, d & 1], dst_ref=inbox_out.at[me],
                send_sem=a2a_send, recv_sem=a2a_recv,
                device_id=(d >> 1, sy, d & 1), device_id_type=MESH,
            ).start()

    inner = group - 16

    def send_inner(k, carry):
        send_to(16 * sy + lax.rem(me + k, inner))
        return carry

    def send_edge(k, carry):
        send_to(inner * oy + ((me + k) & 15))
        return carry

    pl.semaphore_wait(word_sem, len(crosswise))
    lax.fori_loop(0, inner // 2, send_inner, 0)
    seconds = []
    for h, (_, after, _, _, keep, give) in enumerate(routes):
        firsts[h].wait()
        part_sum[h] = part[h].astype(F32) + part_got[h].astype(F32)
        quarter_send[h] = part_sum[h, give].astype(BF)
        seconds.append(exchange(1, h, quarter_send.at[h], quarter_got.at[h], after))
        seconds[h].start()
    lax.fori_loop(inner // 2, inner, send_inner, 0)
    rims = [
        pltpu.make_async_remote_copy(
            src_ref=src, dst_ref=dst, send_sem=rim_send.at[i], recv_sem=rim_recv.at[i],
            device_id=dev, device_id_type=MESH,
        )
        for i, (src, dst, dev) in enumerate(
            [
                (row_ref, got_row, (ang, oy, sx)),
                (col_ref, got_col, beside),
                (cor_ref, got_cor, across),
            ]
        )
    ]
    rims[0].start()
    over.wait()
    edge = pl.ds(pl.multiple_of((TILE - RIM) * oy, RIM), RIM)
    edge_low = pl.ds(pl.multiple_of(TILE + (TILE - RIM) * oy, RIM), RIM)
    pairs = pl.ds(56 * oy, 8)
    for s in range(2):
        a = (lines[s, edge, :] + over_got[s, 0].astype(F32)).reshape(8, 8, BLK)
        b = (lines[s, edge_low, :] + over_got[s, 1].astype(F32)).reshape(8, 8, BLK)
        lanes = slice(s * BLK, (s + 1) * BLK)
        msgs[pairs, 0, :, lanes] = jnp.where(top[0:8], a, pltpu.roll(b, 4, 1)).astype(BF)
        msgs[pairs, 1, :, lanes] = jnp.where(top[0:8], pltpu.roll(a, 4, 1), b).astype(BF)
    lax.fori_loop(0, 16, send_edge, 0)
    own = pltpu.make_async_copy(msgs.at[ang, sx], inbox_out.at[me], own_sem)
    own.start()

    thirds = []
    for h, (_, after, base, _, keep, _) in enumerate(routes):
        seconds[h].wait()
        at = total.at[h, base + keep]
        total[h, base + keep] = (part_sum[h, keep] + quarter_got[h].astype(F32)).astype(BF)
        thirds.append(exchange(2, h, at, at, after))
        thirds[h].start()
    rims[1].start()
    rims[2].start()
    fourths, kept = [], []
    for h, (before, _, base, _, _, _) in enumerate(routes):
        thirds[h].wait()
        at = pl.ds(base, 2)
        fourths.append(exchange(3, h, total.at[h, at], total_out.at[h, at], before))
        fourths[h].start()
        kept.append(pltpu.make_async_copy(total.at[h, at], total_out.at[h, at], out_sem.at[h]))
        kept[h].start()
    own.wait()
    pltpu.make_async_copy(
        inbox_out.at[pl.ds(0, group - 1)], inbox_out.at[pl.ds(0, group - 1)], a2a_recv
    ).wait()
    for copy in fourths:
        copy.wait()
    pltpu.make_async_copy(
        inbox_out.at[pl.ds(0, group - 1)], inbox_out.at[pl.ds(0, group - 1)], a2a_send
    ).wait()
    for copy in rims:
        copy.wait()
    for copy in kept:
        copy.wait()


def finish_kernel(
    angles, bi_ref, og_ref, row_ref, col_ref, cor_ref, total_ref, inbox_ref, og_out, pg_out, vol_out,
    og_row, og_col, row, col, cor, total, pg, inbox, vol, seen, in_sem, out_sem,
):
    sy, sx = lax.axis_index("sy"), lax.axis_index("sx")
    oy, ox = 1 - sy, 1 - sx
    row_at = pl.ds(pl.multiple_of((TILE - RIM) * oy, RIM), RIM)
    col_at = pl.ds(pl.multiple_of((TILE - BLK) * ox, BLK), BLK)
    rest_at = pl.ds(pl.multiple_of(BLK * sx, BLK), TILE - BLK)
    loads = [
        pltpu.make_async_copy(src, dst, in_sem.at[i])
        for i, (src, dst) in enumerate(
            [
                (og_ref.at[0, :, row_at, rest_at], og_row), (og_ref.at[0, :, :, col_at], og_col),
                (row_ref, row), (col_ref, col), (cor_ref, cor), (total_ref, total), (inbox_ref, inbox),
            ]
        )
    ]
    for copy in loads:
        copy.start()
    summed, arrived = loads[5:]
    for a in range(angles):
        seen[a] = 0
    summed.wait()
    for q in range(4):
        pg[0, q // 2, q % 2, 0:BLK, :] = total[0, q].astype(F32) * (1.0 / math.sqrt(8.0))
        pg[0, q // 2, q % 2, BLK:, :] = total[1, SECOND[q]].astype(F32) * (1.0 / math.sqrt(8.0))
    pg_copy = pltpu.make_async_copy(pg, pg_out, out_sem.at[0])
    pg_copy.start()
    for copy in loads[0:5]:
        copy.wait()
    for got, at in ((col, pl.ds(0, TILE)), (cor, row_at)):
        wide = got[...].astype(F32)
        turned = swap_halves(wide)
        low = lax.broadcasted_iota(jnp.int32, wide.shape, 1) < RIM
        added = (
            jnp.where(sx == 1, jnp.where(low, wide, 0.0), jnp.where(low, 0.0, turned)),
            jnp.where(sx == 1, jnp.where(low, turned, 0.0), jnp.where(low, 0.0, wide)),
        )
        for c in range(2):
            og_col[c, at, :] = og_col[c, at, :] + added[c]
    for c in range(2):
        og_row[c] = og_row[c] + row[c, :, rest_at].astype(F32)
        og_col[c, row_at, :] = og_col[c, row_at, :] + row[c, :, col_at].astype(F32)
    og_copies = [
        pltpu.make_async_copy(og_row, og_out.at[0, :, row_at, rest_at], out_sem.at[2]),
        pltpu.make_async_copy(og_col, og_out.at[0, :, :, col_at], out_sem.at[3]),
    ]
    for copy in og_copies:
        copy.start()
    arrived.wait()
    for b in range(8):
        line = jnp.zeros((8, BLK), F32)
        for k in range(16):
            source = bi_ref[b, k] >> 3
            slot = seen[source]
            seen[source] = 1
            lane = pl.multiple_of(slot * BLK, BLK)
            for h in range(2):
                line = line + inbox[source * 2 + h, :, pl.ds(lane, BLK)].astype(F32)
        for c in range(2):
            for r in range(4):
                vol[0, r, c, b * BLK : (b + 1) * BLK] = line[c * 4 + r]
    vol_copy = pltpu.make_async_copy(vol, vol_out, out_sem.at[1])
    vol_copy.start()
    for copy in og_copies:
        copy.wait()
    pg_copy.wait()
    vol_copy.wait()


def body(angles, tables, objects, probe, data, positions, block_index, block_values):
    forward, backward, ramp = (jnp.asarray(t) for t in tables)
    group = 2 * angles
    dma = pltpu.SemaphoreType.DMA
    smem = pl.BlockSpec(memory_space=pltpu.SMEM)
    hbm = pl.BlockSpec(memory_space=pltpu.HBM)

    def shape(dims, kind):
        return jax.ShapeDtypeStruct(dims, kind)

    rim_shapes = (shape((2, RIM, TILE), BF), shape((TILE, BLK), BF), shape((RIM, BLK), BF))
    halos = pl.pallas_call(
        strips_kernel,
        out_shape=rim_shapes,
        in_specs=[hbm],
        out_specs=[hbm] * 3,
        scratch_shapes=[
            pltpu.VMEM((2, TILE, BLK), BF), pltpu.VMEM((TILE, BLK), BF), dma, dma((3,)), dma((3,)),
        ],
        compiler_params=pltpu.CompilerParams(
            collective_id=0, has_side_effects=True, vmem_limit_bytes=62 * 1024 * 1024
        ),
    )(objects)
    og_part, row, col, cor, parts, ramp_two, bv_two, sino = pl.pallas_call(
        functools.partial(patch_kernel, angles),
        out_shape=(shape((1, 2, TILE, TILE), F32),) + rim_shapes + (
            shape((2, 4, BLK, PATCH), BF), shape((2, SPAN, BLK), BF), shape((2, BLK, BLK), BF),
            shape((2 * ROWS - 2 * RIM, SPAN), BF),
        ),
        in_specs=[smem] * 2 + [hbm] * 10,
        out_specs=[hbm] * 8,
        scratch_shapes=[
            pltpu.VMEM((2, ROWS, COLS), BF),
            pltpu.VMEM((ROWS, BLK), BF),
            pltpu.VMEM((2, 2, PATCH, PATCH), F32),
            pltpu.VMEM((2, PATCH, PATCH), BF),
            pltpu.VMEM((512, 512), BF),
            pltpu.VMEM((512, 512), BF),
            pltpu.VMEM((2, SPAN, BLK), BF),
            pltpu.VMEM((2, BLK, BLK), BF),
            pltpu.VMEM((2, 2, 272, BLK), F32),
            pltpu.VMEM((2, 2, PATCH, PATCH), F32),
            pltpu.VMEM((2, 512, PATCH), BF),
            pltpu.VMEM((2, PATCH, 512), BF),
            pltpu.VMEM((2, PATCH, 512), F32),
            pltpu.VMEM((2, 2, PATCH, 512), F32),
            pltpu.VMEM((4, 5, 384, BLK), F32),
            pltpu.VMEM((2, TILE, TILE), F32),
            pltpu.VMEM((2, RIM, TILE), BF),
            pltpu.VMEM((TILE, BLK), BF),
            pltpu.VMEM((RIM, BLK), BF),
            pltpu.VMEM((2, 4, BLK, PATCH), BF),
            pltpu.VMEM((2 * ROWS - 2 * RIM, SPAN), BF),
            dma((8,)), dma((4,)), dma((7,)), dma((8, 3)),
        ],
        compiler_params=pltpu.CompilerParams(vmem_limit_bytes=62 * 1024 * 1024),
    )(positions, block_index, objects, *halos, probe, data, forward, backward, ramp, block_values)
    got_row, got_col, got_cor, total, inbox = pl.pallas_call(
        functools.partial(regroup_kernel, angles),
        out_shape=rim_shapes + (shape((2, 4, BLK, PATCH), BF), shape((group, 8, 2 * BLK), BF)),
        in_specs=[hbm] * 7,
        out_specs=[hbm] * 5,
        scratch_shapes=[
            pltpu.VMEM((2 * ROWS - 2 * RIM, SPAN), BF),
            pltpu.VMEM((2, 2, BLK, PATCH), BF),
            pltpu.VMEM((2, SPAN, BLK), BF),
            pltpu.VMEM((2, BLK, BLK), BF),
            pltpu.VMEM((2, 2, BLK, PATCH), BF),
            pltpu.VMEM((2, 2, BLK, PATCH), F32),
            pltpu.VMEM((2, BLK, PATCH), BF),
            pltpu.VMEM((2, BLK, PATCH), BF),
            pltpu.VMEM((2, 4, BLK, PATCH), BF),
            pltpu.VMEM((2, 2 * ROWS - 2 * RIM, BLK), F32),
            pltpu.VMEM((2, 2, RIM, BLK), BF),
            pltpu.VMEM((2, 2, RIM, BLK), BF),
            pltpu.VMEM((group // 2, 2, 8, 2 * BLK), BF),
            dma((5,)), dma((3,)), dma((3,)), dma((4, 2)), dma((4, 2)), dma, dma,
            pltpu.SemaphoreType.REGULAR, dma, dma, dma, dma((2,)),
        ],
        compiler_params=pltpu.CompilerParams(
            collective_id=1, has_side_effects=True, vmem_limit_bytes=62 * 1024 * 1024
        ),
    )(sino, row, col, cor, parts, ramp_two, bv_two)
    return pl.pallas_call(
        functools.partial(finish_kernel, angles),
        out_shape=(
            shape((1, 2, TILE, TILE), F32), shape((1, 2, 2, PATCH, PATCH), F32), shape((1, 4, 2, 1024), F32),
        ),
        in_specs=[smem] + [hbm] * 6,
        out_specs=[hbm] * 3,
        scratch_shapes=[
            pltpu.VMEM((2, RIM, TILE - BLK), F32),
            pltpu.VMEM((2, TILE, BLK), F32),
            pltpu.VMEM((2, RIM, TILE), BF),
            pltpu.VMEM((TILE, BLK), BF),
            pltpu.VMEM((RIM, BLK), BF),
            pltpu.VMEM((2, 4, BLK, PATCH), BF),
            pltpu.VMEM((1, 2, 2, PATCH, PATCH), F32),
            pltpu.VMEM((group, 8, 2 * BLK), BF),
            pltpu.VMEM((1, 4, 2, 1024), F32),
            pltpu.SMEM((angles,), jnp.int32),
            dma((7,)), dma((4,)),
        ],
        input_output_aliases={1: 0},
        compiler_params=pltpu.CompilerParams(vmem_limit_bytes=62 * 1024 * 1024),
    )(block_index, og_part, got_row, got_col, got_cor, total, inbox)


def solution(mesh):
    tables = dft_tables() + (ramp_blocks(8),)
    return jax.shard_map(
        functools.partial(body, mesh.shape["ang"], tables),
        mesh=mesh,
        in_specs=(
            P("ang", None, "sy", "sx"),
            P(),
            P("ang", "sy", "sx", None, None, None),
            P("ang", "sy", "sx", None, None),
            P(),
            P(),
        ),
        out_specs=(
            P("ang", None, "sy", "sx"),
            P("ang", None, None, None, None),
            P("sy", ("ang", "sx"), None, None),
        ),
        check_vma=False,
    )
```
